32 devices in a mesh: dp: 4 (over z), ctx: 4 (over y, core), tensor: 2 (over x).
Axes of the slice: x: 2, y: 2, z: 4, core: 2. Of those that a mesh axis runs over, the one named last changes fastest.
Arguments:
- tokens: bfloat16 [4096, 1536], P(('dp', 'ctx'), 'tensor'), may hold values from -6 to 6
- segments: int32 [4, 1024], P('dp'), may hold values from 0 to 1, never falling along the last dimension, each value on 1 to 768 neighbouring positions
- order: int32 [4, 1024], P('dp'), may hold values from 0 to 1023, each once within a row
- routes: int32 [4096, 8], P('dp'), may hold values from 0 to 39, all different within a row
- gain_one: float32 [1536], P('tensor'), may hold values from 0.5 to 1.5
- w_query: bfloat16 [1536, 1536], P('dp', 'tensor'), may hold values from -0.15625 to 0.15625
- w_key: bfloat16 [1536, 512], P('dp', 'tensor'), may hold values from -0.15625 to 0.15625
- w_value: bfloat16 [1536, 512], P('dp', 'tensor'), may hold values from -0.15625 to 0.15625
- w_output: bfloat16 [1536, 1536], P('dp', 'tensor'), may hold values from -1.25 to 1.25
- gain_two: float32 [1536], P('tensor'), may hold values from 0.5 to 1.5
- w_router: bfloat16 [1536, 40], P('dp'), may hold values from -0.06982422 to 0.06982422
- w_expert_in: bfloat16 [1536, 40, 1024], P('dp', 'tensor'), may hold values from -0.15625 to 0.15625
- w_expert_out: bfloat16 [1536, 40, 512], P('dp', 'tensor'), may hold values from -0.75 to 0.75
- cotangent: bfloat16 [4096, 1536], P(('dp', 'ctx'), 'tensor'), may hold values from -6 to 6
Outputs:
- output: bfloat16 [4096, 1536], P(('dp', 'ctx'), 'tensor')
- grad_tokens: float32 [4096, 1536], P(('dp', 'ctx'), 'tensor')
- grad_gain_one: float32 [1536], P('tensor')
- grad_query: float32 [1536, 1536], P('dp', 'tensor')
- grad_key: float32 [1536, 512], P('dp', 'tensor')
- grad_value: float32 [1536, 512], P('dp', 'tensor')
- grad_output: float32 [1536, 1536], P('dp', 'tensor')
- grad_gain_two: float32 [1536], P('tensor')
- grad_router: float32 [1536, 40], P('dp')
- grad_expert_in: float32 [1536, 40, 1024], P('dp', 'tensor')
- grad_expert_out: float32 [1536, 40, 512], P('dp', 'tensor')
The draws below stay inside these ranges and needn't reach their ends.
Inputs may be any that keep to these rules, and one draw needn't show every extreme that they name: `routes`: each row names 8 different experts. `segments`: in each pack the document numbers never fall and each of the 2 documents has at least one token; no document has more than 768 tokens. `order`: each row names every position of its pack once.
All inputs are finite; a program needn't handle non-finite values.
Results may differ from the reference program's by a relative error of at most 0.015.
Values may be sent and summed in bfloat16 or wider, within the bound.
A program may use at most 640 MiB of HBM per device.

```python
import math
import jax
import jax.numpy as jnp
import numpy as np
from jax import lax

D = 1536
HEADS = 24
KV_HEADS = 8
HEAD_DIM = 64
EXPERTS = 40
TOP_K = 8
FF = 512
TOK_DEV = 256
TOKENS = 4096
PACK = 1024
CAP = 96
DOCS = 2
LONGEST = 768
N_DP = 4
N_CTX = 4


def shard_levels(own_key, dims, pieces, low, high):
    factor_of, own = 1.0, jax.random.fold_in(own_key, 6)
    for dim, blocks in pieces:
        steps = jnp.exp(jax.random.uniform(jax.random.fold_in(own, dim), (blocks,), jnp.float32, low / len(pieces), high / len(pieces)))
        factor_of = factor_of * jnp.repeat(steps, dims[dim] // blocks).reshape([-1 if axis == dim else 1 for axis in range(len(dims))])
    return factor_of


def picks_of(key, rows, number_of, top, lift):
    sequence = jax.random.permutation(jax.random.fold_in(key, 1), number_of)
    pull = sequence
    for power in range(3):
        pull = pull * pull // number_of
    pull = pull * lift // number_of
    tickets = jax.random.randint(jax.random.fold_in(key, 2), (rows, number_of), 0, 4096) + pull
    fixed_rows = jax.random.permutation(jax.random.fold_in(key, 3), rows)[jnp.arange(number_of) % rows]
    tickets = jnp.where(jnp.arange(rows)[:, None] == fixed_rows[None, :], 1 << 14, tickets)
    priority = tickets * number_of + jnp.arange(number_of)
    return lax.top_k(priority.astype(jnp.int32), top)[1].astype(jnp.int32)


def profile(count, total, limit, slope):
    weights = [(1 << 20) // math.isqrt(standing ** slope) + 1 for standing in range(2, count + 1)]
    spare, holding = total - limit - (count - 1), [1] * (count - 1)
    while spare > 0:
        movable = [i for i in range(count - 1) if holding[i] < limit]
        whole, budget = sum([weights[i] for i in movable]), spare
        for i in movable:
            extra = min(limit - holding[i], max(1, budget * weights[i] // whole), spare)
            holding[i] = holding[i] + extra
            spare = spare - extra
    return np.array([limit] + holding)


def uneven_parts(key, number_of, total, most, slope):
    if number_of == 2:
        one = jax.random.randint(key, (), max(1, total - most), min(most, total - 1) + 1)
        return jnp.stack([one, total - one])
    sizes = jnp.asarray(profile(number_of, total, most, slope), jnp.int32)
    twos = (number_of - 1) // 2
    source_of, receiver = sizes[1:1 + 2 * twos:2], sizes[2:2 + 2 * twos:2]
    room = jnp.minimum(source_of - 1, most - receiver)
    moved = jax.random.randint(jax.random.fold_in(key, 1), (twos,), 0, 1 << 20) % (room + 1)
    sizes = sizes.at[1:1 + 2 * twos:2].set(source_of - moved).at[2:2 + 2 * twos:2].set(receiver + moved)
    return sizes[jax.random.permutation(jax.random.fold_in(key, 2), number_of)]


def noise(key, shape, scale, bound, split=(), kind=jnp.bfloat16):
    array = scale * jax.random.normal(key, shape, jnp.float32)
    if split:
        array = array * shard_levels(key, shape, split, -0.22, 0.18)
    return jnp.clip(array, -bound, bound).astype(kind)


def setup_inputs(seed: int = 0) -> dict:
    streams_of = jax.random.split(jax.random.key(seed), 15)
    return {
        "tokens": noise(streams_of[0], (TOKENS, D), 1.0, 6.0, ((0, 16), (1, 2))),
        "segments": jax.vmap(lambda own: jnp.searchsorted(jnp.cumsum(uneven_parts(own, DOCS, PACK, LONGEST, 0)), jnp.arange(PACK), side="right"))(jax.random.split(streams_of[1], N_DP)).reshape((N_DP, PACK)).astype(jnp.int32),
        "order": jax.vmap(lambda own: jax.random.permutation(own, PACK))(jax.random.split(streams_of[2], N_DP)).reshape((N_DP, PACK)).astype(jnp.int32),
        "routes": picks_of(streams_of[3], TOKENS, EXPERTS, TOP_K, 1638),
        "gain_one": jnp.clip(1.0 + 0.1 * jax.random.normal(streams_of[4], (D,), jnp.float32), 0.5, 1.5),
        "w_query": noise(streams_of[5], (D, HEADS * HEAD_DIM), D ** -0.5, 0.15625, ((0, 4), (1, 2))),
        "w_key": noise(streams_of[6], (D, KV_HEADS * HEAD_DIM), D ** -0.5, 0.15625, ((0, 4), (1, 2))),
        "w_value": noise(streams_of[7], (D, KV_HEADS * HEAD_DIM), D ** -0.5, 0.15625, ((0, 4), (1, 2))),
        "w_output": noise(streams_of[8], (D, HEADS * HEAD_DIM), (HEADS * HEAD_DIM // 64) ** -0.5, 1.25, ((0, 4), (1, 2))),
        "gain_two": jnp.clip(1.0 + 0.1 * jax.random.normal(streams_of[9], (D,), jnp.float32), 0.5, 1.5),
        "w_router": noise(streams_of[10], (D, EXPERTS), 0.0128, 0.06982422, ((0, 4),)),
        "w_expert_in": noise(streams_of[11], (D, EXPERTS, 2 * FF), D ** -0.5, 0.15625, ((0, 4), (1, 2))),
        "w_expert_out": noise(streams_of[12], (D, EXPERTS, FF), (FF // 8) ** -0.5, 0.75, ((0, 4), (1, 2))),
        "cotangent": noise(streams_of[13], (TOKENS, D), 1.0, 6.0, ((0, 16), (1, 2))),
    }


@jax.custom_vjp
def low(v):
    return lax.optimization_barrier(v.astype(jnp.bfloat16)).astype(jnp.float32)

@jax.custom_vjp
def low_back(v):
    return v

def low_keep(v):
    return (low(v), None)

def low_pass(kept, grad):
    return (grad,)

def back_keep(v):
    return (v, None)

def back_low(kept, grad):
    return (low(grad),)
low.defvjp(low_keep, low_pass)
low_back.defvjp(back_keep, back_low)
EPS = 1e-06
THETA = 10000.0
NEG = -1e+30
HIGH = lax.Precision.HIGHEST

def positions(segment_row):
    length = segment_row.shape[0]
    places = jnp.arange(length, dtype=jnp.int32)
    change = jnp.concatenate([jnp.ones((1,), jnp.bool_), segment_row[1:] != segment_row[:-1]])
    starts = lax.cummax(jnp.where(change, places, 0).astype(jnp.int32), axis=0)
    return (places - starts).astype(jnp.float32)

def rope_tables(position):
    halves = HEAD_DIM // 2
    frequency = THETA ** (-2.0 * jnp.arange(halves, dtype=jnp.float32) / HEAD_DIM)
    angles = position[:, None] * frequency[None, :]
    return (jnp.cos(angles)[:, None, :], jnp.sin(angles)[:, None, :])

def rotate(values, cosine_table, sine_table):
    halves = values.shape[-1] // 2
    first_half, second_half = (values[..., :halves], values[..., halves:])
    return jnp.concatenate([first_half * cosine_table - second_half * sine_table, second_half * cosine_table + first_half * sine_table], axis=-1)

def rms_norm(columns, gain_vec):
    inverse = lax.rsqrt(lax.optimization_barrier(jnp.mean(columns * columns, axis=-1, keepdims=True)) + EPS)
    return low(columns * inverse * gain_vec[None, :])

def dispatch(route_rows, first_expert, local_count, capacity):
    flat_routes = route_rows.reshape(-1).astype(jnp.int32)
    pairs_total = flat_routes.shape[0]
    experts_all = jnp.arange(EXPERTS, dtype=jnp.int32)
    onehot = (flat_routes[:, None] == experts_all[None, :]).astype(jnp.int32)
    ranking = lax.optimization_barrier(jnp.sum((jnp.cumsum(onehot, axis=0).astype(jnp.int32) - 1) * onehot, axis=1)).astype(jnp.int32)
    local_expert = flat_routes - first_expert
    usable = (ranking < capacity) & (local_expert >= 0) & (local_expert < local_count)
    pair_slot = jnp.where(usable, local_expert * capacity + ranking, local_count * capacity).astype(jnp.int32)
    pair_index = jnp.arange(pairs_total, dtype=jnp.int32)
    slot_pair = jnp.full((local_count * capacity + 1,), pairs_total, jnp.int32).at[pair_slot].set(pair_index)[:-1]
    return (pair_slot, slot_pair)

def attend_pack(normed, segment_row, query_w, key_w, value_w, output_w):
    length = normed.shape[0]
    group_size = HEADS // KV_HEADS
    score_scale = HEAD_DIM ** (-0.5)
    cosine_table, sine_table = rope_tables(positions(segment_row))
    queries = jnp.dot(normed, query_w, precision=HIGH).reshape(length, HEADS, HEAD_DIM)
    queries = low(rotate(low_back(queries), cosine_table, sine_table))
    key_rows = jnp.dot(normed, key_w, precision=HIGH).reshape(length, KV_HEADS, HEAD_DIM)
    key_rows = low(rotate(low_back(key_rows), cosine_table, sine_table))
    values = low(low_back(jnp.dot(normed, value_w, precision=HIGH))).reshape(length, KV_HEADS, HEAD_DIM)
    places = jnp.arange(length, dtype=jnp.int32)
    allowed = (segment_row[:, None] == segment_row[None, :]) & (places[:, None] >= places[None, :])
    queries = jnp.moveaxis(queries.reshape(length, KV_HEADS, group_size, HEAD_DIM), 1, 0)
    key_rows = jnp.moveaxis(key_rows, 1, 0)
    values = jnp.moveaxis(values, 1, 0)

    def one_head(operands):
        query_head, key_head, value_head = operands
        scores = low_back(score_scale * jnp.einsum('igd,jd->gij', query_head, key_head, precision=HIGH))
        scores = jnp.where(allowed[None], scores, NEG)
        shares = jax.nn.softmax(scores, axis=-1)
        blended = jnp.einsum('gij,jd->igd', low(shares), value_head, precision=HIGH)
        return low_back(low(blended))
    heads_out = lax.map(jax.checkpoint(one_head), (queries, key_rows, values))
    merged = jnp.moveaxis(heads_out, 0, 1).reshape(length, HEADS * HEAD_DIM)
    return low_back(jnp.dot(merged, output_w.T, precision=HIGH))

def expert_group(rows_in, route_rows, gain_two, router_w, upper_w, lower_w):
    length = rows_in.shape[0]
    normed = rms_norm(rows_in, gain_two)
    logits = low_back(jnp.dot(normed, router_w, precision=HIGH))
    gate_probs = jax.nn.softmax(jnp.take_along_axis(logits, route_rows, axis=1), axis=-1)
    pair_slot, slot_pair = dispatch(route_rows, 0, EXPERTS, CAP)
    token_of = slot_pair // TOP_K
    padded = jnp.concatenate([normed, jnp.zeros((1, D), jnp.float32)])
    inputs_slot = padded[token_of].reshape(EXPERTS, CAP, D)
    hidden_pre = low_back(jnp.einsum('ecd,def->ecf', inputs_slot, upper_w, precision=HIGH))
    active = low(jax.nn.silu(hidden_pre[..., :FF]) * hidden_pre[..., FF:])
    output = low_back(jnp.einsum('ecf,def->ecd', active, lower_w, precision=HIGH))
    out_pad = jnp.concatenate([output.reshape(EXPERTS * CAP, D), jnp.zeros((1, D), jnp.float32)])
    pair_out = out_pad[pair_slot].reshape(length, TOP_K, D)
    return rows_in + lax.optimization_barrier(jnp.sum(gate_probs[:, :, None] * pair_out, axis=1))

def reference(tokens, segments, order, routes, gain_one, w_query, w_key, w_value, w_output, gain_two, w_router, w_expert_in, w_expert_out, cotangent):
    params = (tokens.astype(jnp.float32), gain_one.astype(jnp.float32), w_query.astype(jnp.float32), w_key.astype(jnp.float32), w_value.astype(jnp.float32), w_output.astype(jnp.float32), gain_two.astype(jnp.float32), w_router.astype(jnp.float32), w_expert_in.astype(jnp.float32), w_expert_out.astype(jnp.float32))
    order_idx = order.astype(jnp.int32)
    pack_ids = jnp.broadcast_to(jnp.arange(N_DP, dtype=jnp.int32)[:, None], (N_DP, PACK))
    inverse = jnp.zeros((N_DP, PACK), jnp.int32).at[pack_ids, order_idx].set(jnp.broadcast_to(jnp.arange(PACK, dtype=jnp.int32)[None, :], (N_DP, PACK)))
    route_dealt = jnp.take_along_axis(routes.astype(jnp.int32).reshape(N_DP, PACK, TOP_K), order_idx[:, :, None], axis=1)
    route_groups = route_dealt.reshape(N_DP * N_CTX, TOK_DEV, TOP_K)

    def forward(tokens_f, gain_one_f, query_w, key_w, value_w, output_w, gain_two_f, router_w, upper_w, lower_w):
        pack_rows_all = tokens_f.reshape(N_DP, PACK, D)

        def pack_step(operands):
            pack_rows, segment_row = operands
            normed = rms_norm(pack_rows, gain_one_f)
            return pack_rows + attend_pack(normed, segment_row, query_w, key_w, value_w, output_w)
        middle = lax.map(jax.checkpoint(pack_step), (pack_rows_all, segments))
        dealt = jnp.take_along_axis(middle, order_idx[:, :, None], axis=1)
        groups = dealt.reshape(N_DP * N_CTX, TOK_DEV, D)

        def group_step(operands):
            group_rows, route_rows = operands
            return expert_group(group_rows, route_rows, gain_two_f, router_w, upper_w, lower_w)
        mixed = lax.map(jax.checkpoint(group_step), (groups, route_groups)).reshape(N_DP, PACK, D)
        restored = jnp.take_along_axis(mixed, inverse[:, :, None], axis=1)
        return restored.reshape(TOKENS, D)
    result, pullback = jax.vjp(forward, *params)
    gradients = pullback(cotangent.astype(jnp.float32))
    return (result.astype(jnp.bfloat16), gradients[0], gradients[1], gradients[2], gradients[3], gradients[4], gradients[5], gradients[6], gradients[7], gradients[8], gradients[9])
```

```python
import jax
import jax.numpy as jnp
from jax import lax
from jax.sharding import PartitionSpec as P

D = 1536
HEAD_DIM = 64
EXPERTS = 40
TOP_K = 8
FF = 512
EPS = 1e-06
THETA = 10000.0
NEG = -1e30
LANES = 128
ALL = ("dp", "ctx", "tensor")
BF = jnp.bfloat16
F32 = jnp.float32


def rope_tables(position):
    halves = HEAD_DIM // 2
    frequency = THETA ** (-2.0 * jnp.arange(halves, dtype=F32) / HEAD_DIM)
    angles = position[:, None] * frequency[None, :]
    return (jnp.cos(angles)[:, None, :], jnp.sin(angles)[:, None, :])


def rotate(values, cosine_table, sine_table):
    halves = values.shape[-1] // 2
    first_half, second_half = (values[..., :halves], values[..., halves:])
    return jnp.concatenate(
        [
            first_half * cosine_table - second_half * sine_table,
            second_half * cosine_table + first_half * sine_table,
        ],
        axis=-1,
    )


def dot(a, b, dims):
    return lax.dot_general(a, b, (dims, ((), ())), preferred_element_type=F32)


def norm_forward(rows, gain):
    inverse = lax.rsqrt(jnp.mean(rows * rows, axis=1, keepdims=True) + EPS)
    return (inverse, (rows * inverse * gain[None, :]).astype(BF))


def norm_backward(rows, gain, inverse, grad_normed):
    weighted = grad_normed * gain[None, :]
    inner = jnp.sum(weighted * rows, axis=1, keepdims=True)
    grad_rows = weighted * inverse - rows * (inverse * inverse * inverse * inner / D)
    return (grad_rows, jnp.sum(grad_normed * rows * inverse, axis=0))


def exchange(parts, at, count):
    result = lax.dynamic_update_index_in_dim(
        jnp.zeros_like(parts), lax.dynamic_index_in_dim(parts, at, 0), at, 0
    )
    for hop in range(1, count):
        sent = lax.dynamic_index_in_dim(parts, (at + hop) % count, 0)
        got = lax.ppermute(sent, "dp", [(i, (i + hop) % count) for i in range(count)])
        result = lax.dynamic_update_index_in_dim(result, got, (at - hop) % count, 0)
    return result


def on_device(
    tokens,
    segments,
    order,
    routes,
    gain_one,
    w_query,
    w_key,
    w_value,
    w_output,
    gain_two,
    w_router,
    w_expert_in,
    w_expert_out,
    cotangent,
):
    nd, nc, nt = (lax.axis_size("dp"), lax.axis_size("ctx"), lax.axis_size("tensor"))
    dp_at, ctx_at, tensor_at = (
        lax.axis_index("dp"),
        lax.axis_index("ctx"),
        lax.axis_index("tensor"),
    )
    n_rows, part_width = tokens.shape
    sub = n_rows // nt
    pack_len = order.shape[1]
    d_local = w_query.shape[0]
    q_width, kv_width = (w_query.shape[1], w_key.shape[1])
    q_heads, kv_heads = (q_width // HEAD_DIM, kv_width // HEAD_DIM)
    group = q_heads // kv_heads
    qkv_width = q_width + 2 * kv_width
    local_count = w_expert_in.shape[1]
    capacity = n_rows * 3 // 8

    gains = lax.all_gather(jnp.stack([gain_one, gain_two]), "tensor", axis=1, tiled=True)
    gain_one_full, gain_two_full = (gains[0], gains[1])
    tokens_full = lax.all_gather(tokens, "tensor", axis=1, tiled=True)
    packed = jnp.concatenate([w_query, w_key, w_value, w_router], axis=1)
    share = d_local // nc
    packed = lax.dynamic_slice_in_dim(packed, ctx_at * share, share, 0)
    packed = lax.all_gather(packed, ("dp", "ctx"), axis=0, tiled=True)
    qkv_w, router_w = (packed[:, :qkv_width], packed[:, qkv_width:])
    output_w = lax.all_gather(
        lax.dynamic_slice_in_dim(w_output, ctx_at * share, share, 0),
        ("dp", "ctx"),
        axis=0,
        tiled=True,
    )
    cot_sub = lax.all_to_all(cotangent, "tensor", 0, 1, tiled=True)
    cot_all = lax.all_gather(cot_sub, ALL, axis=0, tiled=True)
    tokens_sub = lax.dynamic_slice_in_dim(tokens_full, tensor_at * sub, sub, 0).astype(F32)

    by_expert = local_count % nc == 0
    own_count = local_count // nc if by_expert else local_count
    units = FF // nd if by_expert else FF // (nd * nc)
    first_expert = tensor_at * local_count + (ctx_at * own_count if by_expert else 0)
    if by_expert:
        own_in = lax.dynamic_slice_in_dim(w_expert_in, ctx_at * own_count, own_count, 1)
        own_out = lax.dynamic_slice_in_dim(w_expert_out, ctx_at * own_count, own_count, 1)
        own_in = own_in.reshape(d_local, own_count, 2, nd, units)
        own_out = own_out.reshape(d_local, own_count, nd, units)
    else:
        own_in = w_expert_in.reshape(d_local, own_count, 2, nd, nc, units)
        own_out = w_expert_out.reshape(d_local, own_count, nd, nc, units)
        own_in = lax.dynamic_index_in_dim(own_in, ctx_at, 4, False)
        own_out = lax.dynamic_index_in_dim(own_out, ctx_at, 3, False)
    own_in = jnp.transpose(own_in, (3, 0, 2, 1, 4)).reshape(nd, d_local, 2 * own_count * units)
    own_out = jnp.transpose(own_out, (2, 0, 1, 3)).reshape(nd, d_local, own_count * units)
    width = own_count * units
    expert_w = exchange(jnp.concatenate([own_in, own_out], axis=2), dp_at, nd)
    expert_w = expert_w.reshape(D, 3 * width)
    upper_w, lower_w = (expert_w[:, : 2 * width], expert_w[:, 2 * width :])

    order_row = order[0]
    places = jnp.arange(pack_len, dtype=jnp.int32)
    dealt = jnp.sum(jnp.where(order_row[:, None] == places[None, :], places[:, None], 0), axis=0)
    sub_start = ctx_at * n_rows + tensor_at * sub
    dealt_sub = lax.dynamic_slice_in_dim(dealt, sub_start, sub)
    experts_all = jnp.arange(EXPERTS, dtype=jnp.int32)
    uses = jnp.any(routes[:, :, None] == experts_all[None, None, :], axis=1)
    earlier = (dealt_sub[:, None] // n_rows == dealt[None, :] // n_rows) & (
        dealt[None, :] < dealt_sub[:, None]
    )
    ranks = dot(earlier.astype(BF), uses.astype(BF), ((1,), (0,)))
    uses_sub = lax.dynamic_slice_in_dim(uses, sub_start, sub, 0)
    kept = (uses_sub & (ranks < capacity)).astype(F32)

    segment_row = segments[0]
    local_segs = lax.dynamic_slice_in_dim(segment_row, ctx_at * n_rows, n_rows)
    local_places = ctx_at * n_rows + jnp.arange(n_rows, dtype=jnp.int32)
    starts = jnp.sum((segment_row[None, :] < local_segs[:, None]).astype(jnp.int32), axis=1)
    cosine_table, sine_table = rope_tables((local_places - starts).astype(F32))
    _, h_one = norm_forward(tokens_full.astype(F32), gain_one_full)
    projected = dot(h_one, qkv_w, ((1,), (0,)))
    turned = rotate(
        projected[:, : q_width + kv_width].reshape(n_rows, q_heads + kv_heads, HEAD_DIM),
        cosine_table,
        sine_table,
    ).astype(BF)
    queries = turned[:, :q_heads].reshape(n_rows, kv_heads, group, HEAD_DIM)
    kv_rows = jnp.concatenate(
        [
            turned[:, q_heads:].reshape(n_rows, kv_width),
            projected[:, q_width + kv_width :].astype(BF),
        ],
        axis=1,
    )
    kv_all = lax.all_gather(kv_rows, "ctx", axis=0, tiled=True)
    key_heads = kv_all[:, :kv_width].reshape(pack_len, kv_heads, HEAD_DIM)
    value_heads = kv_all[:, kv_width:].reshape(pack_len, kv_heads, HEAD_DIM)
    allowed = (local_segs[:, None] == segment_row[None, :]) & (
        local_places[:, None] >= places[None, :]
    )
    score_scale = HEAD_DIM ** (-0.5)
    scores = score_scale * jnp.einsum(
        "bagd,pad->agbp", queries, key_heads, preferred_element_type=F32
    )
    scores = jnp.where(allowed[None, None], scores, NEG)
    highest = jnp.max(scores, axis=-1, keepdims=True)
    weights = jnp.exp(scores - highest)
    totals = jnp.sum(weights, axis=-1, keepdims=True)
    shares_low = (weights / totals).astype(BF)
    log_totals = highest + jnp.log(totals)
    attended = (
        jnp.einsum("agbp,pad->bagd", shares_low, value_heads, preferred_element_type=F32)
        .astype(BF)
        .reshape(n_rows, q_width)
    )
    attended_sub = lax.all_to_all(attended, "tensor", 0, 1, tiled=True)
    output_full = lax.all_gather(output_w, "tensor", axis=1, tiled=True)
    middle = tokens_sub + dot(attended_sub, output_full, ((1,), (1,)))

    inverse_two, h_two = norm_forward(middle, gain_two_full)
    logits = jnp.where(uses_sub, dot(h_two, router_w, ((1,), (0,))), NEG)
    raised = jnp.exp(logits - jnp.max(logits, axis=1, keepdims=True))
    gates = raised / jnp.sum(raised, axis=1, keepdims=True)
    gates_kept = gates * kept
    gates_high = gates_kept.astype(BF)
    gates_low = (gates_kept - gates_high.astype(F32)).astype(BF)
    extra = jnp.zeros((sub, LANES - 2 * EXPERTS), BF)
    h_all = lax.all_gather(
        jnp.concatenate([h_two, gates_high, gates_low, extra], axis=1), ALL, axis=0, tiled=True
    )
    gates_all = (
        h_all[:, D : D + EXPERTS].astype(F32) + h_all[:, D + EXPERTS : D + 2 * EXPERTS].astype(F32)
    )
    total_rows = h_all.shape[0]
    gates_own = lax.dynamic_slice_in_dim(gates_all, first_expert, own_count, 1)
    h_all = h_all[:, :D]

    gate_wide = jnp.broadcast_to(gates_own[:, :, None], (total_rows, own_count, units)).reshape(
        total_rows, width
    )
    hidden = dot(h_all, upper_w, ((1,), (0,)))
    grad_raw = dot(cot_all, lower_w, ((1,), (0,)))
    gate_part, up_part = (hidden[:, :width], hidden[:, width:])
    sigmoid = jax.nn.sigmoid(gate_part)
    silu = gate_part * sigmoid
    active = (silu * up_part).astype(BF).astype(F32)
    active_gated = (active * gate_wide).astype(BF)
    grad_gates = jnp.sum((grad_raw * active).reshape(total_rows, own_count, units), axis=2)
    grad_active = grad_raw * gate_wide
    grad_hidden = jnp.concatenate(
        [
            grad_active * up_part * sigmoid * (1.0 + gate_part * (1.0 - sigmoid)),
            grad_active * silu,
        ],
        axis=1,
    ).astype(BF)
    grad_in = dot(grad_hidden, upper_w, ((1,), (1,))).astype(BF)
    grad_gates = lax.dynamic_update_slice_in_dim(
        jnp.zeros((total_rows, LANES), BF), grad_gates.astype(BF), first_expert, 1
    )
    mixed = dot(active_gated, lower_w, ((1,), (1,))).astype(BF)
    back_sub = lax.psum_scatter(
        jnp.concatenate([grad_in, grad_gates], axis=1), ALL, scatter_dimension=0, tiled=True
    ).astype(F32)
    mixed_sub = lax.psum_scatter(mixed, ALL, scatter_dimension=0, tiled=True).astype(F32)
    grad_upper = dot(h_all, grad_hidden, ((0,), (0,))).astype(BF)
    grad_lower = dot(cot_all, active_gated, ((0,), (0,))).astype(BF)
    grad_expert = jnp.concatenate([grad_upper, grad_lower], axis=1).reshape(nd, d_local, 3 * width)
    grad_expert = exchange(grad_expert, dp_at, nd)
    grad_expert = lax.all_gather(grad_expert, "ctx", axis=0)
    grad_up = grad_expert[..., : 2 * width].reshape(nc, nd, d_local, 2, own_count, units)
    grad_low = grad_expert[..., 2 * width :].reshape(nc, nd, d_local, own_count, units)
    if by_expert:
        grad_up = jnp.transpose(grad_up, (2, 0, 4, 3, 1, 5))
        grad_low = jnp.transpose(grad_low, (2, 0, 3, 1, 4))
    else:
        grad_up = jnp.transpose(grad_up, (2, 4, 3, 1, 0, 5))
        grad_low = jnp.transpose(grad_low, (2, 3, 1, 0, 4))
    grad_expert_in = grad_up.reshape(d_local, local_count, 2 * FF).astype(F32)
    grad_expert_out = grad_low.reshape(d_local, local_count, FF).astype(F32)

    result = lax.all_to_all((middle + mixed_sub).astype(BF), "tensor", 1, 0, tiled=True)

    gate_grads = back_sub[:, D : D + EXPERTS] * kept
    logit_grads = (
        gates * (gate_grads - jnp.sum(gates * gate_grads, axis=1, keepdims=True))
    ).astype(BF)
    grad_norm_two = back_sub[:, :D] + dot(logit_grads, router_w, ((1,), (1,)))
    grad_middle, grad_gain_two = norm_backward(middle, gain_two_full, inverse_two, grad_norm_two)
    grad_middle = grad_middle + cot_sub.astype(F32)
    extra = jnp.zeros((sub, LANES - EXPERTS), BF)
    grad_attn = lax.all_gather(
        jnp.concatenate([grad_middle.astype(BF), logit_grads, extra], axis=1),
        "tensor",
        axis=0,
        tiled=True,
    )
    logit_grads_full = grad_attn[:, D : D + EXPERTS]
    grad_attn = grad_attn[:, :D]
    h_two_full = lax.dynamic_slice_in_dim(h_all, (dp_at * nc + ctx_at) * n_rows, n_rows, 0)
    grad_router = dot(h_two_full, logit_grads_full, ((0,), (0,)))

    grad_output_w = dot(grad_attn, attended, ((0,), (0,)))
    grad_blended = (
        dot(grad_attn, output_w, ((1,), (0,)))
        .astype(BF)
        .reshape(n_rows, kv_heads, group, HEAD_DIM)
    )
    shares = jnp.exp(scores - log_totals)
    grad_shares = jnp.einsum(
        "bagd,pad->agbp", grad_blended, value_heads, preferred_element_type=F32
    )
    inner = jnp.sum(shares * grad_shares, axis=-1, keepdims=True)
    grad_scores = (shares * (grad_shares - inner)).astype(BF)
    grad_queries = score_scale * jnp.einsum(
        "agbp,pad->bagd", grad_scores, key_heads, preferred_element_type=F32
    )
    grad_keys = score_scale * jnp.einsum(
        "agbp,bagd->pad", grad_scores, queries, preferred_element_type=F32
    )
    grad_values = jnp.einsum(
        "agbp,bagd->pad", shares_low, grad_blended, preferred_element_type=F32
    )
    grad_kv = lax.psum_scatter(
        jnp.concatenate(
            [grad_keys.reshape(pack_len, kv_width), grad_values.reshape(pack_len, kv_width)],
            axis=1,
        ).astype(BF),
        "ctx",
        scatter_dimension=0,
        tiled=True,
    ).astype(F32)
    grad_turned = jnp.concatenate(
        [
            grad_queries.reshape(n_rows, q_heads, HEAD_DIM),
            grad_kv[:, :kv_width].reshape(n_rows, kv_heads, HEAD_DIM),
        ],
        axis=1,
    )
    grad_qkv = jnp.concatenate(
        [
            rotate(grad_turned, cosine_table, -sine_table)
            .astype(BF)
            .reshape(n_rows, q_width + kv_width),
            grad_kv[:, kv_width:].astype(BF),
        ],
        axis=1,
    )
    qkv_full = lax.all_gather(qkv_w, "tensor", axis=1, tiled=True)
    grad_qkv_sub = lax.all_to_all(grad_qkv, "tensor", 0, 1, tiled=True)
    grad_norm_one = dot(grad_qkv_sub, qkv_full, ((1,), (1,)))
    inverse_sub = lax.rsqrt(jnp.mean(tokens_sub * tokens_sub, axis=1, keepdims=True) + EPS)
    grad_tokens, grad_gain_one = norm_backward(
        tokens_sub, gain_one_full, inverse_sub, grad_norm_one
    )
    grad_tokens = lax.all_to_all(grad_tokens + grad_middle, "tensor", 1, 0, tiled=True)

    grad_qkv_w = dot(h_one, grad_qkv, ((0,), (0,)))
    weight_grads = jnp.concatenate([grad_qkv_w, grad_output_w, grad_router], axis=1).astype(BF)
    weight_grads = lax.psum_scatter(weight_grads, ("dp", "ctx"), scatter_dimension=0, tiled=True)
    weight_grads = lax.all_gather(weight_grads, "ctx", axis=0, tiled=True).astype(F32)
    edges = [0, q_width, q_width + kv_width, qkv_width, qkv_width + q_width]
    gain_grads = lax.psum(jnp.stack([grad_gain_one, grad_gain_two]), ALL)
    gain_grads = lax.dynamic_slice_in_dim(gain_grads, tensor_at * part_width, part_width, 1)
    return (
        result,
        grad_tokens,
        gain_grads[0],
        weight_grads[:, edges[0] : edges[1]],
        weight_grads[:, edges[1] : edges[2]],
        weight_grads[:, edges[2] : edges[3]],
        weight_grads[:, edges[3] : edges[4]],
        gain_grads[1],
        weight_grads[:, edges[4] :],
        grad_expert_in,
        grad_expert_out,
    )


def solution(mesh):
    return jax.shard_map(
        on_device,
        mesh=mesh,
        in_specs=(
            P(("dp", "ctx"), "tensor"),
            P("dp", None),
            P("dp", None),
            P("dp", None),
            P("tensor"),
            P("dp", "tensor"),
            P("dp", "tensor"),
            P("dp", "tensor"),
            P("dp", "tensor"),
            P("tensor"),
            P("dp", None),
            P("dp", "tensor", None),
            P("dp", "tensor", None),
            P(("dp", "ctx"), "tensor"),
        ),
        out_specs=(
            P(("dp", "ctx"), "tensor"),
            P(("dp", "ctx"), "tensor"),
            P("tensor"),
            P("dp", "tensor"),
            P("dp", "tensor"),
            P("dp", "tensor"),
            P("dp", "tensor"),
            P("tensor"),
            P("dp", None),
            P("dp", "tensor", None),
            P("dp", "tensor", None),
        ),
        check_vma=False,
    )
```

```python
import jax
import jax.numpy as jnp
from jax import lax
from jax.experimental import pallas as pl
from jax.experimental.pallas import tpu as pltpu
from jax.sharding import PartitionSpec as P

D = 1536
HEAD_DIM = 64
EXPERTS = 40
TOP_K = 8
FF = 512
EPS = 1e-06
THETA = 10000.0
NEG = -1e30
LANES = 128
ALL = ("dp", "ctx", "tensor")
BF = jnp.bfloat16
F32 = jnp.float32
MESH = pl.DeviceIdType.MESH
COST = pl.CostEstimate(flops=0, bytes_accessed=250_000_000, transcendentals=0)


def place():
    ctx = lax.axis_index("ctx")
    return (lax.axis_index("dp"), ctx // 2, ctx % 2, lax.axis_index("tensor"))


def device(z, y, k, x):
    return {"dp": z, "ctx": y * 2 + k, "tensor": x}


def greet(partners):
    barrier = pltpu.get_barrier_semaphore()
    for partner in partners:
        pl.semaphore_signal(barrier, inc=1, device_id=partner, device_id_type=MESH)
    pl.semaphore_wait(barrier, len(partners))


def partners_of(nd, z, y, k, x):
    return [device((z + hop) % nd, y, k, x) for hop in range(1, nd)] + [
        device(z, y, k, 1 - x),
        device(z, 1 - y, k, x),
        device(z, y, 1 - k, x),
    ]


def gather_kernel(own_ref, out_ref, local_sem, send_sem, recv_sem):
    nd, width = (out_ref.shape[0], own_ref.shape[2])
    wide = out_ref.shape[-1] != width
    z, y, k, x = place()
    up, down = (device((z + 1) % nd, y, k, x), device((z + nd - 1) % nd, y, k, x))
    greet([up, down, device(z, y, k, 1 - x), device(z, 1 - y, k, x), device(z, y, 1 - k, x)])
    low = jnp.minimum(z, nd - 1 - z)
    places = []
    for step in range(nd):
        near = (step + 1) // 2
        zigzag = low + near if step % 2 else low - near
        from_low = jnp.where(step <= 2 * low, zigzag, step)
        places.append(jnp.where(2 * z < nd, from_low, nd - 1 - from_low))
    sends = []

    def at(piece):
        step, dy, dk, dx, half = piece
        chip, core, side = ((y + dy) % 2, (k + dk) % 2, (x + dx) % 2)
        if not wide:
            return out_ref.at[places[step], chip, core, side, half]
        columns = pl.ds(pl.multiple_of(side * width, LANES), width)
        return out_ref.at[places[step], chip, core, half, :, columns]

    def slot(piece):
        step, dy, dk, dx, half = piece
        return (((places[step] * 2 + dy) * 2 + dk) * 2 + dx) * 2 + half

    def send(piece, link, condition=None):
        step, dy, dk, dx, half = piece
        if link == "up":
            target, there = (up, piece)
        elif link == "down":
            target, there = (down, piece)
        elif link == "x":
            target, there = (device(z, y, k, 1 - x), (step, dy, dk, 1 - dx, half))
        elif link == "y":
            target, there = (device(z, 1 - y, k, x), (step, 1 - dy, dk, dx, half))
        else:
            target, there = (device(z, y, 1 - k, x), (step, dy, 1 - dk, dx, half))
        own = piece[:4] == (0, 0, 0, 0)
        copy = pltpu.make_async_remote_copy(
            src_ref=own_ref.at[half] if own else at(piece),
            dst_ref=at(piece),
            send_sem=send_sem.at[len(sends)],
            recv_sem=recv_sem.at[slot(there)],
            device_id=target,
            device_id_type=MESH,
        )
        if condition is None:
            copy.start()
        else:
            pl.when(condition)(copy.start)
        sends.append((copy, condition))

    def arrived(piece):
        pltpu.make_async_remote_copy(
            src_ref=at(piece),
            dst_ref=at(piece),
            send_sem=send_sem.at[0],
            recv_sem=recv_sem.at[slot(piece)],
            device_id=device(z, y, k, 1 - x),
            device_id_type=MESH,
        ).wait_recv()

    own_copies = []
    for half in range(2):
        own_copy = pltpu.make_async_copy(
            own_ref.at[half], at((0, 0, 0, 0, half)), local_sem.at[half]
        )
        own_copy.start()
        own_copies.append(own_copy)
    links = (("x", "y"), ("y", "x"))
    for step in range(nd + 2):
        if step < nd:
            came = places[step]
            for half in range(2):
                piece = (step, 0, 0, 0, half)
                if step:
                    arrived(piece)
                send(piece, "up", (came <= z) & (z < nd - 1))
                send(piece, "down", (came >= z) & (z > 0))
                send(piece, links[half][0])
            for half in range(2):
                piece = (step, 0, 0, 0, half)
                send(piece, links[half][1])
                send(piece, "k")
        if 1 <= step < nd + 1:
            for half in range(2):
                piece = (step - 1, half, 0, 1 - half, half)
                arrived(piece)
                send(piece, links[half][1])
                send(piece, "k")
        if 2 <= step:
            for half in range(2):
                for d in range(2):
                    piece = (step - 2, 1, 0, d, 0) if half == 0 else (step - 2, d, 0, 1, 1)
                    arrived(piece)
                    send(piece, "k")
    for step in range(nd):
        for dy in range(2):
            for dx in range(2):
                for half in range(2):
                    arrived((step, dy, 1, dx, half))
    for own_copy in own_copies:
        own_copy.wait()
    for copy, condition in sends:
        if condition is None:
            copy.wait_send()
        else:
            pl.when(condition)(copy.wait_send)


def gather_rows(own, nd, collective_id, wide=False):
    rows, width = own.shape
    half = rows // 2
    shape = (nd, 2, 2, 2, half, 2 * width) if wide else (nd, 2, 2, 2, 2, half, width)
    out = pl.pallas_call(
        gather_kernel,
        in_specs=[pl.BlockSpec(memory_space=pltpu.VMEM)],
        out_specs=pl.BlockSpec(memory_space=pl.ANY),
        out_shape=jax.ShapeDtypeStruct(shape, own.dtype),
        scratch_shapes=[
            pltpu.SemaphoreType.DMA((2,)),
            pltpu.SemaphoreType.DMA((nd * 18,)),
            pltpu.SemaphoreType.DMA((nd * 16,)),
        ],
        compiler_params=pltpu.CompilerParams(collective_id=collective_id, has_side_effects=True),
        cost_estimate=COST,
        name="gather_rows",
    )(own.reshape(2, half, width))
    return out.reshape(-1, shape[-1])


def reduce_kernel(
    part_ref, out_ref, own, from_core, first, second, across, load_sem, send_sem, recv_sem
):
    nd = part_ref.shape[0]
    z, y, k, x = place()
    greet(partners_of(nd, z, y, k, x))
    order = [hop for hop in (2, 1, 3, 0)] if nd == 4 else list(range(1, nd)) + [0]
    sends, loads = ([], [])

    def spot(step, dy, dx, half):
        return ((step * 2 + dy) * 2 + dx) * 2 + half

    def send(source, there, target, slot):
        copy = pltpu.make_async_remote_copy(
            src_ref=source,
            dst_ref=there,
            send_sem=send_sem.at[len(sends)],
            recv_sem=recv_sem.at[slot],
            device_id=target,
            device_id_type=MESH,
        )
        copy.start()
        sends.append(copy)

    def arrived(there, slot):
        pltpu.make_async_remote_copy(
            src_ref=there,
            dst_ref=there,
            send_sem=send_sem.at[0],
            recv_sem=recv_sem.at[slot],
            device_id=device(z, y, k, 1 - x),
            device_id_type=MESH,
        ).wait_recv()

    def add(to, what, index):
        to_rows = own.shape[1]

        def body(i, carry):
            rows = pl.ds(i * 16, 16)
            total = own[to, rows, :].astype(F32) + what[index, rows, :].astype(F32)
            own[to, rows, :] = total.astype(BF)
            return carry

        lax.fori_loop(0, to_rows // 16, body, 0)

    core_slot, first_slot, second_slot, across_slot = (0, nd * 4, nd * 8, nd * 10)
    for step, dz in enumerate(order):
        for dy in range(2):
            for dx in range(2):
                there = pl.ds(spot(step, dy, dx, 0), 2)
                block = ((z + dz) % nd, (y + dy) % 2)
                send(
                    part_ref.at[block[0], block[1], 1 - k, (x + dx) % 2],
                    from_core.at[there],
                    device(z, y, 1 - k, x),
                    core_slot + (step * 2 + dy) * 2 + dx,
                )
                load = pltpu.make_async_copy(
                    part_ref.at[block[0], block[1], k, (x + dx) % 2],
                    own.at[there],
                    load_sem.at[len(loads)],
                )
                load.start()
                loads.append(load)
    x_partner, y_partner = (device(z, y, k, 1 - x), device(z, 1 - y, k, x))
    for step in range(nd + 2):
        if step < nd:
            for at in range(4):
                loads[step * 4 + at].wait()
                base = spot(step, 0, 0, 0) + at * 2
                arrived(from_core.at[pl.ds(base, 2)], core_slot + step * 4 + at)

            def pair(i, carry, step=step):
                add(step * 8 + i, from_core, step * 8 + i)
                return carry

            lax.fori_loop(0, 8, pair, 0)
            for d in range(2):
                slot = step * 4 + d
                send(own.at[spot(step, 1, d, 0)], first.at[slot], y_partner, first_slot + slot)
                slot = step * 4 + 2 + d
                send(own.at[spot(step, d, 1, 1)], first.at[slot], x_partner, first_slot + slot)
        if 1 <= step < nd + 1:
            now = step - 1
            for d in (1, 0):
                slot = now * 4 + d
                arrived(first.at[slot], first_slot + slot)
                add(spot(now, 0, d, 0), first, slot)
                slot = now * 4 + 2 + d
                arrived(first.at[slot], first_slot + slot)
                add(spot(now, d, 0, 1), first, slot)
                if d == 1:
                    slot = now * 2
                    send(own.at[spot(now, 0, 1, 0)], second.at[slot], x_partner, second_slot + slot)
                    slot = now * 2 + 1
                    send(own.at[spot(now, 1, 0, 1)], second.at[slot], y_partner, second_slot + slot)
        if 2 <= step:
            now = step - 2
            for half in range(2):
                slot = now * 2 + half
                arrived(second.at[slot], second_slot + slot)
                add(spot(now, 0, 0, half), second, slot)
            hop = order[now]
            if hop:
                slot = nd - hop - 1
                send(
                    own.at[pl.ds(spot(now, 0, 0, 0), 2)],
                    across.at[slot],
                    device((z + hop) % nd, y, k, x),
                    across_slot + slot,
                )
    for slot in range(nd - 1):
        arrived(across.at[slot], across_slot + slot)
    mine = spot(order.index(0), 0, 0, 0)
    for half in range(2):

        def total(i, carry, half=half):
            rows = pl.ds(i * 16, 16)
            value = own[mine + half, rows, :].astype(F32)
            for slot in range(nd - 1):
                value = value + across[slot, half, rows, :].astype(F32)
            out_ref[half, rows, :] = value
            return carry

        lax.fori_loop(0, own.shape[1] // 16, total, 0)
    for copy in sends:
        copy.wait_send()


def reduce_rows(part, nd, collective_id):
    total, width = part.shape
    rows = total // (nd * 8)
    half = rows // 2
    out = pl.pallas_call(
        reduce_kernel,
        in_specs=[pl.BlockSpec(memory_space=pl.ANY)],
        out_specs=pl.BlockSpec(memory_space=pltpu.VMEM),
        out_shape=jax.ShapeDtypeStruct((2, half, width), F32),
        scratch_shapes=[
            pltpu.VMEM((nd * 8, half, width), BF),
            pltpu.VMEM((nd * 8, half, width), BF),
            pltpu.VMEM((nd * 4, half, width), BF),
            pltpu.VMEM((nd * 2, half, width), BF),
            pltpu.VMEM((nd - 1, 2, half, width), BF),
            pltpu.SemaphoreType.DMA((nd * 4,)),
            pltpu.SemaphoreType.DMA((nd * 11,)),
            pltpu.SemaphoreType.DMA((nd * 11,)),
        ],
        compiler_params=pltpu.CompilerParams(
            collective_id=collective_id, has_side_effects=True, vmem_limit_bytes=48 << 20
        ),
        cost_estimate=COST,
        name="reduce_rows",
    )(part.reshape(nd, 2, 2, 2, 2, half, width))
    return out.reshape(rows, width)


def rope_tables(position):
    halves = HEAD_DIM // 2
    frequency = THETA ** (-2.0 * jnp.arange(halves, dtype=F32) / HEAD_DIM)
    angles = position[:, None] * frequency[None, :]
    return (jnp.cos(angles)[:, None, :], jnp.sin(angles)[:, None, :])


def rotate(values, cosine_table, sine_table):
    halves = values.shape[-1] // 2
    first_half, second_half = (values[..., :halves], values[..., halves:])
    return jnp.concatenate(
        [
            first_half * cosine_table - second_half * sine_table,
            second_half * cosine_table + first_half * sine_table,
        ],
        axis=-1,
    )


def dot(a, b, dims):
    return lax.dot_general(a, b, (dims, ((), ())), preferred_element_type=F32)


def norm_forward(rows, gain):
    inverse = lax.rsqrt(jnp.mean(rows * rows, axis=1, keepdims=True) + EPS)
    return (inverse, (rows * inverse * gain[None, :]).astype(BF))


def norm_backward(rows, gain, inverse, grad_normed):
    weighted = grad_normed * gain[None, :]
    inner = jnp.sum(weighted * rows, axis=1, keepdims=True)
    grad_rows = weighted * inverse - rows * (inverse * inverse * inverse * inner / D)
    return (grad_rows, jnp.sum(grad_normed * rows * inverse, axis=0))


def exchange(parts, at, count):
    result = lax.dynamic_update_index_in_dim(
        jnp.zeros_like(parts), lax.dynamic_index_in_dim(parts, at, 0), at, 0
    )
    for hop in range(1, count):
        sent = lax.dynamic_index_in_dim(parts, (at + hop) % count, 0)
        got = lax.ppermute(sent, "dp", [(i, (i + hop) % count) for i in range(count)])
        result = lax.dynamic_update_index_in_dim(result, got, (at - hop) % count, 0)
    return result


def expert_major_kernel(gate_ref, up_ref, low_ref, out_ref):
    count, units = (gate_ref.shape[0], gate_ref.shape[2])
    for part, ref in enumerate((gate_ref, up_ref, low_ref)):
        for at in range(count):
            out_ref[0, :, (part * count + at) * units : (part * count + at + 1) * units] = ref[at]


def expert_major(received, own_count, units):
    nd, d_local, _ = received.shape

    def spec(part):
        return pl.BlockSpec((nd, d_local, units), lambda e: (0, 0, part * own_count + e))

    return pl.pallas_call(
        expert_major_kernel,
        grid=(own_count,),
        in_specs=[spec(0), spec(1), spec(2)],
        out_specs=pl.BlockSpec((1, d_local, 3 * nd * units), lambda e: (e, 0, 0)),
        out_shape=jax.ShapeDtypeStruct((own_count, d_local, 3 * nd * units), received.dtype),
        name="expert_major",
    )(received, received, received)


def scatter_rows(partial, at, count):
    if count != 2:
        return lax.psum_scatter(
            partial.astype(BF), "tensor", scatter_dimension=0, tiled=True
        ).astype(F32)
    half = partial.shape[0] // 2
    sent = lax.dynamic_slice_in_dim(partial, (1 - at) * half, half, 0).astype(BF)
    got = lax.ppermute(sent, "tensor", [(0, 1), (1, 0)])
    return lax.dynamic_slice_in_dim(partial, at * half, half, 0) + got.astype(F32)


def on_device(
    tokens,
    segments,
    order,
    routes,
    gain_one,
    w_query,
    w_key,
    w_value,
    w_output,
    gain_two,
    w_router,
    w_expert_in,
    w_expert_out,
    cotangent,
):
    nd, nc, nt = (lax.axis_size("dp"), lax.axis_size("ctx"), lax.axis_size("tensor"))
    dp_at, ctx_at, tensor_at = (
        lax.axis_index("dp"),
        lax.axis_index("ctx"),
        lax.axis_index("tensor"),
    )
    n_rows, part_width = tokens.shape
    sub = n_rows // nt
    pack_len = order.shape[1]
    d_local = w_query.shape[0]
    q_width, kv_width = (w_query.shape[1], w_key.shape[1])
    q_heads, kv_heads = (q_width // HEAD_DIM, kv_width // HEAD_DIM)
    group = q_heads // kv_heads
    qkv_width = q_width + 2 * kv_width
    local_count = w_expert_in.shape[1]
    capacity = n_rows * 3 // 8

    gains = lax.all_gather(jnp.stack([gain_one, gain_two]), "tensor", axis=1, tiled=True)
    gain_one_full, gain_two_full = (gains[0], gains[1])
    tokens_full = lax.all_gather(tokens, "tensor", axis=1, tiled=True)
    packed = jnp.concatenate([w_query, w_key, w_value, w_router], axis=1)
    share = d_local // nc
    packed = lax.dynamic_slice_in_dim(packed, ctx_at * share, share, 0)
    packed = lax.all_gather(packed, ("dp", "ctx"), axis=0, tiled=True)
    qkv_w, router_w = (packed[:, :qkv_width], packed[:, qkv_width:])
    output_w = lax.all_gather(
        lax.dynamic_slice_in_dim(w_output, ctx_at * share, share, 0),
        ("dp", "ctx"),
        axis=0,
        tiled=True,
    )
    kernels = (nd, nc, nt) == (4, 4, 2)
    if kernels:
        cot_all = gather_rows(cotangent, nd, 1, wide=True)
        cot_sub = lax.dynamic_slice_in_dim(
            cot_all, (dp_at * nc + ctx_at) * n_rows + tensor_at * sub, sub, 0
        )
    else:
        cot_sub = lax.all_to_all(cotangent, "tensor", 0, 1, tiled=True)
        cot_all = lax.all_gather(cot_sub, ALL, axis=0, tiled=True)
    tokens_sub = lax.dynamic_slice_in_dim(tokens_full, tensor_at * sub, sub, 0).astype(F32)

    by_expert = local_count % nc == 0
    own_count = local_count // nc if by_expert else local_count
    units = FF // nd if by_expert else FF // (nd * nc)
    first_expert = tensor_at * local_count + (ctx_at * own_count if by_expert else 0)
    if by_expert:
        own_in = lax.dynamic_slice_in_dim(w_expert_in, ctx_at * own_count, own_count, 1)
        own_out = lax.dynamic_slice_in_dim(w_expert_out, ctx_at * own_count, own_count, 1)
        own_in = own_in.reshape(d_local, own_count, 2, nd, units)
        own_out = own_out.reshape(d_local, own_count, nd, units)
    else:
        own_in = w_expert_in.reshape(d_local, own_count, 2, nd, nc, units)
        own_out = w_expert_out.reshape(d_local, own_count, nd, nc, units)
        own_in = lax.dynamic_index_in_dim(own_in, ctx_at, 4, False)
        own_out = lax.dynamic_index_in_dim(own_out, ctx_at, 3, False)
    own_in = jnp.transpose(own_in, (3, 0, 2, 1, 4)).reshape(nd, d_local, 2 * own_count * units)
    own_out = jnp.transpose(own_out, (2, 0, 1, 3)).reshape(nd, d_local, own_count * units)
    width = own_count * units
    expert_parts = jnp.concatenate([own_in, own_out], axis=2)
    tokens_full, expert_parts = lax.optimization_barrier((tokens_full, expert_parts))
    expert_w = exchange(expert_parts, dp_at, nd)

    order_row = order[0]
    places = jnp.arange(pack_len, dtype=jnp.int32)
    dealt = jnp.sum(jnp.where(order_row[:, None] == places[None, :], places[:, None], 0), axis=0)
    sub_start = ctx_at * n_rows + tensor_at * sub
    dealt_sub = lax.dynamic_slice_in_dim(dealt, sub_start, sub)
    experts_all = jnp.arange(EXPERTS, dtype=jnp.int32)
    uses = jnp.any(routes[:, :, None] == experts_all[None, None, :], axis=1)
    earlier = (dealt_sub[:, None] // n_rows == dealt[None, :] // n_rows) & (
        dealt[None, :] < dealt_sub[:, None]
    )
    ranks = dot(earlier.astype(BF), uses.astype(BF), ((1,), (0,)))
    uses_sub = lax.dynamic_slice_in_dim(uses, sub_start, sub, 0)
    kept = (uses_sub & (ranks < capacity)).astype(F32)

    segment_row = segments[0]
    local_segs = lax.dynamic_slice_in_dim(segment_row, ctx_at * n_rows, n_rows)
    local_places = ctx_at * n_rows + jnp.arange(n_rows, dtype=jnp.int32)
    starts = jnp.sum((segment_row[None, :] < local_segs[:, None]).astype(jnp.int32), axis=1)
    cosine_table, sine_table = rope_tables((local_places - starts).astype(F32))
    _, h_one = norm_forward(tokens_full.astype(F32), gain_one_full)
    if kernels:
        h_one, cot_all, cot_sub = lax.optimization_barrier((h_one, cot_all, cot_sub))
    projected = dot(h_one, qkv_w, ((1,), (0,)))
    turned = rotate(
        projected[:, : q_width + kv_width].reshape(n_rows, q_heads + kv_heads, HEAD_DIM),
        cosine_table,
        sine_table,
    ).astype(BF)
    queries = turned[:, :q_heads].reshape(n_rows, kv_heads, group, HEAD_DIM)
    kv_rows = jnp.concatenate(
        [
            turned[:, q_heads:].reshape(n_rows, kv_width),
            projected[:, q_width + kv_width :].astype(BF),
        ],
        axis=1,
    )
    kv_all = lax.all_gather(kv_rows, "ctx", axis=0, tiled=True)
    key_heads = kv_all[:, :kv_width].reshape(pack_len, kv_heads, HEAD_DIM)
    value_heads = kv_all[:, kv_width:].reshape(pack_len, kv_heads, HEAD_DIM)
    allowed = (local_segs[:, None] == segment_row[None, :]) & (
        local_places[:, None] >= places[None, :]
    )
    score_scale = HEAD_DIM ** (-0.5)
    scores = score_scale * jnp.einsum(
        "bagd,pad->agbp", queries, key_heads, preferred_element_type=F32
    )
    scores = jnp.where(allowed[None, None], scores, NEG)
    highest = jnp.max(scores, axis=-1, keepdims=True)
    weights = jnp.exp(scores - highest)
    totals = jnp.sum(weights, axis=-1, keepdims=True)
    shares_low = (weights / totals).astype(BF)
    log_totals = highest + jnp.log(totals)
    attended = (
        jnp.einsum("agbp,pad->bagd", shares_low, value_heads, preferred_element_type=F32)
        .astype(BF)
        .reshape(n_rows, q_width)
    )
    middle = tokens_sub + scatter_rows(dot(attended, output_w, ((1,), (1,))), tensor_at, nt)

    inverse_two, h_two = norm_forward(middle, gain_two_full)
    logits = jnp.where(uses_sub, dot(h_two, router_w, ((1,), (0,))), NEG)
    raised = jnp.exp(logits - jnp.max(logits, axis=1, keepdims=True))
    gates = raised / jnp.sum(raised, axis=1, keepdims=True)
    gates_kept = gates * kept
    gates_high = gates_kept.astype(BF)
    gates_low = (gates_kept - gates_high.astype(F32)).astype(BF)
    extra = jnp.zeros((sub, LANES - 2 * EXPERTS), BF)
    h_ext = jnp.concatenate([h_two, gates_high, gates_low, extra], axis=1)
    h_ext, expert_w = lax.optimization_barrier((h_ext, expert_w))
    expert_w = expert_w.reshape(D, 3 * width)
    upper_w, lower_w = (expert_w[:, : 2 * width], expert_w[:, 2 * width :])
    if kernels:
        h_all = gather_rows(h_ext, nd, 2)
    else:
        h_all = lax.all_gather(h_ext, ALL, axis=0, tiled=True)
    gates_all = (
        h_all[:, D : D + EXPERTS].astype(F32) + h_all[:, D + EXPERTS : D + 2 * EXPERTS].astype(F32)
    )
    total_rows = h_all.shape[0]
    gates_own = lax.dynamic_slice_in_dim(gates_all, first_expert, own_count, 1)
    h_all = h_all[:, :D]

    gate_wide = jnp.broadcast_to(gates_own[:, :, None], (total_rows, own_count, units)).reshape(
        total_rows, width
    )
    hidden = dot(h_all, upper_w, ((1,), (0,)))
    grad_raw = dot(cot_all, lower_w, ((1,), (0,)))
    gate_part, up_part = (hidden[:, :width], hidden[:, width:])
    sigmoid = jax.nn.sigmoid(gate_part)
    silu = gate_part * sigmoid
    active = (silu * up_part).astype(BF).astype(F32)
    active_gated = (active * gate_wide).astype(BF)
    grad_gates = jnp.sum((grad_raw * active).reshape(total_rows, own_count, units), axis=2)
    grad_active = grad_raw * gate_wide
    grad_hidden = jnp.concatenate(
        [
            grad_active * up_part * sigmoid * (1.0 + gate_part * (1.0 - sigmoid)),
            grad_active * silu,
        ],
        axis=1,
    ).astype(BF)
    grad_in = dot(grad_hidden, upper_w, ((1,), (1,))).astype(BF)
    grad_gates = lax.dynamic_update_slice_in_dim(
        jnp.zeros((total_rows, LANES), BF), grad_gates.astype(BF), first_expert, 1
    )
    mixed = dot(active_gated, lower_w, ((1,), (1,))).astype(BF)
    back = jnp.concatenate([grad_in, grad_gates], axis=1)
    grad_upper = dot(h_all, grad_hidden, ((0,), (0,))).astype(BF)
    grad_lower = dot(cot_all, active_gated, ((0,), (0,))).astype(BF)
    grad_expert = jnp.concatenate([grad_upper, grad_lower], axis=1).reshape(nd, d_local, 3 * width)
    if kernels:
        back, grad_expert = lax.optimization_barrier((back, grad_expert))
        back_sub = reduce_rows(back, nd, 3)
        mixed, back_sub = lax.optimization_barrier((mixed, back_sub))
        mixed_sub = reduce_rows(mixed, nd, 4)
        back_sub, mixed_sub = lax.optimization_barrier((back_sub, mixed_sub))
    else:
        back_sub = lax.psum_scatter(back, ALL, scatter_dimension=0, tiled=True).astype(F32)
        mixed_sub = lax.psum_scatter(mixed, ALL, scatter_dimension=0, tiled=True).astype(F32)
    grad_expert = exchange(grad_expert, dp_at, nd)
    if by_expert:
        grad_expert = expert_major(grad_expert, own_count, units)
        grad_expert = lax.all_gather(grad_expert, "ctx", axis=0, tiled=True)
        grad_expert = jnp.transpose(grad_expert, (1, 0, 2)).astype(F32)
        grad_expert_in, grad_expert_out = (grad_expert[..., : 2 * FF], grad_expert[..., 2 * FF :])
    else:
        grad_expert = lax.all_gather(grad_expert, "ctx", axis=0)
        grad_up = grad_expert[..., : 2 * width].reshape(nc, nd, d_local, 2, own_count, units)
        grad_low = grad_expert[..., 2 * width :].reshape(nc, nd, d_local, own_count, units)
        grad_up = jnp.transpose(grad_up, (2, 4, 3, 1, 0, 5))
        grad_low = jnp.transpose(grad_low, (2, 3, 1, 0, 4))
        grad_expert_in = grad_up.reshape(d_local, local_count, 2 * FF).astype(F32)
        grad_expert_out = grad_low.reshape(d_local, local_count, FF).astype(F32)

    result = lax.all_to_all((middle + mixed_sub).astype(BF), "tensor", 1, 0, tiled=True)

    gate_grads = back_sub[:, D : D + EXPERTS] * kept
    logit_grads = (
        gates * (gate_grads - jnp.sum(gates * gate_grads, axis=1, keepdims=True))
    ).astype(BF)
    grad_norm_two = back_sub[:, :D] + dot(logit_grads, router_w, ((1,), (1,)))
    grad_middle, grad_gain_two = norm_backward(middle, gain_two_full, inverse_two, grad_norm_two)
    grad_middle = grad_middle + cot_sub.astype(F32)
    extra = jnp.zeros((sub, LANES - EXPERTS), BF)
    grad_attn = lax.all_gather(
        jnp.concatenate([grad_middle.astype(BF), logit_grads, extra], axis=1),
        "tensor",
        axis=0,
        tiled=True,
    )
    logit_grads_full = grad_attn[:, D : D + EXPERTS]
    grad_attn = grad_attn[:, :D]
    h_two_full = lax.dynamic_slice_in_dim(h_all, (dp_at * nc + ctx_at) * n_rows, n_rows, 0)
    grad_router = dot(h_two_full, logit_grads_full, ((0,), (0,)))

    grad_output_w = dot(grad_attn, attended, ((0,), (0,)))
    grad_blended = (
        dot(grad_attn, output_w, ((1,), (0,)))
        .astype(BF)
        .reshape(n_rows, kv_heads, group, HEAD_DIM)
    )
    shares = jnp.exp(scores - log_totals)
    grad_shares = jnp.einsum(
        "bagd,pad->agbp", grad_blended, value_heads, preferred_element_type=F32
    )
    inner = jnp.sum(shares * grad_shares, axis=-1, keepdims=True)
    grad_scores = (shares * (grad_shares - inner)).astype(BF)
    grad_queries = score_scale * jnp.einsum(
        "agbp,pad->bagd", grad_scores, key_heads, preferred_element_type=F32
    )
    grad_keys = score_scale * jnp.einsum(
        "agbp,bagd->pad", grad_scores, queries, preferred_element_type=F32
    )
    grad_values = jnp.einsum(
        "agbp,bagd->pad", shares_low, grad_blended, preferred_element_type=F32
    )
    grad_kv = lax.psum_scatter(
        jnp.concatenate(
            [grad_keys.reshape(pack_len, kv_width), grad_values.reshape(pack_len, kv_width)],
            axis=1,
        ).astype(BF),
        "ctx",
        scatter_dimension=0,
        tiled=True,
    ).astype(F32)
    grad_turned = jnp.concatenate(
        [
            grad_queries.reshape(n_rows, q_heads, HEAD_DIM),
            grad_kv[:, :kv_width].reshape(n_rows, kv_heads, HEAD_DIM),
        ],
        axis=1,
    )
    grad_qkv = jnp.concatenate(
        [
            rotate(grad_turned, cosine_table, -sine_table)
            .astype(BF)
            .reshape(n_rows, q_width + kv_width),
            grad_kv[:, kv_width:].astype(BF),
        ],
        axis=1,
    )
    grad_norm_one = scatter_rows(dot(grad_qkv, qkv_w, ((1,), (1,))), tensor_at, nt)
    inverse_sub = lax.rsqrt(jnp.mean(tokens_sub * tokens_sub, axis=1, keepdims=True) + EPS)
    grad_tokens, grad_gain_one = norm_backward(
        tokens_sub, gain_one_full, inverse_sub, grad_norm_one
    )
    grad_tokens = lax.all_to_all(grad_tokens + grad_middle, "tensor", 1, 0, tiled=True)

    grad_qkv_w = dot(h_one, grad_qkv, ((0,), (0,)))
    weight_grads = jnp.concatenate([grad_qkv_w, grad_output_w, grad_router], axis=1).astype(BF)
    weight_grads = lax.psum_scatter(weight_grads, ("dp", "ctx"), scatter_dimension=0, tiled=True)
    weight_grads = lax.all_gather(weight_grads, "ctx", axis=0, tiled=True).astype(F32)
    edges = [0, q_width, q_width + kv_width, qkv_width, qkv_width + q_width]
    gain_grads = jnp.sum(
        lax.all_gather(jnp.stack([grad_gain_one, grad_gain_two]), ALL, axis=0), axis=0
    )
    gain_grads = lax.dynamic_slice_in_dim(gain_grads, tensor_at * part_width, part_width, 1)
    return (
        result,
        grad_tokens,
        gain_grads[0],
        weight_grads[:, edges[0] : edges[1]],
        weight_grads[:, edges[1] : edges[2]],
        weight_grads[:, edges[2] : edges[3]],
        weight_grads[:, edges[3] : edges[4]],
        gain_grads[1],
        weight_grads[:, edges[4] :],
        grad_expert_in,
        grad_expert_out,
    )


def solution(mesh):
    return jax.shard_map(
        on_device,
        mesh=mesh,
        in_specs=(
            P(("dp", "ctx"), "tensor"),
            P("dp", None),
            P("dp", None),
            P("dp", None),
            P("tensor"),
            P("dp", "tensor"),
            P("dp", "tensor"),
            P("dp", "tensor"),
            P("dp", "tensor"),
            P("tensor"),
            P("dp", None),
            P("dp", "tensor", None),
            P("dp", "tensor", None),
            P(("dp", "ctx"), "tensor"),
        ),
        out_specs=(
            P(("dp", "ctx"), "tensor"),
            P(("dp", "ctx"), "tensor"),
            P("tensor"),
            P("dp", "tensor"),
            P("dp", "tensor"),
            P("dp", "tensor"),
            P("dp", "tensor"),
            P("tensor"),
            P("dp", None),
            P("dp", "tensor", None),
            P("dp", "tensor", None),
        ),
        check_vma=False,
    )
```

```python
import functools

import jax
import jax.numpy as jnp
from jax import lax
from jax.experimental import pallas as pl
from jax.experimental.pallas import tpu as pltpu
from jax.sharding import PartitionSpec as P

D = 1536
HEAD_DIM = 64
EXPERTS = 40
TOP_K = 8
FF = 512
EPS = 1e-06
THETA = 10000.0
NEG = -1e30
LANES = 128
ALL = ("dp", "ctx", "tensor")
BF = jnp.bfloat16
F32 = jnp.float32
MESH = pl.DeviceIdType.MESH
COST = pl.CostEstimate(flops=0, bytes_accessed=250_000_000, transcendentals=0)


def place():
    ctx = lax.axis_index("ctx")
    return (lax.axis_index("dp"), ctx // 2, ctx % 2, lax.axis_index("tensor"))


def device(z, y, k, x):
    return {"dp": z, "ctx": y * 2 + k, "tensor": x}


def greet(partners):
    barrier = pltpu.get_barrier_semaphore()
    for partner in partners:
        pl.semaphore_signal(barrier, inc=1, device_id=partner, device_id_type=MESH)
    pl.semaphore_wait(barrier, len(partners))


def partners_of(nd, z, y, k, x):
    return [device((z + hop) % nd, y, k, x) for hop in range(1, nd)] + [
        device(z, y, k, 1 - x),
        device(z, 1 - y, k, x),
        device(z, y, 1 - k, x),
    ]


def gather_kernel(own_count, *refs):
    if own_count:
        own_ref, in_ref, low_ref, out_ref, upper_ref, lower_ref = refs[:6]
        move_local_sem, move_send_sem, move_recv_sem, local_sem, send_sem, recv_sem = refs[6:]
    else:
        own_ref, out_ref, local_sem, send_sem, recv_sem = refs
    nd, width = (out_ref.shape[0], own_ref.shape[2])
    wide = out_ref.shape[-1] != width
    z, y, k, x = place()
    up, down = (device((z + 1) % nd, y, k, x), device((z + nd - 1) % nd, y, k, x))
    greet(partners_of(nd, z, y, k, x))
    moves, kept = ([], [])

    def move(hop):
        rows, units = (in_ref.shape[1], low_ref.shape[2] // nd)
        to_z, from_z = ((z + hop) % nd, (z + nd - hop) % nd)
        for part in range(3):
            for e in range(own_count):
                source_ref, base = (in_ref, part * nd * units) if part < 2 else (low_ref, 0)
                to_ref = upper_ref if part < 2 else lower_ref
                columns = pl.ds((part % 2 * own_count + e) * units, units)
                source = source_ref.at[
                    (y * 2 + k) * own_count + e,
                    :,
                    pl.ds(pl.multiple_of(base + to_z * units, LANES), units),
                ]
                target = to_ref.at[pl.ds(pl.multiple_of(z * rows, 16), rows), columns]
                if hop == 0:
                    copy = pltpu.make_async_copy(source, target, move_local_sem.at[len(kept)])
                    copy.start()
                    kept.append(copy)
                    continue
                slot = len(moves)
                copy = pltpu.make_async_remote_copy(
                    src_ref=source,
                    dst_ref=target,
                    send_sem=move_send_sem.at[slot],
                    recv_sem=move_recv_sem.at[slot],
                    device_id=device(to_z, y, k, x),
                    device_id_type=MESH,
                )
                copy.start()
                arrival = to_ref.at[pl.ds(pl.multiple_of(from_z * rows, 16), rows), columns]
                moves.append((copy, arrival, slot))

    low = jnp.minimum(z, nd - 1 - z)
    places = []
    for step in range(nd):
        near = (step + 1) // 2
        zigzag = low + near if step % 2 else low - near
        from_low = jnp.where(step <= 2 * low, zigzag, step)
        places.append(jnp.where(2 * z < nd, from_low, nd - 1 - from_low))
    sends = []

    def at(piece):
        step, dy, dk, dx, half = piece
        chip, core, side = ((y + dy) % 2, (k + dk) % 2, (x + dx) % 2)
        if not wide:
            return out_ref.at[places[step], chip, core, side, half]
        columns = pl.ds(pl.multiple_of(side * width, LANES), width)
        return out_ref.at[places[step], chip, core, half, :, columns]

    def slot(piece):
        step, dy, dk, dx, half = piece
        return (((places[step] * 2 + dy) * 2 + dk) * 2 + dx) * 2 + half

    def send(piece, link, condition=None):
        step, dy, dk, dx, half = piece
        if link == "up":
            target, there = (up, piece)
        elif link == "down":
            target, there = (down, piece)
        elif link == "x":
            target, there = (device(z, y, k, 1 - x), (step, dy, dk, 1 - dx, half))
        elif link == "y":
            target, there = (device(z, 1 - y, k, x), (step, 1 - dy, dk, dx, half))
        else:
            target, there = (device(z, y, 1 - k, x), (step, dy, 1 - dk, dx, half))
        own = piece[:4] == (0, 0, 0, 0)
        copy = pltpu.make_async_remote_copy(
            src_ref=own_ref.at[half] if own else at(piece),
            dst_ref=at(piece),
            send_sem=send_sem.at[len(sends)],
            recv_sem=recv_sem.at[slot(there)],
            device_id=target,
            device_id_type=MESH,
        )
        if condition is None:
            copy.start()
        else:
            pl.when(condition)(copy.start)
        sends.append((copy, condition))

    def arrived(piece):
        pltpu.make_async_remote_copy(
            src_ref=at(piece),
            dst_ref=at(piece),
            send_sem=send_sem.at[0],
            recv_sem=recv_sem.at[slot(piece)],
            device_id=device(z, y, k, 1 - x),
            device_id_type=MESH,
        ).wait_recv()

    own_copies = []
    for half in range(2):
        own_copy = pltpu.make_async_copy(
            own_ref.at[half], at((0, 0, 0, 0, half)), local_sem.at[half]
        )
        own_copy.start()
        own_copies.append(own_copy)
    links = (("x", "y"), ("y", "x"))
    for step in range(nd + 2):
        if step < nd:
            came = places[step]
            for half in range(2):
                piece = (step, 0, 0, 0, half)
                if step:
                    arrived(piece)
                send(piece, "up", (came <= z) & (z < nd - 1))
                send(piece, "down", (came >= z) & (z > 0))
                send(piece, links[half][0])
            for half in range(2):
                piece = (step, 0, 0, 0, half)
                send(piece, links[half][1])
                send(piece, "k")
            if own_count:
                move((step + 1) % nd)
        if 1 <= step < nd + 1:
            for half in range(2):
                piece = (step - 1, half, 0, 1 - half, half)
                arrived(piece)
                send(piece, links[half][1])
                send(piece, "k")
        if 2 <= step:
            for half in range(2):
                for d in range(2):
                    piece = (step - 2, 1, 0, d, 0) if half == 0 else (step - 2, d, 0, 1, 1)
                    arrived(piece)
                    send(piece, "k")
    for step in range(nd):
        for dy in range(2):
            for dx in range(2):
                for half in range(2):
                    arrived((step, dy, 1, dx, half))
    for own_copy in own_copies + kept:
        own_copy.wait()
    for copy, arrival, slot in moves:
        pltpu.make_async_remote_copy(
            src_ref=arrival,
            dst_ref=arrival,
            send_sem=move_send_sem.at[slot],
            recv_sem=move_recv_sem.at[slot],
            device_id=device(z, y, k, 1 - x),
            device_id_type=MESH,
        ).wait_recv()
        copy.wait_send()
    for copy, condition in sends:
        if condition is None:
            copy.wait_send()
        else:
            pl.when(condition)(copy.wait_send)


def gather_rows(own, nd, collective_id, wide=False, weights=None, own_count=0):
    rows, width = own.shape
    half = rows // 2
    shape = (nd, 2, 2, 2, half, 2 * width) if wide else (nd, 2, 2, 2, 2, half, width)
    shapes = [jax.ShapeDtypeStruct(shape, own.dtype)]
    operands = [own.reshape(2, half, width)]
    semaphores = [
        pltpu.SemaphoreType.DMA((2,)),
        pltpu.SemaphoreType.DMA((nd * 18,)),
        pltpu.SemaphoreType.DMA((nd * 16,)),
    ]
    if weights:
        depth, count = (nd * weights[0].shape[1], 3 * own_count)
        operands += list(weights)
        units = weights[1].shape[2] // nd
        for parts in (2, 1):
            shapes.append(jax.ShapeDtypeStruct((depth, parts * own_count * units), own.dtype))
        semaphores = [
            pltpu.SemaphoreType.DMA((count,)),
            pltpu.SemaphoreType.DMA(((nd - 1) * count,)),
            pltpu.SemaphoreType.DMA(((nd - 1) * count,)),
        ] + semaphores
    out = pl.pallas_call(
        functools.partial(gather_kernel, own_count),
        in_specs=[pl.BlockSpec(memory_space=pltpu.VMEM)]
        + [pl.BlockSpec(memory_space=pl.ANY)] * (len(operands) - 1),
        out_specs=[pl.BlockSpec(memory_space=pl.ANY)] * len(shapes),
        out_shape=shapes,
        scratch_shapes=semaphores,
        compiler_params=pltpu.CompilerParams(collective_id=collective_id, has_side_effects=True),
        cost_estimate=COST,
        name="gather_rows",
    )(*operands)
    gathered = out[0].reshape(-1, shape[-1])
    return (gathered, out[1], out[2]) if weights else gathered


def reduce_kernel(count, *refs):
    parts, moved_ref, out_ref, arrived_ref = (refs[:count], *refs[count : count + 3])
    own, from_core, first, second, across, load_sem, send_sem, recv_sem = refs[count + 3 : -3]
    move_local_sem, move_send_sem, move_recv_sem = refs[-3:]
    nd = parts[0].shape[0]
    z, y, k, x = place()
    greet(partners_of(nd, z, y, k, x))
    order = [hop for hop in (2, 1, 3, 0)] if nd == 4 else list(range(1, nd)) + [0]
    sends, loads = ([], [])

    def spot(step, dy, dx, half):
        return ((step * 2 + dy) * 2 + dx) * 2 + half

    def send(source, there, target, slot):
        copy = pltpu.make_async_remote_copy(
            src_ref=source,
            dst_ref=there,
            send_sem=send_sem.at[len(sends)],
            recv_sem=recv_sem.at[slot],
            device_id=target,
            device_id_type=MESH,
        )
        copy.start()
        sends.append(copy)

    def arrived(there, slot):
        pltpu.make_async_remote_copy(
            src_ref=there,
            dst_ref=there,
            send_sem=send_sem.at[0],
            recv_sem=recv_sem.at[slot],
            device_id=device(z, y, k, 1 - x),
            device_id_type=MESH,
        ).wait_recv()

    def add(to, what, index):
        to_rows = own.shape[1]

        def body(i, carry):
            rows = pl.ds(i * 16, 16)
            total = own[to, rows, :].astype(F32) + what[index, rows, :].astype(F32)
            own[to, rows, :] = total.astype(BF)
            return carry

        lax.fori_loop(0, to_rows // 16, body, 0)

    spans, start = ([], 0)
    for ref in parts:
        spans.append(pl.ds(start, ref.shape[-1]))
        start += ref.shape[-1]
    first_slot, second_slot, across_slot, core_slot = (0, nd * 4, nd * 6, nd * 7)
    for step, dz in enumerate(order):
        for dy in range(2):
            for dx in range(2):
                there = pl.ds(spot(step, dy, dx, 0), 2)
                block = ((z + dz) % nd, (y + dy) % 2)
                for ref, span in zip(parts, spans):
                    send(
                        ref.at[block[0], block[1], 1 - k, (x + dx) % 2],
                        from_core.at[there, :, span],
                        device(z, y, 1 - k, x),
                        core_slot + len(loads),
                    )
                    load = pltpu.make_async_copy(
                        ref.at[block[0], block[1], k, (x + dx) % 2],
                        own.at[there, :, span],
                        load_sem.at[len(loads)],
                    )
                    load.start()
                    loads.append(load)
    x_partner, y_partner = (device(z, y, k, 1 - x), device(z, 1 - y, k, x))
    kept = pltpu.make_async_copy(moved_ref.at[z], arrived_ref.at[z], move_local_sem)
    kept.start()
    moves = []

    def move(hop):
        to_z = (z + hop) % nd
        copy = pltpu.make_async_remote_copy(
            src_ref=moved_ref.at[to_z],
            dst_ref=arrived_ref.at[z],
            send_sem=move_send_sem.at[hop - 1],
            recv_sem=move_recv_sem.at[hop - 1],
            device_id=device(to_z, y, k, x),
            device_id_type=MESH,
        )
        copy.start()
        moves.append((copy, hop))

    for step in range(nd + 2):
        if step == 0 or 3 <= step < nd + 1:
            move(step - 1 if step else 1)
        if step < nd:
            for at in range(4):
                base = spot(step, 0, 0, 0) + at * 2
                for which, span in enumerate(spans):
                    slot = (step * 4 + at) * count + which
                    loads[slot].wait()
                    arrived(from_core.at[pl.ds(base, 2), :, span], core_slot + slot)

            def pair(i, carry, step=step):
                add(step * 8 + i, from_core, step * 8 + i)
                return carry

            lax.fori_loop(0, 8, pair, 0)
            for d in range(2):
                slot = step * 4 + d
                send(own.at[spot(step, 1, d, 0)], first.at[slot], y_partner, first_slot + slot)
                slot = step * 4 + 2 + d
                send(own.at[spot(step, d, 1, 1)], first.at[slot], x_partner, first_slot + slot)
        if 1 <= step < nd + 1:
            now = step - 1
            for d in (1, 0):
                slot = now * 4 + d
                arrived(first.at[slot], first_slot + slot)
                add(spot(now, 0, d, 0), first, slot)
                slot = now * 4 + 2 + d
                arrived(first.at[slot], first_slot + slot)
                add(spot(now, d, 0, 1), first, slot)
                if d == 1:
                    slot = now * 2
                    send(own.at[spot(now, 0, 1, 0)], second.at[slot], x_partner, second_slot + slot)
                    slot = now * 2 + 1
                    send(own.at[spot(now, 1, 0, 1)], second.at[slot], y_partner, second_slot + slot)
        if 2 <= step:
            now = step - 2
            for half in range(2):
                slot = now * 2 + half
                arrived(second.at[slot], second_slot + slot)
                add(spot(now, 0, 0, half), second, slot)
            hop = order[now]
            if hop:
                slot = nd - hop - 1
                send(
                    own.at[pl.ds(spot(now, 0, 0, 0), 2)],
                    across.at[slot],
                    device((z + hop) % nd, y, k, x),
                    across_slot + slot,
                )
    for slot in range(nd - 1):
        arrived(across.at[slot], across_slot + slot)
    mine = spot(order.index(0), 0, 0, 0)
    for half in range(2):

        def total(i, carry, half=half):
            rows = pl.ds(i * 16, 16)
            value = own[mine + half, rows, :].astype(F32)
            for slot in range(nd - 1):
                value = value + across[slot, half, rows, :].astype(F32)
            out_ref[half, rows, :] = value
            return carry

        lax.fori_loop(0, own.shape[1] // 16, total, 0)
    kept.wait()
    for copy, hop in moves:
        there = arrived_ref.at[(z + nd - hop) % nd]
        pltpu.make_async_remote_copy(
            src_ref=there,
            dst_ref=there,
            send_sem=move_send_sem.at[hop - 1],
            recv_sem=move_recv_sem.at[hop - 1],
            device_id=x_partner,
            device_id_type=MESH,
        ).wait_recv()
        copy.wait_send()
    for copy in sends:
        copy.wait_send()


def reduce_rows(parts, moved, nd, collective_id):
    moved = moved.reshape(nd, moved.shape[0] // nd, moved.shape[1])
    rows = parts[0].shape[0] // (nd * 8)
    width = sum(part.shape[1] for part in parts)
    half, count = (rows // 2, len(parts))
    sends = nd * (4 * count + 7)
    out = pl.pallas_call(
        functools.partial(reduce_kernel, count),
        in_specs=[pl.BlockSpec(memory_space=pl.ANY)] * (count + 1),
        out_specs=[pl.BlockSpec(memory_space=pltpu.VMEM), pl.BlockSpec(memory_space=pl.ANY)],
        out_shape=[
            jax.ShapeDtypeStruct((2, half, width), F32),
            jax.ShapeDtypeStruct(moved.shape, moved.dtype),
        ],
        scratch_shapes=[
            pltpu.VMEM((nd * 8, half, width), BF),
            pltpu.VMEM((nd * 8, half, width), BF),
            pltpu.VMEM((nd * 4, half, width), BF),
            pltpu.VMEM((nd * 2, half, width), BF),
            pltpu.VMEM((nd - 1, 2, half, width), BF),
            pltpu.SemaphoreType.DMA((nd * 4 * count,)),
            pltpu.SemaphoreType.DMA((sends,)),
            pltpu.SemaphoreType.DMA((sends,)),
            pltpu.SemaphoreType.DMA,
            pltpu.SemaphoreType.DMA((nd - 1,)),
            pltpu.SemaphoreType.DMA((nd - 1,)),
        ],
        compiler_params=pltpu.CompilerParams(
            collective_id=collective_id, has_side_effects=True, vmem_limit_bytes=48 << 20
        ),
        cost_estimate=COST,
        name="reduce_rows",
    )(*[part.reshape(nd, 2, 2, 2, 2, half, part.shape[1]) for part in parts], moved)
    return (out[0].reshape(rows, width), out[1])


def sum_kernel(across_dp, part_ref, gain_ref, out_ref, total_ref, *scratch):
    own, from_core, from_chip, across, result, gains, load_sem, send_sem, recv_sem, gain_sems = scratch
    nd = part_ref.shape[0]
    z, y, k, x = place()
    y_partner, core = (device(z, 1 - y, k, x), device(z, y, 1 - k, x))
    x_partner = device(z, y, k, 1 - x)
    greet([device((z + hop) % nd, y, k, x) for hop in range(1, nd)] + [x_partner, y_partner, core])
    gain_sends = []

    def gain_copy(slot, target):
        copy = pltpu.make_async_remote_copy(
            src_ref=gains.at[0, slot],
            dst_ref=gains.at[1, slot],
            send_sem=gain_sems.at[0, slot],
            recv_sem=gain_sems.at[1, slot],
            device_id=target,
            device_id_type=MESH,
        )
        copy.start()
        gain_sends.append(copy)

    gains[0, 0] = gain_ref[...]
    gain_copy(0, core)
    order = ([2, 1, 3] if nd == 4 else list(range(1, nd))) + [0]
    sends, loads = ([], [])
    core_slot, chip_slot, across_slot, result_slot = (0, nd * 2, nd * 3, nd * 4)

    def send(source, there, target, slot):
        copy = pltpu.make_async_remote_copy(
            src_ref=source,
            dst_ref=there,
            send_sem=send_sem.at[len(sends)],
            recv_sem=recv_sem.at[slot],
            device_id=target,
            device_id_type=MESH,
        )
        copy.start()
        sends.append(copy)

    def arrived(there, slot):
        pltpu.make_async_remote_copy(
            src_ref=there,
            dst_ref=there,
            send_sem=send_sem.at[0],
            recv_sem=recv_sem.at[slot],
            device_id=core,
            device_id_type=MESH,
        ).wait_recv()

    def add(to, what, index):
        def body(i, carry):
            rows = pl.ds(i * 16, 16)
            total = own[to, rows, :].astype(F32) + what[index, rows, :].astype(F32)
            own[to, rows, :] = total.astype(BF)
            return carry

        lax.fori_loop(0, own.shape[1] // 16, body, 0)

    for step, dz in enumerate(order):
        for dy in (1, 0):
            at = step * 2 + dy
            block = part_ref.at[(z + dz) % nd, (y + dy) % 2]
            send(block.at[1 - k], from_core.at[at], core, core_slot + at)
            load = pltpu.make_async_copy(block.at[k], own.at[at], load_sem.at[at])
            load.start()
            loads.append(load)
    stages = [y_partner, x_partner]
    if nd > 1:
        stages += [device(z + 1 - z % 2 * 2, y, k, x), device((z + 2) % nd, y, k, x)]
    for slot, target in enumerate(stages + [None], 1):
        gain_sends[-1].wait_recv()
        gains[0, slot] = gains[0, slot - 1] + gains[1, slot - 1]
        if target is not None:
            gain_copy(slot, target)
    total_ref[...] = gains[0, len(stages) + 1]
    for step in range(nd + 1):
        if step < nd:
            for dy in (1, 0):
                at = step * 2 + dy
                loads[step * 2 + 1 - dy].wait()
                arrived(from_core.at[at], core_slot + at)
                add(at, from_core, at)
                if dy:
                    send(own.at[at], from_chip.at[step], y_partner, chip_slot + step)
        if step:
            now = step - 1
            arrived(from_chip.at[now], chip_slot + now)
            hop = order[now]
            if hop or across_dp:
                add(now * 2, from_chip, now)
            if hop:
                slot = nd - hop - 1
                target = device((z + hop) % nd, y, k, x)
                send(own.at[now * 2], across.at[slot], target, across_slot + slot)
    for slot in range(nd - 1):
        arrived(across.at[slot], across_slot + slot)
    mine = (nd - 1) * 2

    def total(i, carry):
        rows = pl.ds(i * 16, 16)
        value = own[mine, rows, :].astype(F32)
        if across_dp:
            for slot in range(nd - 1):
                value = value + across[slot, rows, :].astype(F32)
            result[y, k, rows, :] = value.astype(BF)
        else:
            out_ref[rows, :] = value + from_chip[0, rows, :].astype(F32)
        return carry

    lax.fori_loop(0, own.shape[1] // 16, total, 0)
    if across_dp:
        send(result.at[y, k], result.at[y, k], y_partner, result_slot)
        send(result.at[y, k], result.at[y, k], core, result_slot + 1)
        arrived(result.at[1 - y, k], result_slot)
        send(result.at[1 - y, k], result.at[1 - y, k], core, result_slot + 2)
        arrived(result.at[y, 1 - k], result_slot + 1)
        arrived(result.at[1 - y, 1 - k], result_slot + 2)

        def widen(i, carry):
            rows = pl.ds(i * 16, 16)
            for chip in range(2):
                for side in range(2):
                    out_ref[chip, side, rows, :] = result[chip, side, rows, :].astype(F32)
            return carry

        lax.fori_loop(0, own.shape[1] // 16, widen, 0)
    for copy in gain_sends:
        copy.wait_send()
    for copy in sends:
        copy.wait_send()


def sum_blocks(part, gain, nd, collective_id):
    rows, width = (part.shape[0] // (nd * 4), part.shape[1])
    shape = (2, 2, rows, width) if nd > 1 else (rows, width)
    out = pl.pallas_call(
        functools.partial(sum_kernel, nd > 1),
        in_specs=[pl.BlockSpec(memory_space=pl.ANY), pl.BlockSpec(memory_space=pltpu.VMEM)],
        out_specs=[pl.BlockSpec(memory_space=pltpu.VMEM)] * 2,
        out_shape=[jax.ShapeDtypeStruct(shape, F32), jax.ShapeDtypeStruct(gain.shape, F32)],
        scratch_shapes=[
            pltpu.VMEM((nd * 2, rows, width), BF),
            pltpu.VMEM((nd * 2, rows, width), BF),
            pltpu.VMEM((nd, rows, width), BF),
            pltpu.VMEM((max(nd - 1, 1), rows, width), BF),
            pltpu.VMEM((2, 2, rows, width) if nd > 1 else (1, 1, 16, LANES), BF),
            pltpu.VMEM((2, 6, *gain.shape), F32),
            pltpu.SemaphoreType.DMA((nd * 2,)),
            pltpu.SemaphoreType.DMA((nd * 4 + 3,)),
            pltpu.SemaphoreType.DMA((nd * 4 + 3,)),
            pltpu.SemaphoreType.DMA((2, 5)),
        ],
        compiler_params=pltpu.CompilerParams(
            collective_id=collective_id, has_side_effects=True, vmem_limit_bytes=48 << 20
        ),
        cost_estimate=COST,
        name="sum_blocks",
    )(part.reshape(nd, 2, 2, rows, width), gain)
    return (out[0].reshape(-1, width), out[1])


def spread_kernel(up_ref, low_ref, in_ref, out_ref):
    nc, nd = up_ref.shape[:2]
    own_count = in_ref.shape[0] // nc
    units = low_ref.shape[3] // own_count
    for c in range(nc):
        for e in range(own_count):
            for part in range(3):
                got_ref, to_ref, base = ((up_ref, in_ref, part) if part < 2 else (low_ref, out_ref, 0))
                start = (base * own_count + e) * units
                for at in range(nd):
                    columns = slice((base * nd + at) * units, (base * nd + at + 1) * units)
                    to_ref[c * own_count + e, :, columns] = got_ref[
                        c, at, :, start : start + units
                    ].astype(F32)


def spread(up, low, own_count):
    nc, nd, d_local, low_width = low.shape
    experts, units = (nc * own_count, low_width // own_count)
    block = 32
    into, out = pl.pallas_call(
        spread_kernel,
        grid=(d_local // block,),
        in_specs=[
            pl.BlockSpec((nc, nd, block, ref.shape[3]), lambda i: (0, 0, i, 0)) for ref in (up, low)
        ],
        out_specs=[
            pl.BlockSpec((experts, block, parts * nd * units), lambda i: (0, i, 0))
            for parts in (2, 1)
        ],
        out_shape=[
            jax.ShapeDtypeStruct((experts, d_local, parts * nd * units), F32) for parts in (2, 1)
        ],
        name="spread",
    )(up, low)
    return (jnp.transpose(into, (1, 0, 2)), jnp.transpose(out, (1, 0, 2)))


def rope_tables(position):
    halves = HEAD_DIM // 2
    frequency = THETA ** (-2.0 * jnp.arange(halves, dtype=F32) / HEAD_DIM)
    angles = position[:, None] * frequency[None, :]
    return (jnp.cos(angles)[:, None, :], jnp.sin(angles)[:, None, :])


def rotate(values, cosine_table, sine_table):
    halves = values.shape[-1] // 2
    first_half, second_half = (values[..., :halves], values[..., halves:])
    return jnp.concatenate(
        [
            first_half * cosine_table - second_half * sine_table,
            second_half * cosine_table + first_half * sine_table,
        ],
        axis=-1,
    )


def dot(a, b, dims):
    return lax.dot_general(a, b, (dims, ((), ())), preferred_element_type=F32)


def norm_forward(rows, gain):
    inverse = lax.rsqrt(jnp.mean(rows * rows, axis=1, keepdims=True) + EPS)
    return (inverse, (rows * inverse * gain[None, :]).astype(BF))


def norm_backward(rows, gain, inverse, grad_normed):
    weighted = grad_normed * gain[None, :]
    inner = jnp.sum(weighted * rows, axis=1, keepdims=True)
    grad_rows = weighted * inverse - rows * (inverse * inverse * inverse * inner / D)
    return (grad_rows, jnp.sum(grad_normed * rows * inverse, axis=0))


def exchange(parts, at, count):
    result = lax.dynamic_update_index_in_dim(
        jnp.zeros_like(parts), lax.dynamic_index_in_dim(parts, at, 0), at, 0
    )
    for hop in range(1, count):
        sent = lax.dynamic_index_in_dim(parts, (at + hop) % count, 0)
        got = lax.ppermute(sent, "dp", [(i, (i + hop) % count) for i in range(count)])
        result = lax.dynamic_update_index_in_dim(result, got, (at - hop) % count, 0)
    return result


def scatter_rows(partial, at, count):
    if count != 2:
        return lax.psum_scatter(
            partial.astype(BF), "tensor", scatter_dimension=0, tiled=True
        ).astype(F32)
    half = partial.shape[0] // 2
    sent = lax.dynamic_slice_in_dim(partial, (1 - at) * half, half, 0).astype(BF)
    got = lax.ppermute(sent, "tensor", [(0, 1), (1, 0)])
    return lax.dynamic_slice_in_dim(partial, at * half, half, 0) + got.astype(F32)


def on_device(
    tokens,
    segments,
    order,
    routes,
    gain_one,
    w_query,
    w_key,
    w_value,
    w_output,
    gain_two,
    w_router,
    w_expert_in,
    w_expert_out,
    cotangent,
):
    nd, nc, nt = (lax.axis_size("dp"), lax.axis_size("ctx"), lax.axis_size("tensor"))
    dp_at, ctx_at, tensor_at = (
        lax.axis_index("dp"),
        lax.axis_index("ctx"),
        lax.axis_index("tensor"),
    )
    n_rows, part_width = tokens.shape
    sub = n_rows // nt
    pack_len = order.shape[1]
    d_local = w_query.shape[0]
    q_width, kv_width = (w_query.shape[1], w_key.shape[1])
    q_heads, kv_heads = (q_width // HEAD_DIM, kv_width // HEAD_DIM)
    group = q_heads // kv_heads
    qkv_width = q_width + 2 * kv_width
    local_count = w_expert_in.shape[1]
    capacity = n_rows * 3 // 8

    gains = lax.all_gather(jnp.stack([gain_one, gain_two]), "tensor", axis=1, tiled=True)
    gain_one_full, gain_two_full = (gains[0], gains[1])
    tokens_full = lax.all_gather(tokens, "tensor", axis=1, tiled=True)
    packed = jnp.concatenate([w_query, w_key, w_value, w_router], axis=1)
    share = d_local // nc
    packed = lax.dynamic_slice_in_dim(packed, ctx_at * share, share, 0)
    packed = lax.all_gather(packed, ("dp", "ctx"), axis=0, tiled=True)
    qkv_w, router_w = (packed[:, :qkv_width], packed[:, qkv_width:])
    output_w = lax.all_gather(
        lax.dynamic_slice_in_dim(w_output, ctx_at * share, share, 0),
        ("dp", "ctx"),
        axis=0,
        tiled=True,
    )
    kernels = (nd, nc, nt) == (4, 4, 2)
    by_expert = local_count % nc == 0
    own_count = local_count // nc if by_expert else local_count
    units = FF // nd if by_expert else FF // (nd * nc)
    width = own_count * units
    if kernels:
        natural = [jnp.transpose(w, (1, 0, 2)) for w in (w_expert_in, w_expert_out)]
        cot_all, upper_w, lower_w = gather_rows(
            cotangent, nd, 1, wide=True, weights=natural, own_count=own_count
        )
        cot_sub = lax.dynamic_slice_in_dim(
            cot_all, (dp_at * nc + ctx_at) * n_rows + tensor_at * sub, sub, 0
        )
    else:
        cot_sub = lax.all_to_all(cotangent, "tensor", 0, 1, tiled=True)
        cot_all = lax.all_gather(cot_sub, ALL, axis=0, tiled=True)
    tokens_sub = lax.dynamic_slice_in_dim(tokens_full, tensor_at * sub, sub, 0).astype(F32)

    first_expert = tensor_at * local_count + (ctx_at * own_count if by_expert else 0)
    if not kernels:
        if by_expert:
            own_in = lax.dynamic_slice_in_dim(w_expert_in, ctx_at * own_count, own_count, 1)
            own_out = lax.dynamic_slice_in_dim(w_expert_out, ctx_at * own_count, own_count, 1)
            own_in = own_in.reshape(d_local, own_count, 2, nd, units)
            own_out = own_out.reshape(d_local, own_count, nd, units)
        else:
            own_in = w_expert_in.reshape(d_local, own_count, 2, nd, nc, units)
            own_out = w_expert_out.reshape(d_local, own_count, nd, nc, units)
            own_in = lax.dynamic_index_in_dim(own_in, ctx_at, 4, False)
            own_out = lax.dynamic_index_in_dim(own_out, ctx_at, 3, False)
        own_in = jnp.transpose(own_in, (3, 0, 2, 1, 4)).reshape(nd, d_local, 2 * width)
        own_out = jnp.transpose(own_out, (2, 0, 1, 3)).reshape(nd, d_local, width)
        expert_w = exchange(jnp.concatenate([own_in, own_out], axis=2), dp_at, nd)
        expert_w = expert_w.reshape(D, 3 * width)
        upper_w, lower_w = (expert_w[:, : 2 * width], expert_w[:, 2 * width :])

    order_row = order[0]
    places = jnp.arange(pack_len, dtype=jnp.int32)
    dealt = jnp.sum(jnp.where(order_row[:, None] == places[None, :], places[:, None], 0), axis=0)
    sub_start = ctx_at * n_rows + tensor_at * sub
    dealt_sub = lax.dynamic_slice_in_dim(dealt, sub_start, sub)
    experts_all = jnp.arange(EXPERTS, dtype=jnp.int32)
    uses = jnp.any(routes[:, :, None] == experts_all[None, None, :], axis=1)
    earlier = (dealt_sub[:, None] // n_rows == dealt[None, :] // n_rows) & (
        dealt[None, :] < dealt_sub[:, None]
    )
    ranks = dot(earlier.astype(BF), uses.astype(BF), ((1,), (0,)))
    uses_sub = lax.dynamic_slice_in_dim(uses, sub_start, sub, 0)
    kept = (uses_sub & (ranks < capacity)).astype(F32)

    segment_row = segments[0]
    local_segs = lax.dynamic_slice_in_dim(segment_row, ctx_at * n_rows, n_rows)
    local_places = ctx_at * n_rows + jnp.arange(n_rows, dtype=jnp.int32)
    starts = jnp.sum((segment_row[None, :] < local_segs[:, None]).astype(jnp.int32), axis=1)
    cosine_table, sine_table = rope_tables((local_places - starts).astype(F32))
    _, h_one = norm_forward(tokens_full.astype(F32), gain_one_full)
    if kernels:
        h_one, cot_all, cot_sub = lax.optimization_barrier((h_one, cot_all, cot_sub))
    projected = dot(h_one, qkv_w, ((1,), (0,)))
    turned = rotate(
        projected[:, : q_width + kv_width].reshape(n_rows, q_heads + kv_heads, HEAD_DIM),
        cosine_table,
        sine_table,
    ).astype(BF)
    queries = turned[:, :q_heads].reshape(n_rows, kv_heads, group, HEAD_DIM)
    kv_rows = jnp.concatenate(
        [
            turned[:, q_heads:].reshape(n_rows, kv_width),
            projected[:, q_width + kv_width :].astype(BF),
        ],
        axis=1,
    )
    kv_all = lax.all_gather(kv_rows, "ctx", axis=0, tiled=True)
    key_heads = kv_all[:, :kv_width].reshape(pack_len, kv_heads, HEAD_DIM)
    value_heads = kv_all[:, kv_width:].reshape(pack_len, kv_heads, HEAD_DIM)
    allowed = (local_segs[:, None] == segment_row[None, :]) & (
        local_places[:, None] >= places[None, :]
    )
    score_scale = HEAD_DIM ** (-0.5)
    scores = score_scale * jnp.einsum(
        "bagd,pad->agbp", queries, key_heads, preferred_element_type=F32
    )
    scores = jnp.where(allowed[None, None], scores, NEG)
    highest = jnp.max(scores, axis=-1, keepdims=True)
    weights = jnp.exp(scores - highest)
    totals = jnp.sum(weights, axis=-1, keepdims=True)
    shares_low = (weights / totals).astype(BF)
    log_totals = highest + jnp.log(totals)
    attended = (
        jnp.einsum("agbp,pad->bagd", shares_low, value_heads, preferred_element_type=F32)
        .astype(BF)
        .reshape(n_rows, q_width)
    )
    middle = tokens_sub + scatter_rows(dot(attended, output_w, ((1,), (1,))), tensor_at, nt)

    inverse_two, h_two = norm_forward(middle, gain_two_full)
    logits = jnp.where(uses_sub, dot(h_two, router_w, ((1,), (0,))), NEG)
    raised = jnp.exp(logits - jnp.max(logits, axis=1, keepdims=True))
    gates = raised / jnp.sum(raised, axis=1, keepdims=True)
    gates_kept = gates * kept
    gates_high = gates_kept.astype(BF)
    gates_low = (gates_kept - gates_high.astype(F32)).astype(BF)
    extra = jnp.zeros((sub, LANES - 2 * EXPERTS), BF)
    h_ext = jnp.concatenate([h_two, gates_high, gates_low, extra], axis=1)
    if kernels:
        h_all = gather_rows(h_ext, nd, 2)
    else:
        h_all = lax.all_gather(h_ext, ALL, axis=0, tiled=True)
    gates_all = (
        h_all[:, D : D + EXPERTS].astype(F32) + h_all[:, D + EXPERTS : D + 2 * EXPERTS].astype(F32)
    )
    total_rows = h_all.shape[0]
    gates_own = lax.dynamic_slice_in_dim(gates_all, first_expert, own_count, 1)
    h_all = h_all[:, :D]

    gate_wide = jnp.broadcast_to(gates_own[:, :, None], (total_rows, own_count, units)).reshape(
        total_rows, width
    )
    hidden = dot(h_all, upper_w, ((1,), (0,)))
    grad_raw = dot(cot_all, lower_w, ((1,), (0,)))
    gate_part, up_part = (hidden[:, :width], hidden[:, width:])
    sigmoid = jax.nn.sigmoid(gate_part)
    silu = gate_part * sigmoid
    active = (silu * up_part).astype(BF).astype(F32)
    active_gated = (active * gate_wide).astype(BF)
    grad_gates = jnp.sum((grad_raw * active).reshape(total_rows, own_count, units), axis=2)
    grad_active = grad_raw * gate_wide
    grad_hidden = jnp.concatenate(
        [
            grad_active * up_part * sigmoid * (1.0 + gate_part * (1.0 - sigmoid)),
            grad_active * silu,
        ],
        axis=1,
    ).astype(BF)
    grad_in = dot(grad_hidden, upper_w, ((1,), (1,))).astype(BF)
    grad_gates = lax.dynamic_update_slice_in_dim(
        jnp.zeros((total_rows, LANES), BF), grad_gates.astype(BF), first_expert, 1
    )
    mixed = dot(active_gated, lower_w, ((1,), (1,))).astype(BF)
    grad_upper = dot(h_all, grad_hidden, ((0,), (0,))).astype(BF)
    grad_lower = dot(cot_all, active_gated, ((0,), (0,))).astype(BF)
    if kernels:
        grad_in, grad_upper, grad_lower = lax.optimization_barrier((grad_in, grad_upper, grad_lower))
        back_sub, grad_upper = reduce_rows([grad_in, grad_gates], grad_upper, nd, 3)
        mixed, back_sub = lax.optimization_barrier((mixed, back_sub))
        mixed_sub, grad_lower = reduce_rows([mixed], grad_lower, nd, 4)
        back_sub, mixed_sub = lax.optimization_barrier((back_sub, mixed_sub))
        grad_upper = lax.all_gather(grad_upper, "ctx", axis=0)
        grad_lower = lax.all_gather(grad_lower, "ctx", axis=0)
        grad_expert_in, grad_expert_out = spread(grad_upper, grad_lower, own_count)
    else:
        back = jnp.concatenate([grad_in, grad_gates], axis=1)
        back_sub = lax.psum_scatter(back, ALL, scatter_dimension=0, tiled=True).astype(F32)
        mixed_sub = lax.psum_scatter(mixed, ALL, scatter_dimension=0, tiled=True).astype(F32)
        grad_expert = jnp.concatenate([grad_upper, grad_lower], axis=1)
        grad_expert = exchange(grad_expert.reshape(nd, d_local, 3 * width), dp_at, nd)
        grad_expert = lax.all_gather(grad_expert, "ctx", axis=0)
        split = (1, nc) if by_expert else (nc, 1)
        grad_up = grad_expert[..., : 2 * width].reshape(*split, nd, d_local, 2, own_count, units)
        grad_low = grad_expert[..., 2 * width :].reshape(*split, nd, d_local, own_count, units)
        grad_up = jnp.transpose(grad_up, (3, 1, 5, 4, 2, 0, 6))
        grad_low = jnp.transpose(grad_low, (3, 1, 4, 2, 0, 5))
        grad_expert_in = grad_up.reshape(d_local, local_count, 2 * FF).astype(F32)
        grad_expert_out = grad_low.reshape(d_local, local_count, FF).astype(F32)

    result = lax.all_to_all((middle + mixed_sub).astype(BF), "tensor", 1, 0, tiled=True)

    gate_grads = back_sub[:, D : D + EXPERTS] * kept
    logit_grads = (
        gates * (gate_grads - jnp.sum(gates * gate_grads, axis=1, keepdims=True))
    ).astype(BF)
    grad_norm_two = back_sub[:, :D] + dot(logit_grads, router_w, ((1,), (1,)))
    grad_middle, grad_gain_two = norm_backward(middle, gain_two_full, inverse_two, grad_norm_two)
    grad_middle = grad_middle + cot_sub.astype(F32)
    extra = jnp.zeros((sub, LANES - EXPERTS), BF)
    grad_attn = lax.all_gather(
        jnp.concatenate([grad_middle.astype(BF), logit_grads, extra], axis=1),
        "tensor",
        axis=0,
        tiled=True,
    )
    logit_grads_full = grad_attn[:, D : D + EXPERTS]
    grad_attn = grad_attn[:, :D]
    h_two_full = lax.dynamic_slice_in_dim(h_all, (dp_at * nc + ctx_at) * n_rows, n_rows, 0)
    grad_router = dot(h_two_full, logit_grads_full, ((0,), (0,)))

    grad_output_w = dot(grad_attn, attended, ((0,), (0,)))
    grad_blended = (
        dot(grad_attn, output_w, ((1,), (0,)))
        .astype(BF)
        .reshape(n_rows, kv_heads, group, HEAD_DIM)
    )
    shares = jnp.exp(scores - log_totals)
    grad_shares = jnp.einsum(
        "bagd,pad->agbp", grad_blended, value_heads, preferred_element_type=F32
    )
    inner = jnp.sum(shares * grad_shares, axis=-1, keepdims=True)
    grad_scores = (shares * (grad_shares - inner)).astype(BF)
    grad_queries = score_scale * jnp.einsum(
        "agbp,pad->bagd", grad_scores, key_heads, preferred_element_type=F32
    )
    grad_keys = score_scale * jnp.einsum(
        "agbp,bagd->pad", grad_scores, queries, preferred_element_type=F32
    )
    grad_values = jnp.einsum(
        "agbp,bagd->pad", shares_low, grad_blended, preferred_element_type=F32
    )
    grad_kv = jnp.concatenate(
        [grad_keys.reshape(pack_len, kv_width), grad_values.reshape(pack_len, kv_width)], axis=1
    ).astype(BF)
    if kernels:
        grad_kv, _ = sum_blocks(grad_kv, jnp.zeros((8, LANES), F32), 1, 5)
    else:
        grad_kv = lax.psum_scatter(grad_kv, "ctx", scatter_dimension=0, tiled=True).astype(F32)
    grad_turned = jnp.concatenate(
        [
            grad_queries.reshape(n_rows, q_heads, HEAD_DIM),
            grad_kv[:, :kv_width].reshape(n_rows, kv_heads, HEAD_DIM),
        ],
        axis=1,
    )
    grad_qkv = jnp.concatenate(
        [
            rotate(grad_turned, cosine_table, -sine_table)
            .astype(BF)
            .reshape(n_rows, q_width + kv_width),
            grad_kv[:, kv_width:].astype(BF),
        ],
        axis=1,
    )
    grad_norm_one = scatter_rows(dot(grad_qkv, qkv_w, ((1,), (1,))), tensor_at, nt)
    inverse_sub = lax.rsqrt(jnp.mean(tokens_sub * tokens_sub, axis=1, keepdims=True) + EPS)
    grad_tokens, grad_gain_one = norm_backward(
        tokens_sub, gain_one_full, inverse_sub, grad_norm_one
    )
    grad_tokens = lax.all_to_all(grad_tokens + grad_middle, "tensor", 1, 0, tiled=True)

    grad_qkv_w = dot(h_one, grad_qkv, ((0,), (0,)))
    gain_grads = jnp.stack([grad_gain_one, grad_gain_two])
    extra = jnp.zeros((D, LANES - EXPERTS), F32)
    weight_grads = jnp.concatenate([grad_qkv_w, grad_output_w, grad_router, extra], axis=1).astype(BF)
    if kernels:
        weight_grads, gain_grads = sum_blocks(weight_grads, gain_grads, nd, 6)
    else:
        weight_grads = lax.psum_scatter(
            weight_grads, ("dp", "ctx"), scatter_dimension=0, tiled=True
        )
        weight_grads = lax.all_gather(weight_grads, "ctx", axis=0, tiled=True).astype(F32)
        gain_grads = jnp.sum(lax.all_gather(gain_grads, ALL, axis=0), axis=0)
    edges = [0, q_width, q_width + kv_width, qkv_width, qkv_width + q_width]
    gain_grads = lax.dynamic_slice_in_dim(gain_grads, tensor_at * part_width, part_width, 1)
    return (
        result,
        grad_tokens,
        gain_grads[0],
        weight_grads[:, edges[0] : edges[1]],
        weight_grads[:, edges[1] : edges[2]],
        weight_grads[:, edges[2] : edges[3]],
        weight_grads[:, edges[3] : edges[4]],
        gain_grads[1],
        weight_grads[:, edges[4] : edges[4] + EXPERTS],
        grad_expert_in,
        grad_expert_out,
    )


def solution(mesh):
    return jax.shard_map(
        on_device,
        mesh=mesh,
        in_specs=(
            P(("dp", "ctx"), "tensor"),
            P("dp", None),
            P("dp", None),
            P("dp", None),
            P("tensor"),
            P("dp", "tensor"),
            P("dp", "tensor"),
            P("dp", "tensor"),
            P("dp", "tensor"),
            P("tensor"),
            P("dp", None),
            P("dp", "tensor", None),
            P("dp", "tensor", None),
            P(("dp", "ctx"), "tensor"),
        ),
        out_specs=(
            P(("dp", "ctx"), "tensor"),
            P(("dp", "ctx"), "tensor"),
            P("tensor"),
            P("dp", "tensor"),
            P("dp", "tensor"),
            P("dp", "tensor"),
            P("dp", "tensor"),
            P("tensor"),
            P("dp", None),
            P("dp", "tensor", None),
            P("dp", "tensor", None),
        ),
        check_vma=False,
    )
```

```python
import functools

import jax
import jax.numpy as jnp
from jax import lax
from jax.experimental import pallas as pl
from jax.experimental.pallas import tpu as pltpu
from jax.sharding import PartitionSpec as P

D = 1536
HEAD_DIM = 64
EXPERTS = 40
TOP_K = 8
FF = 512
EPS = 1e-06
THETA = 10000.0
NEG = -1e30
LANES = 128
ALL = ("dp", "ctx", "tensor")
BF = jnp.bfloat16
F32 = jnp.float32
MESH = pl.DeviceIdType.MESH
COST = pl.CostEstimate(flops=0, bytes_accessed=250_000_000, transcendentals=0)


def place():
    ctx = lax.axis_index("ctx")
    return (lax.axis_index("dp"), ctx // 2, ctx % 2, lax.axis_index("tensor"))


def device(z, y, k, x):
    return {"dp": z, "ctx": y * 2 + k, "tensor": x}


def greet(partners):
    barrier = pltpu.get_barrier_semaphore()
    for partner in partners:
        pl.semaphore_signal(barrier, inc=1, device_id=partner, device_id_type=MESH)
    pl.semaphore_wait(barrier, len(partners))


def partners_of(nd, z, y, k, x):
    return [device((z + hop) % nd, y, k, x) for hop in range(1, nd)] + [
        device(z, y, k, 1 - x),
        device(z, 1 - y, k, x),
        device(z, y, 1 - k, x),
    ]


def gather_kernel(own_count, units, pairs, *refs):
    own_ref, weight_ref, pair_refs = (refs[0], refs[1], refs[2 : 2 + pairs])
    out_ref, moved_ref, paired_refs = (refs[2 + pairs], refs[3 + pairs], refs[4 + pairs : 4 + 2 * pairs])
    local_sem, send_sem, recv_sem, move_local_sem, move_send_sem, move_recv_sem, pair_sem, held = refs[
        4 + 2 * pairs :
    ]
    nd, width = (out_ref.shape[0], own_ref.shape[2])
    wide = out_ref.shape[-1] != width
    z, y, k, x = place()
    up, down = (device((z + 1) % nd, y, k, x), device((z + nd - 1) % nd, y, k, x))
    greet(partners_of(nd, z, y, k, x))
    moves, kept = ([], [])
    rows, parts = (weight_ref.shape[1], weight_ref.shape[2] // (nd * units))

    def move(hop):
        to_z, from_z = ((z + hop) % nd, (z + nd - hop) % nd)
        for part in range(parts):
            for e in range(own_count):
                columns = pl.ds((part * own_count + e) * units, units)
                start = pl.multiple_of((part * nd + to_z) * units, LANES)
                source = weight_ref.at[(y * 2 + k) * own_count + e, :, pl.ds(start, units)]
                target = moved_ref.at[pl.ds(pl.multiple_of(z * rows, 16), rows), columns]
                if hop == 0:
                    at = len(kept)
                    copy = pltpu.make_async_copy(source, held.at[at], move_local_sem.at[0, at])
                    copy.start()
                    put = pltpu.make_async_copy(held.at[at], target, move_local_sem.at[1, at])
                    kept.append((copy, put))
                    continue
                slot = len(moves)
                copy = pltpu.make_async_remote_copy(
                    src_ref=source,
                    dst_ref=target,
                    send_sem=move_send_sem.at[slot],
                    recv_sem=move_recv_sem.at[slot],
                    device_id=device(to_z, y, k, x),
                    device_id_type=MESH,
                )
                copy.start()
                arrival = moved_ref.at[pl.ds(pl.multiple_of(from_z * rows, 16), rows), columns]
                moves.append((copy, arrival, slot))

    swaps = []
    for at_pair, (ref, full_ref) in enumerate(zip(pair_refs, paired_refs)):
        span = ref.shape[-1]
        mine = full_ref.at[:, pl.ds(pl.multiple_of(x * span, LANES), span)]
        copy = pltpu.make_async_remote_copy(
            src_ref=ref,
            dst_ref=mine,
            send_sem=pair_sem.at[0, at_pair],
            recv_sem=pair_sem.at[1, at_pair],
            device_id=device(z, y, k, 1 - x),
            device_id_type=MESH,
        )
        copy.start()
        swaps.append(copy)
        copy = pltpu.make_async_copy(ref, mine, pair_sem.at[2, at_pair])
        copy.start()
        swaps.append(copy)
    low = jnp.minimum(z, nd - 1 - z)
    places = []
    for step in range(nd):
        near = (step + 1) // 2
        zigzag = low + near if step % 2 else low - near
        from_low = jnp.where(step <= 2 * low, zigzag, step)
        places.append(jnp.where(2 * z < nd, from_low, nd - 1 - from_low))
    sends = []

    def at(piece):
        step, dy, dk, dx, half = piece
        chip, core, side = ((y + dy) % 2, (k + dk) % 2, (x + dx) % 2)
        if not wide:
            return out_ref.at[places[step], chip, core, side, half]
        columns = pl.ds(pl.multiple_of(side * width, LANES), width)
        return out_ref.at[places[step], chip, core, half, :, columns]

    def slot(piece):
        step, dy, dk, dx, half = piece
        return (((places[step] * 2 + dy) * 2 + dk) * 2 + dx) * 2 + half

    def send(piece, link, condition=None):
        step, dy, dk, dx, half = piece
        if link == "up":
            target, there = (up, piece)
        elif link == "down":
            target, there = (down, piece)
        elif link == "x":
            target, there = (device(z, y, k, 1 - x), (step, dy, dk, 1 - dx, half))
        elif link == "y":
            target, there = (device(z, 1 - y, k, x), (step, 1 - dy, dk, dx, half))
        else:
            target, there = (device(z, y, 1 - k, x), (step, dy, 1 - dk, dx, half))
        own = piece[:4] == (0, 0, 0, 0)
        copy = pltpu.make_async_remote_copy(
            src_ref=own_ref.at[half] if own else at(piece),
            dst_ref=at(piece),
            send_sem=send_sem.at[len(sends)],
            recv_sem=recv_sem.at[slot(there)],
            device_id=target,
            device_id_type=MESH,
        )
        if condition is None:
            copy.start()
        else:
            pl.when(condition)(copy.start)
        sends.append((copy, condition))

    def arrived(piece):
        pltpu.make_async_remote_copy(
            src_ref=at(piece),
            dst_ref=at(piece),
            send_sem=send_sem.at[0],
            recv_sem=recv_sem.at[slot(piece)],
            device_id=device(z, y, k, 1 - x),
            device_id_type=MESH,
        ).wait_recv()

    own_copies = []
    for half in range(2):
        own_copy = pltpu.make_async_copy(
            own_ref.at[half], at((0, 0, 0, 0, half)), local_sem.at[half]
        )
        own_copy.start()
        own_copies.append(own_copy)
    links = (("x", "y"), ("y", "x"))
    for step in range(nd + 2):
        if step < nd:
            came = places[step]
            for half in range(2):
                piece = (step, 0, 0, 0, half)
                if step:
                    arrived(piece)
                send(piece, "up", (came <= z) & (z < nd - 1))
                send(piece, "down", (came >= z) & (z > 0))
                send(piece, links[half][0])
            for half in range(2):
                piece = (step, 0, 0, 0, half)
                send(piece, links[half][1])
                send(piece, "k")
            if step == 0:
                move(0)
            if step == 1:
                for copy, put in kept:
                    copy.wait()
                    put.start()
            if step == nd - 2:
                for hop in [2, 1, 3] if nd == 4 else range(1, nd):
                    move(hop)
        if 1 <= step < nd + 1:
            for half in range(2):
                piece = (step - 1, half, 0, 1 - half, half)
                arrived(piece)
                send(piece, links[half][1])
                send(piece, "k")
        if 2 <= step:
            for half in range(2):
                for d in range(2):
                    piece = (step - 2, 1, 0, d, 0) if half == 0 else (step - 2, d, 0, 1, 1)
                    arrived(piece)
                    send(piece, "k")
    for step in range(nd):
        for dy in range(2):
            for dx in range(2):
                for half in range(2):
                    arrived((step, dy, 1, dx, half))
    for own_copy in own_copies + [put for _, put in kept]:
        own_copy.wait()
    for copy in swaps:
        copy.wait()
    for copy, arrival, slot in moves:
        pltpu.make_async_remote_copy(
            src_ref=arrival,
            dst_ref=arrival,
            send_sem=move_send_sem.at[slot],
            recv_sem=move_recv_sem.at[slot],
            device_id=device(z, y, k, 1 - x),
            device_id_type=MESH,
        ).wait_recv()
        copy.wait_send()
    for copy, condition in sends:
        if condition is None:
            copy.wait_send()
        else:
            pl.when(condition)(copy.wait_send)


def gather_rows(own, weight, units, own_count, nd, collective_id, pairs=(), wide=False):
    rows, width = own.shape
    half = rows // 2
    shape = (nd, 2, 2, 2, half, 2 * width) if wide else (nd, 2, 2, 2, 2, half, width)
    depth, moved = (nd * weight.shape[1], own_count * weight.shape[2] // nd)
    count = moved // units
    vmem, anywhere = (pl.BlockSpec(memory_space=pltpu.VMEM), pl.BlockSpec(memory_space=pl.ANY))
    out = pl.pallas_call(
        functools.partial(gather_kernel, own_count, units, len(pairs)),
        in_specs=[vmem, anywhere] + [vmem] * len(pairs),
        out_specs=[anywhere] * (2 + len(pairs)),
        out_shape=[
            jax.ShapeDtypeStruct(shape, own.dtype),
            jax.ShapeDtypeStruct((depth, moved), weight.dtype),
        ]
        + [jax.ShapeDtypeStruct((p.shape[0], 2 * p.shape[1]), p.dtype) for p in pairs],
        scratch_shapes=[
            pltpu.SemaphoreType.DMA((2,)),
            pltpu.SemaphoreType.DMA((nd * 18,)),
            pltpu.SemaphoreType.DMA((nd * 16,)),
            pltpu.SemaphoreType.DMA((2, count)),
            pltpu.SemaphoreType.DMA(((nd - 1) * count,)),
            pltpu.SemaphoreType.DMA(((nd - 1) * count,)),
            pltpu.SemaphoreType.DMA((3, max(len(pairs), 1))),
            pltpu.VMEM((count, weight.shape[1], units), weight.dtype),
        ],
        compiler_params=pltpu.CompilerParams(collective_id=collective_id, has_side_effects=True),
        cost_estimate=COST,
        name="gather_rows",
    )(own.reshape(2, half, width), weight, *pairs)
    return (out[0].reshape(-1, shape[-1]), *out[1:])


def ctx_kernel(own_ref, out_ref, local_sem, send_sem, recv_sem):
    z, y, k, x = place()
    y_partner, core = (device(z, 1 - y, k, x), device(z, y, 1 - k, x))
    greet([y_partner, core])
    kept = pltpu.make_async_copy(own_ref, out_ref.at[y, k], local_sem)
    kept.start()
    copies = []
    for at, (source, chip, target) in enumerate(
        ((own_ref, y, y_partner), (own_ref, y, core), (out_ref.at[1 - y, k], 1 - y, core))
    ):
        if at == 2:
            copies[0].wait_recv()
        copy = pltpu.make_async_remote_copy(
            src_ref=source,
            dst_ref=out_ref.at[chip, k],
            send_sem=send_sem.at[at],
            recv_sem=recv_sem.at[at],
            device_id=target,
            device_id_type=MESH,
        )
        copy.start()
        copies.append(copy)
    kept.wait()
    for copy in copies[1:]:
        copy.wait_recv()
    for copy in copies:
        copy.wait_send()


def gather_ctx(own, collective_id):
    out = pl.pallas_call(
        ctx_kernel,
        in_specs=[pl.BlockSpec(memory_space=pltpu.VMEM)],
        out_specs=pl.BlockSpec(memory_space=pl.ANY),
        out_shape=jax.ShapeDtypeStruct((2, 2, *own.shape), own.dtype),
        scratch_shapes=[
            pltpu.SemaphoreType.DMA,
            pltpu.SemaphoreType.DMA((3,)),
            pltpu.SemaphoreType.DMA((3,)),
        ],
        compiler_params=pltpu.CompilerParams(collective_id=collective_id, has_side_effects=True),
        name="gather_ctx",
    )(own)
    return out.reshape(-1, own.shape[1])


def reduce_kernel(count, when, *refs):
    parts, moved_ref, out_ref, arrived_ref = (refs[:count], *refs[count : count + 3])
    own, from_core, first, second, across, load_sem, send_sem, recv_sem = refs[count + 3 : -4]
    move_local_sem, move_send_sem, move_recv_sem, held = refs[-4:]
    nd = parts[0].shape[0]
    z, y, k, x = place()
    greet(partners_of(nd, z, y, k, x))
    order = [hop for hop in (2, 1, 3, 0)] if nd == 4 else list(range(1, nd)) + [0]
    sends, loads = ([], [])

    def spot(step, dy, dx, half):
        return ((step * 2 + dy) * 2 + dx) * 2 + half

    def send(source, there, target, slot):
        copy = pltpu.make_async_remote_copy(
            src_ref=source,
            dst_ref=there,
            send_sem=send_sem.at[len(sends)],
            recv_sem=recv_sem.at[slot],
            device_id=target,
            device_id_type=MESH,
        )
        copy.start()
        sends.append(copy)

    def arrived(there, slot):
        pltpu.make_async_remote_copy(
            src_ref=there,
            dst_ref=there,
            send_sem=send_sem.at[0],
            recv_sem=recv_sem.at[slot],
            device_id=device(z, y, k, 1 - x),
            device_id_type=MESH,
        ).wait_recv()

    def add(to, what, index):
        to_rows = own.shape[1]

        def body(i, carry):
            rows = pl.ds(i * 16, 16)
            total = own[to, rows, :].astype(F32) + what[index, rows, :].astype(F32)
            own[to, rows, :] = total.astype(BF)
            return carry

        lax.fori_loop(0, to_rows // 16, body, 0)

    spans, start = ([], 0)
    for ref in parts:
        spans.append(pl.ds(start, ref.shape[-1]))
        start += ref.shape[-1]
    first_slot, second_slot, across_slot, core_slot = (0, nd * 4, nd * 6, nd * 7)
    for step, dz in enumerate(order):
        for dy in range(2):
            for dx in range(2):
                there = pl.ds(spot(step, dy, dx, 0), 2)
                block = ((z + dz) % nd, (y + dy) % 2)
                for ref, span in zip(parts, spans):
                    send(
                        ref.at[block[0], block[1], 1 - k, (x + dx) % 2],
                        from_core.at[there, :, span],
                        device(z, y, 1 - k, x),
                        core_slot + len(loads),
                    )
                    load = pltpu.make_async_copy(
                        ref.at[block[0], block[1], k, (x + dx) % 2],
                        own.at[there, :, span],
                        load_sem.at[len(loads)],
                    )
                    load.start()
                    loads.append(load)
    x_partner, y_partner = (device(z, y, k, 1 - x), device(z, 1 - y, k, x))
    taken = pltpu.make_async_copy(moved_ref.at[z], held, move_local_sem.at[0])
    taken.start()
    kept = pltpu.make_async_copy(held, arrived_ref.at[z], move_local_sem.at[1])
    moves = []

    def move(hop):
        to_z = (z + hop) % nd
        copy = pltpu.make_async_remote_copy(
            src_ref=moved_ref.at[to_z],
            dst_ref=arrived_ref.at[z],
            send_sem=move_send_sem.at[hop - 1],
            recv_sem=move_recv_sem.at[hop - 1],
            device_id=device(to_z, y, k, x),
            device_id_type=MESH,
        )
        copy.start()
        moves.append((copy, hop))

    for step in range(nd + 2):
        if step == 0 and step in when:
            move(when[step])
        if step == 1:
            taken.wait()
            kept.start()
        if step < nd:
            for at in range(4):
                base = spot(step, 0, 0, 0) + at * 2
                for which, span in enumerate(spans):
                    slot = (step * 4 + at) * count + which
                    loads[slot].wait()
                    arrived(from_core.at[pl.ds(base, 2), :, span], core_slot + slot)

            def pair(i, carry, step=step):
                add(step * 8 + i, from_core, step * 8 + i)
                return carry

            lax.fori_loop(0, 8, pair, 0)
            for d in range(2):
                slot = step * 4 + d
                send(own.at[spot(step, 1, d, 0)], first.at[slot], y_partner, first_slot + slot)
                slot = step * 4 + 2 + d
                send(own.at[spot(step, d, 1, 1)], first.at[slot], x_partner, first_slot + slot)
        if 1 <= step < nd + 1:
            now = step - 1
            for d in (1, 0):
                slot = now * 4 + d
                arrived(first.at[slot], first_slot + slot)
                add(spot(now, 0, d, 0), first, slot)
                slot = now * 4 + 2 + d
                arrived(first.at[slot], first_slot + slot)
                add(spot(now, d, 0, 1), first, slot)
                if d == 1:
                    slot = now * 2
                    send(own.at[spot(now, 0, 1, 0)], second.at[slot], x_partner, second_slot + slot)
                    slot = now * 2 + 1
                    send(own.at[spot(now, 1, 0, 1)], second.at[slot], y_partner, second_slot + slot)
        if 2 <= step:
            now = step - 2
            for half in range(2):
                slot = now * 2 + half
                arrived(second.at[slot], second_slot + slot)
                add(spot(now, 0, 0, half), second, slot)
            hop = order[now]
            if hop:
                slot = nd - hop - 1
                send(
                    own.at[pl.ds(spot(now, 0, 0, 0), 2)],
                    across.at[slot],
                    device((z + hop) % nd, y, k, x),
                    across_slot + slot,
                )
        if step and step in when:
            move(when[step])
    for slot in range(nd - 1):
        arrived(across.at[slot], across_slot + slot)
    mine = spot(order.index(0), 0, 0, 0)
    for half in range(2):

        def total(i, carry, half=half):
            rows = pl.ds(i * 16, 16)
            value = own[mine + half, rows, :].astype(F32)
            for slot in range(nd - 1):
                value = value + across[slot, half, rows, :].astype(F32)
            out_ref[half, rows, :] = value
            return carry

        lax.fori_loop(0, own.shape[1] // 16, total, 0)
    kept.wait()
    for copy, hop in moves:
        there = arrived_ref.at[(z + nd - hop) % nd]
        pltpu.make_async_remote_copy(
            src_ref=there,
            dst_ref=there,
            send_sem=move_send_sem.at[hop - 1],
            recv_sem=move_recv_sem.at[hop - 1],
            device_id=x_partner,
            device_id_type=MESH,
        ).wait_recv()
        copy.wait_send()
    for copy in sends:
        copy.wait_send()


def reduce_rows(parts, moved, when, nd, collective_id):
    moved = moved.reshape(nd, moved.shape[0] // nd, moved.shape[1])
    rows = parts[0].shape[0] // (nd * 8)
    width = sum(part.shape[1] for part in parts)
    half, count = (rows // 2, len(parts))
    sends = nd * (4 * count + 7)
    out = pl.pallas_call(
        functools.partial(reduce_kernel, count, when),
        in_specs=[pl.BlockSpec(memory_space=pl.ANY)] * (count + 1),
        out_specs=[pl.BlockSpec(memory_space=pltpu.VMEM), pl.BlockSpec(memory_space=pl.ANY)],
        out_shape=[
            jax.ShapeDtypeStruct((2, half, width), F32),
            jax.ShapeDtypeStruct(moved.shape, moved.dtype),
        ],
        scratch_shapes=[
            pltpu.VMEM((nd * 8, half, width), BF),
            pltpu.VMEM((nd * 8, half, width), BF),
            pltpu.VMEM((nd * 4, half, width), BF),
            pltpu.VMEM((nd * 2, half, width), BF),
            pltpu.VMEM((nd - 1, 2, half, width), BF),
            pltpu.SemaphoreType.DMA((nd * 4 * count,)),
            pltpu.SemaphoreType.DMA((sends,)),
            pltpu.SemaphoreType.DMA((sends,)),
            pltpu.SemaphoreType.DMA((2,)),
            pltpu.SemaphoreType.DMA((nd - 1,)),
            pltpu.SemaphoreType.DMA((nd - 1,)),
            pltpu.VMEM(moved.shape[1:], moved.dtype),
        ],
        compiler_params=pltpu.CompilerParams(
            collective_id=collective_id, has_side_effects=True, vmem_limit_bytes=48 << 20
        ),
        cost_estimate=COST,
        name="reduce_rows",
    )(*[part.reshape(nd, 2, 2, 2, 2, half, part.shape[1]) for part in parts], moved)
    return (out[0].reshape(rows, width), out[1])


def sum_kernel(across_dp, part_ref, gain_ref, out_ref, total_ref, *scratch):
    own, from_core, from_chip, across, result, gains, load_sem, send_sem, recv_sem, gain_sems = scratch
    nd = part_ref.shape[0]
    z, y, k, x = place()
    y_partner, core = (device(z, 1 - y, k, x), device(z, y, 1 - k, x))
    x_partner = device(z, y, k, 1 - x)
    greet([device((z + hop) % nd, y, k, x) for hop in range(1, nd)] + [x_partner, y_partner, core])
    gain_sends = []

    def gain_copy(slot, target):
        copy = pltpu.make_async_remote_copy(
            src_ref=gains.at[0, slot],
            dst_ref=gains.at[1, slot],
            send_sem=gain_sems.at[0, slot],
            recv_sem=gain_sems.at[1, slot],
            device_id=target,
            device_id_type=MESH,
        )
        copy.start()
        gain_sends.append(copy)

    gains[0, 0] = gain_ref[...]
    gain_copy(0, core)
    order = ([2, 1, 3] if nd == 4 else list(range(1, nd))) + [0]
    sends, loads = ([], [])
    core_slot, chip_slot, across_slot, result_slot = (0, nd * 2, nd * 3, nd * 4)

    def send(source, there, target, slot):
        copy = pltpu.make_async_remote_copy(
            src_ref=source,
            dst_ref=there,
            send_sem=send_sem.at[len(sends)],
            recv_sem=recv_sem.at[slot],
            device_id=target,
            device_id_type=MESH,
        )
        copy.start()
        sends.append(copy)

    def arrived(there, slot):
        pltpu.make_async_remote_copy(
            src_ref=there,
            dst_ref=there,
            send_sem=send_sem.at[0],
            recv_sem=recv_sem.at[slot],
            device_id=core,
            device_id_type=MESH,
        ).wait_recv()

    def add(to, what, index):
        def body(i, carry):
            rows = pl.ds(i * 16, 16)
            total = own[to, rows, :].astype(F32) + what[index, rows, :].astype(F32)
            own[to, rows, :] = total.astype(BF)
            return carry

        lax.fori_loop(0, own.shape[1] // 16, body, 0)

    for step, dz in enumerate(order):
        for dy in (1, 0):
            at = step * 2 + dy
            block = part_ref.at[(z + dz) % nd, (y + dy) % 2]
            send(block.at[1 - k], from_core.at[at], core, core_slot + at)
            load = pltpu.make_async_copy(block.at[k], own.at[at], load_sem.at[at])
            load.start()
            loads.append(load)
    stages = [y_partner, x_partner]
    if nd > 1:
        stages += [device(z + 1 - z % 2 * 2, y, k, x), device((z + 2) % nd, y, k, x)]
    for slot, target in enumerate(stages + [None], 1):
        gain_sends[-1].wait_recv()
        gains[0, slot] = gains[0, slot - 1] + gains[1, slot - 1]
        if target is not None:
            gain_copy(slot, target)
    total_ref[...] = gains[0, len(stages) + 1]
    for step in range(nd + 1):
        if step < nd:
            for dy in (1, 0):
                at = step * 2 + dy
                loads[step * 2 + 1 - dy].wait()
                arrived(from_core.at[at], core_slot + at)
                add(at, from_core, at)
                if dy:
                    send(own.at[at], from_chip.at[step], y_partner, chip_slot + step)
        if step:
            now = step - 1
            arrived(from_chip.at[now], chip_slot + now)
            hop = order[now]
            if hop or across_dp:
                add(now * 2, from_chip, now)
            if hop:
                slot = nd - hop - 1
                target = device((z + hop) % nd, y, k, x)
                send(own.at[now * 2], across.at[slot], target, across_slot + slot)
    for slot in range(nd - 1):
        arrived(across.at[slot], across_slot + slot)
    mine = (nd - 1) * 2

    def total(i, carry):
        rows = pl.ds(i * 16, 16)
        value = own[mine, rows, :].astype(F32)
        if across_dp:
            for slot in range(nd - 1):
                value = value + across[slot, rows, :].astype(F32)
            result[y, k, rows, :] = value.astype(BF)
        else:
            out_ref[rows, :] = value + from_chip[0, rows, :].astype(F32)
        return carry

    lax.fori_loop(0, own.shape[1] // 16, total, 0)
    if across_dp:
        send(result.at[y, k], result.at[y, k], y_partner, result_slot)
        send(result.at[y, k], result.at[y, k], core, result_slot + 1)
        arrived(result.at[1 - y, k], result_slot)
        send(result.at[1 - y, k], result.at[1 - y, k], core, result_slot + 2)
        arrived(result.at[y, 1 - k], result_slot + 1)
        arrived(result.at[1 - y, 1 - k], result_slot + 2)

        def widen(i, carry):
            rows = pl.ds(i * 16, 16)
            for chip in range(2):
                for side in range(2):
                    out_ref[chip, side, rows, :] = result[chip, side, rows, :].astype(F32)
            return carry

        lax.fori_loop(0, own.shape[1] // 16, widen, 0)
    for copy in gain_sends:
        copy.wait_send()
    for copy in sends:
        copy.wait_send()


def sum_blocks(part, gain, nd, collective_id):
    rows, width = (part.shape[0] // (nd * 4), part.shape[1])
    shape = (2, 2, rows, width) if nd > 1 else (rows, width)
    out = pl.pallas_call(
        functools.partial(sum_kernel, nd > 1),
        in_specs=[pl.BlockSpec(memory_space=pl.ANY), pl.BlockSpec(memory_space=pltpu.VMEM)],
        out_specs=[pl.BlockSpec(memory_space=pltpu.VMEM)] * 2,
        out_shape=[jax.ShapeDtypeStruct(shape, F32), jax.ShapeDtypeStruct(gain.shape, F32)],
        scratch_shapes=[
            pltpu.VMEM((nd * 2, rows, width), BF),
            pltpu.VMEM((nd * 2, rows, width), BF),
            pltpu.VMEM((nd, rows, width), BF),
            pltpu.VMEM((max(nd - 1, 1), rows, width), BF),
            pltpu.VMEM((2, 2, rows, width) if nd > 1 else (1, 1, 16, LANES), BF),
            pltpu.VMEM((2, 6, *gain.shape), F32),
            pltpu.SemaphoreType.DMA((nd * 2,)),
            pltpu.SemaphoreType.DMA((nd * 4 + 3,)),
            pltpu.SemaphoreType.DMA((nd * 4 + 3,)),
            pltpu.SemaphoreType.DMA((2, 5)),
        ],
        compiler_params=pltpu.CompilerParams(
            collective_id=collective_id, has_side_effects=True, vmem_limit_bytes=48 << 20
        ),
        cost_estimate=COST,
        name="sum_blocks",
    )(part.reshape(nd, 2, 2, rows, width), gain)
    return (out[0].reshape(-1, width), out[1])


def spread_kernel(up_ref, low_ref, in_ref, out_ref):
    nc, nd = up_ref.shape[:2]
    own_count = in_ref.shape[0] // nc
    units = low_ref.shape[3] // own_count
    for c in range(nc):
        for e in range(own_count):
            for part in range(3):
                got_ref, to_ref, base = ((up_ref, in_ref, part) if part < 2 else (low_ref, out_ref, 0))
                start = (base * own_count + e) * units
                for at in range(nd):
                    columns = slice((base * nd + at) * units, (base * nd + at + 1) * units)
                    to_ref[c * own_count + e, :, columns] = got_ref[
                        c, at, :, start : start + units
                    ].astype(F32)


def spread(up, low, own_count):
    nc, nd, d_local, low_width = low.shape
    experts, units = (nc * own_count, low_width // own_count)
    block = 32
    into, out = pl.pallas_call(
        spread_kernel,
        grid=(d_local // block,),
        in_specs=[
            pl.BlockSpec((nc, nd, block, ref.shape[3]), lambda i: (0, 0, i, 0)) for ref in (up, low)
        ],
        out_specs=[
            pl.BlockSpec((experts, block, parts * nd * units), lambda i: (0, i, 0))
            for parts in (2, 1)
        ],
        out_shape=[
            jax.ShapeDtypeStruct((experts, d_local, parts * nd * units), F32) for parts in (2, 1)
        ],
        name="spread",
    )(up, low)
    return (jnp.transpose(into, (1, 0, 2)), jnp.transpose(out, (1, 0, 2)))


def rope_tables(position):
    halves = HEAD_DIM // 2
    frequency = THETA ** (-2.0 * jnp.arange(halves, dtype=F32) / HEAD_DIM)
    angles = position[:, None] * frequency[None, :]
    return (jnp.cos(angles)[:, None, :], jnp.sin(angles)[:, None, :])


def rotate(values, cosine_table, sine_table):
    halves = values.shape[-1] // 2
    first_half, second_half = (values[..., :halves], values[..., halves:])
    return jnp.concatenate(
        [
            first_half * cosine_table - second_half * sine_table,
            second_half * cosine_table + first_half * sine_table,
        ],
        axis=-1,
    )


def dot(a, b, dims):
    return lax.dot_general(a, b, (dims, ((), ())), preferred_element_type=F32)


def norm_forward(rows, gain):
    inverse = lax.rsqrt(jnp.mean(rows * rows, axis=1, keepdims=True) + EPS)
    return (inverse, (rows * inverse * gain[None, :]).astype(BF))


def norm_backward(rows, gain, inverse, grad_normed):
    weighted = grad_normed * gain[None, :]
    inner = jnp.sum(weighted * rows, axis=1, keepdims=True)
    grad_rows = weighted * inverse - rows * (inverse * inverse * inverse * inner / D)
    return (grad_rows, jnp.sum(grad_normed * rows * inverse, axis=0))


def exchange(parts, at, count):
    result = lax.dynamic_update_index_in_dim(
        jnp.zeros_like(parts), lax.dynamic_index_in_dim(parts, at, 0), at, 0
    )
    for hop in range(1, count):
        sent = lax.dynamic_index_in_dim(parts, (at + hop) % count, 0)
        got = lax.ppermute(sent, "dp", [(i, (i + hop) % count) for i in range(count)])
        result = lax.dynamic_update_index_in_dim(result, got, (at - hop) % count, 0)
    return result


def scatter_rows(partial, at, count):
    if count != 2:
        return lax.psum_scatter(
            partial.astype(BF), "tensor", scatter_dimension=0, tiled=True
        ).astype(F32)
    half = partial.shape[0] // 2
    sent = lax.dynamic_slice_in_dim(partial, (1 - at) * half, half, 0).astype(BF)
    got = lax.ppermute(sent, "tensor", [(0, 1), (1, 0)])
    return lax.dynamic_slice_in_dim(partial, at * half, half, 0) + got.astype(F32)


def on_device(
    tokens,
    segments,
    order,
    routes,
    gain_one,
    w_query,
    w_key,
    w_value,
    w_output,
    gain_two,
    w_router,
    w_expert_in,
    w_expert_out,
    cotangent,
):
    nd, nc, nt = (lax.axis_size("dp"), lax.axis_size("ctx"), lax.axis_size("tensor"))
    dp_at, ctx_at, tensor_at = (
        lax.axis_index("dp"),
        lax.axis_index("ctx"),
        lax.axis_index("tensor"),
    )
    n_rows, part_width = tokens.shape
    sub = n_rows // nt
    pack_len = order.shape[1]
    d_local = w_query.shape[0]
    q_width, kv_width = (w_query.shape[1], w_key.shape[1])
    q_heads, kv_heads = (q_width // HEAD_DIM, kv_width // HEAD_DIM)
    group = q_heads // kv_heads
    qkv_width = q_width + 2 * kv_width
    local_count = w_expert_in.shape[1]
    capacity = n_rows * 3 // 8

    packed = jnp.concatenate([w_query, w_key, w_value, w_router], axis=1)
    share = d_local // nc
    packed = lax.dynamic_slice_in_dim(packed, ctx_at * share, share, 0)
    packed = lax.all_gather(packed, ("dp", "ctx"), axis=0, tiled=True)
    qkv_w, router_w = (packed[:, :qkv_width], packed[:, qkv_width:])
    output_w = lax.all_gather(
        lax.dynamic_slice_in_dim(w_output, ctx_at * share, share, 0),
        ("dp", "ctx"),
        axis=0,
        tiled=True,
    )
    kernels = (nd, nc, nt) == (4, 4, 2)
    by_expert = local_count % nc == 0
    own_count = local_count // nc if by_expert else local_count
    units = FF // nd if by_expert else FF // (nd * nc)
    width = own_count * units
    gains = jnp.stack([gain_one, gain_two])
    if kernels:
        w_expert_in, w_expert_out = [jnp.transpose(w, (1, 0, 2)) for w in (w_expert_in, w_expert_out)]
        cot_all, lower_w, tokens_full, gains = gather_rows(
            cotangent, w_expert_out, units, own_count, nd, 1, (tokens, gains), wide=True
        )
        cot_sub = lax.dynamic_slice_in_dim(
            cot_all, (dp_at * nc + ctx_at) * n_rows + tensor_at * sub, sub, 0
        )
    else:
        tokens_full = lax.all_gather(tokens, "tensor", axis=1, tiled=True)
        gains = lax.all_gather(gains, "tensor", axis=1, tiled=True)
        cot_sub = lax.all_to_all(cotangent, "tensor", 0, 1, tiled=True)
        cot_all = lax.all_gather(cot_sub, ALL, axis=0, tiled=True)
    gain_one_full, gain_two_full = (gains[0], gains[1])
    tokens_sub = lax.dynamic_slice_in_dim(tokens_full, tensor_at * sub, sub, 0).astype(F32)

    first_expert = tensor_at * local_count + (ctx_at * own_count if by_expert else 0)
    if not kernels:
        if by_expert:
            own_in = lax.dynamic_slice_in_dim(w_expert_in, ctx_at * own_count, own_count, 1)
            own_out = lax.dynamic_slice_in_dim(w_expert_out, ctx_at * own_count, own_count, 1)
            own_in = own_in.reshape(d_local, own_count, 2, nd, units)
            own_out = own_out.reshape(d_local, own_count, nd, units)
        else:
            own_in = w_expert_in.reshape(d_local, own_count, 2, nd, nc, units)
            own_out = w_expert_out.reshape(d_local, own_count, nd, nc, units)
            own_in = lax.dynamic_index_in_dim(own_in, ctx_at, 4, False)
            own_out = lax.dynamic_index_in_dim(own_out, ctx_at, 3, False)
        own_in = jnp.transpose(own_in, (3, 0, 2, 1, 4)).reshape(nd, d_local, 2 * width)
        own_out = jnp.transpose(own_out, (2, 0, 1, 3)).reshape(nd, d_local, width)
        expert_w = exchange(jnp.concatenate([own_in, own_out], axis=2), dp_at, nd)
        expert_w = expert_w.reshape(D, 3 * width)
        upper_w, lower_w = (expert_w[:, : 2 * width], expert_w[:, 2 * width :])

    order_row = order[0]
    places = jnp.arange(pack_len, dtype=jnp.int32)
    dealt = jnp.sum(jnp.where(order_row[:, None] == places[None, :], places[:, None], 0), axis=0)
    sub_start = ctx_at * n_rows + tensor_at * sub
    dealt_sub = lax.dynamic_slice_in_dim(dealt, sub_start, sub)
    experts_all = jnp.arange(EXPERTS, dtype=jnp.int32)
    uses = jnp.any(routes[:, :, None] == experts_all[None, None, :], axis=1)
    earlier = (dealt_sub[:, None] // n_rows == dealt[None, :] // n_rows) & (
        dealt[None, :] < dealt_sub[:, None]
    )
    ranks = dot(earlier.astype(BF), uses.astype(BF), ((1,), (0,)))
    uses_sub = lax.dynamic_slice_in_dim(uses, sub_start, sub, 0)
    kept = (uses_sub & (ranks < capacity)).astype(F32)

    segment_row = segments[0]
    local_segs = lax.dynamic_slice_in_dim(segment_row, ctx_at * n_rows, n_rows)
    local_places = ctx_at * n_rows + jnp.arange(n_rows, dtype=jnp.int32)
    starts = jnp.sum((segment_row[None, :] < local_segs[:, None]).astype(jnp.int32), axis=1)
    cosine_table, sine_table = rope_tables((local_places - starts).astype(F32))
    _, h_one = norm_forward(tokens_full.astype(F32), gain_one_full)
    if kernels:
        h_one, cot_all, cot_sub = lax.optimization_barrier((h_one, cot_all, cot_sub))
    projected = dot(h_one, qkv_w, ((1,), (0,)))
    turned = rotate(
        projected[:, : q_width + kv_width].reshape(n_rows, q_heads + kv_heads, HEAD_DIM),
        cosine_table,
        sine_table,
    ).astype(BF)
    queries = turned[:, :q_heads].reshape(n_rows, kv_heads, group, HEAD_DIM)
    kv_rows = jnp.concatenate(
        [
            turned[:, q_heads:].reshape(n_rows, kv_width),
            projected[:, q_width + kv_width :].astype(BF),
        ],
        axis=1,
    )
    if kernels:
        kv_all = gather_ctx(kv_rows, 7)
    else:
        kv_all = lax.all_gather(kv_rows, "ctx", axis=0, tiled=True)
    key_heads = kv_all[:, :kv_width].reshape(pack_len, kv_heads, HEAD_DIM)
    value_heads = kv_all[:, kv_width:].reshape(pack_len, kv_heads, HEAD_DIM)
    allowed = (local_segs[:, None] == segment_row[None, :]) & (
        local_places[:, None] >= places[None, :]
    )
    score_scale = HEAD_DIM ** (-0.5)
    scores = score_scale * jnp.einsum(
        "bagd,pad->agbp", queries, key_heads, preferred_element_type=F32
    )
    scores = jnp.where(allowed[None, None], scores, NEG)
    highest = jnp.max(scores, axis=-1, keepdims=True)
    weights = jnp.exp(scores - highest)
    totals = jnp.sum(weights, axis=-1, keepdims=True)
    shares_low = (weights / totals).astype(BF)
    log_totals = highest + jnp.log(totals)
    attended = (
        jnp.einsum("agbp,pad->bagd", shares_low, value_heads, preferred_element_type=F32)
        .astype(BF)
        .reshape(n_rows, q_width)
    )
    middle = tokens_sub + scatter_rows(dot(attended, output_w, ((1,), (1,))), tensor_at, nt)

    inverse_two, h_two = norm_forward(middle, gain_two_full)
    logits = jnp.where(uses_sub, dot(h_two, router_w, ((1,), (0,))), NEG)
    raised = jnp.exp(logits - jnp.max(logits, axis=1, keepdims=True))
    gates = raised / jnp.sum(raised, axis=1, keepdims=True)
    gates_kept = gates * kept
    gates_high = gates_kept.astype(BF)
    gates_low = (gates_kept - gates_high.astype(F32)).astype(BF)
    extra = jnp.zeros((sub, LANES - 2 * EXPERTS), BF)
    h_ext = jnp.concatenate([h_two, gates_high, gates_low, extra], axis=1)
    if kernels:
        h_all, upper_w = gather_rows(h_ext, w_expert_in, units, own_count, nd, 2)
    else:
        h_all = lax.all_gather(h_ext, ALL, axis=0, tiled=True)
    gates_all = (
        h_all[:, D : D + EXPERTS].astype(F32) + h_all[:, D + EXPERTS : D + 2 * EXPERTS].astype(F32)
    )
    total_rows = h_all.shape[0]
    gates_own = lax.dynamic_slice_in_dim(gates_all, first_expert, own_count, 1)
    h_two_full = lax.dynamic_slice(h_all, ((dp_at * nc + ctx_at) * n_rows, 0), (n_rows, D))
    h_all = h_all[:, :D]

    gate_wide = jnp.broadcast_to(gates_own[:, :, None], (total_rows, own_count, units)).reshape(
        total_rows, width
    )
    hidden = dot(h_all, upper_w, ((1,), (0,)))
    grad_raw = dot(cot_all, lower_w, ((1,), (0,)))
    gate_part, up_part = (hidden[:, :width], hidden[:, width:])
    sigmoid = jax.nn.sigmoid(gate_part)
    silu = gate_part * sigmoid
    active = (silu * up_part).astype(BF).astype(F32)
    active_gated = (active * gate_wide).astype(BF)
    grad_gates = jnp.sum((grad_raw * active).reshape(total_rows, own_count, units), axis=2)
    grad_active = grad_raw * gate_wide
    grad_hidden = jnp.concatenate(
        [
            grad_active * up_part * sigmoid * (1.0 + gate_part * (1.0 - sigmoid)),
            grad_active * silu,
        ],
        axis=1,
    ).astype(BF)
    grad_in = dot(grad_hidden, upper_w, ((1,), (1,))).astype(BF)
    grad_gates = lax.dynamic_update_slice_in_dim(
        jnp.zeros((total_rows, LANES), BF), grad_gates.astype(BF), first_expert, 1
    )
    mixed = dot(active_gated, lower_w, ((1,), (1,))).astype(BF)
    grad_upper = dot(h_all, grad_hidden, ((0,), (0,))).astype(BF)
    grad_lower = dot(cot_all, active_gated, ((0,), (0,))).astype(BF)
    if kernels:
        grad_in, grad_upper, grad_lower = lax.optimization_barrier((grad_in, grad_upper, grad_lower))
        back_sub, grad_upper = reduce_rows([grad_in, grad_gates], grad_upper, {0: 1, 4: 2, 5: 3}, nd, 3)
        mixed, back_sub = lax.optimization_barrier((mixed, back_sub))
        mixed_sub, grad_lower = reduce_rows([mixed], grad_lower, {0: 2, 1: 1, 2: 3}, nd, 4)
        back_sub, mixed_sub = lax.optimization_barrier((back_sub, mixed_sub))
        grad_upper = lax.all_gather(grad_upper, "ctx", axis=0)
        grad_lower = lax.all_gather(grad_lower, "ctx", axis=0)
        grad_expert_in, grad_expert_out = spread(grad_upper, grad_lower, own_count)
    else:
        back = jnp.concatenate([grad_in, grad_gates], axis=1)
        back_sub = lax.psum_scatter(back, ALL, scatter_dimension=0, tiled=True).astype(F32)
        mixed_sub = lax.psum_scatter(mixed, ALL, scatter_dimension=0, tiled=True).astype(F32)
        grad_expert = jnp.concatenate([grad_upper, grad_lower], axis=1)
        grad_expert = exchange(grad_expert.reshape(nd, d_local, 3 * width), dp_at, nd)
        grad_expert = lax.all_gather(grad_expert, "ctx", axis=0)
        split = (1, nc) if by_expert else (nc, 1)
        grad_up = grad_expert[..., : 2 * width].reshape(*split, nd, d_local, 2, own_count, units)
        grad_low = grad_expert[..., 2 * width :].reshape(*split, nd, d_local, own_count, units)
        grad_up = jnp.transpose(grad_up, (3, 1, 5, 4, 2, 0, 6))
        grad_low = jnp.transpose(grad_low, (3, 1, 4, 2, 0, 5))
        grad_expert_in = grad_up.reshape(d_local, local_count, 2 * FF).astype(F32)
        grad_expert_out = grad_low.reshape(d_local, local_count, FF).astype(F32)

    result = lax.all_to_all((middle + mixed_sub).astype(BF), "tensor", 1, 0, tiled=True)

    gate_grads = back_sub[:, D : D + EXPERTS] * kept
    logit_grads = (
        gates * (gate_grads - jnp.sum(gates * gate_grads, axis=1, keepdims=True))
    ).astype(BF)
    grad_norm_two = back_sub[:, :D] + dot(logit_grads, router_w, ((1,), (1,)))
    grad_middle, grad_gain_two = norm_backward(middle, gain_two_full, inverse_two, grad_norm_two)
    grad_middle = grad_middle + cot_sub.astype(F32)
    extra = jnp.zeros((sub, LANES - EXPERTS), BF)
    grad_attn = lax.all_gather(
        jnp.concatenate([grad_middle.astype(BF), logit_grads, extra], axis=1),
        "tensor",
        axis=0,
        tiled=True,
    )
    logit_grads_full = grad_attn[:, D : D + EXPERTS]
    grad_attn = grad_attn[:, :D]
    grad_router = dot(h_two_full, logit_grads_full, ((0,), (0,)))

    grad_output_w = dot(grad_attn, attended, ((0,), (0,)))
    grad_blended = (
        dot(grad_attn, output_w, ((1,), (0,)))
        .astype(BF)
        .reshape(n_rows, kv_heads, group, HEAD_DIM)
    )
    shares = jnp.exp(scores - log_totals)
    grad_shares = jnp.einsum(
        "bagd,pad->agbp", grad_blended, value_heads, preferred_element_type=F32
    )
    inner = jnp.sum(shares * grad_shares, axis=-1, keepdims=True)
    grad_scores = (shares * (grad_shares - inner)).astype(BF)
    grad_queries = score_scale * jnp.einsum(
        "agbp,pad->bagd", grad_scores, key_heads, preferred_element_type=F32
    )
    grad_keys = score_scale * jnp.einsum(
        "agbp,bagd->pad", grad_scores, queries, preferred_element_type=F32
    )
    grad_values = jnp.einsum(
        "agbp,bagd->pad", shares_low, grad_blended, preferred_element_type=F32
    )
    grad_kv = jnp.concatenate(
        [grad_keys.reshape(pack_len, kv_width), grad_values.reshape(pack_len, kv_width)], axis=1
    ).astype(BF)
    if kernels:
        grad_kv, _ = sum_blocks(grad_kv, jnp.zeros((8, LANES), F32), 1, 5)
    else:
        grad_kv = lax.psum_scatter(grad_kv, "ctx", scatter_dimension=0, tiled=True).astype(F32)
    grad_turned = jnp.concatenate(
        [
            grad_queries.reshape(n_rows, q_heads, HEAD_DIM),
            grad_kv[:, :kv_width].reshape(n_rows, kv_heads, HEAD_DIM),
        ],
        axis=1,
    )
    grad_qkv = jnp.concatenate(
        [
            rotate(grad_turned, cosine_table, -sine_table)
            .astype(BF)
            .reshape(n_rows, q_width + kv_width),
            grad_kv[:, kv_width:].astype(BF),
        ],
        axis=1,
    )
    grad_norm_one = scatter_rows(dot(grad_qkv, qkv_w, ((1,), (1,))), tensor_at, nt)
    inverse_sub = lax.rsqrt(jnp.mean(tokens_sub * tokens_sub, axis=1, keepdims=True) + EPS)
    grad_tokens, grad_gain_one = norm_backward(
        tokens_sub, gain_one_full, inverse_sub, grad_norm_one
    )
    grad_tokens = lax.all_to_all(grad_tokens + grad_middle, "tensor", 1, 0, tiled=True)

    grad_qkv_w = dot(h_one, grad_qkv, ((0,), (0,)))
    gain_grads = jnp.stack([grad_gain_one, grad_gain_two])
    extra = jnp.zeros((D, LANES - EXPERTS), F32)
    weight_grads = jnp.concatenate([grad_qkv_w, grad_output_w, grad_router, extra], axis=1).astype(BF)
    if kernels:
        weight_grads, gain_grads = sum_blocks(weight_grads, gain_grads, nd, 6)
    else:
        weight_grads = lax.psum_scatter(
            weight_grads, ("dp", "ctx"), scatter_dimension=0, tiled=True
        )
        weight_grads = lax.all_gather(weight_grads, "ctx", axis=0, tiled=True).astype(F32)
        gain_grads = jnp.sum(lax.all_gather(gain_grads, ALL, axis=0), axis=0)
    edges = [0, q_width, q_width + kv_width, qkv_width, qkv_width + q_width]
    gain_grads = lax.dynamic_slice_in_dim(gain_grads, tensor_at * part_width, part_width, 1)
    return (
        result,
        grad_tokens,
        gain_grads[0],
        weight_grads[:, edges[0] : edges[1]],
        weight_grads[:, edges[1] : edges[2]],
        weight_grads[:, edges[2] : edges[3]],
        weight_grads[:, edges[3] : edges[4]],
        gain_grads[1],
        weight_grads[:, edges[4] : edges[4] + EXPERTS],
        grad_expert_in,
        grad_expert_out,
    )


def solution(mesh):
    return jax.shard_map(
        on_device,
        mesh=mesh,
        in_specs=(
            P(("dp", "ctx"), "tensor"),
            P("dp", None),
            P("dp", None),
            P("dp", None),
            P("tensor"),
            P("dp", "tensor"),
            P("dp", "tensor"),
            P("dp", "tensor"),
            P("dp", "tensor"),
            P("tensor"),
            P("dp", None),
            P("dp", "tensor", None),
            P("dp", "tensor", None),
            P(("dp", "ctx"), "tensor"),
        ),
        out_specs=(
            P(("dp", "ctx"), "tensor"),
            P(("dp", "ctx"), "tensor"),
            P("tensor"),
            P("dp", "tensor"),
            P("dp", "tensor"),
            P("dp", "tensor"),
            P("dp", "tensor"),
            P("tensor"),
            P("dp", None),
            P("dp", "tensor", None),
            P("dp", "tensor", None),
        ),
        check_vma=False,
    )
```

```python
import functools

import jax
import jax.numpy as jnp
from jax import lax
from jax.experimental import pallas as pl
from jax.experimental.pallas import tpu as pltpu
from jax.sharding import PartitionSpec as P

D = 1536
HEAD_DIM = 64
EXPERTS = 40
TOP_K = 8
FF = 512
EPS = 1e-06
THETA = 10000.0
NEG = -1e30
LANES = 128
ALL = ("dp", "ctx", "tensor")
BF = jnp.bfloat16
F32 = jnp.float32
MESH = pl.DeviceIdType.MESH
COST = pl.CostEstimate(flops=0, bytes_accessed=250_000_000, transcendentals=0)


def place():
    ctx = lax.axis_index("ctx")
    return (lax.axis_index("dp"), ctx // 2, ctx % 2, lax.axis_index("tensor"))


def device(z, y, k, x):
    return {"dp": z, "ctx": y * 2 + k, "tensor": x}


def greet(partners):
    barrier = pltpu.get_barrier_semaphore()
    for partner in partners:
        pl.semaphore_signal(barrier, inc=1, device_id=partner, device_id_type=MESH)
    pl.semaphore_wait(barrier, len(partners))


def partners_of(nd, z, y, k, x):
    return [device((z + hop) % nd, y, k, x) for hop in range(1, nd)] + [
        device(z, y, k, 1 - x),
        device(z, 1 - y, k, x),
        device(z, y, 1 - k, x),
    ]


def gather_kernel(own_count, units, pairs, *refs):
    own_ref, weight_ref, pair_refs = (refs[0], refs[1], refs[2 : 2 + pairs])
    out_ref, moved_ref, paired_refs = (refs[2 + pairs], refs[3 + pairs], refs[4 + pairs : 4 + 2 * pairs])
    local_sem, send_sem, recv_sem, move_local_sem, move_send_sem, move_recv_sem, pair_sem, held = refs[
        4 + 2 * pairs :
    ]
    nd, width = (out_ref.shape[0], own_ref.shape[2])
    wide = out_ref.shape[-1] != width
    z, y, k, x = place()
    up, down = (device((z + 1) % nd, y, k, x), device((z + nd - 1) % nd, y, k, x))
    greet(partners_of(nd, z, y, k, x))
    moves, kept = ([], [])
    rows, parts = (weight_ref.shape[1], weight_ref.shape[2] // (nd * units))

    def move(hop):
        to_z, from_z = ((z + hop) % nd, (z + nd - hop) % nd)
        for part in range(parts):
            for e in range(own_count):
                columns = pl.ds((part * own_count + e) * units, units)
                start = pl.multiple_of((part * nd + to_z) * units, LANES)
                source = weight_ref.at[(y * 2 + k) * own_count + e, :, pl.ds(start, units)]
                target = moved_ref.at[pl.ds(pl.multiple_of(z * rows, 16), rows), columns]
                if hop == 0:
                    at = len(kept)
                    copy = pltpu.make_async_copy(source, held.at[at], move_local_sem.at[0, at])
                    copy.start()
                    put = pltpu.make_async_copy(held.at[at], target, move_local_sem.at[1, at])
                    kept.append((copy, put))
                    continue
                slot = len(moves)
                copy = pltpu.make_async_remote_copy(
                    src_ref=source,
                    dst_ref=target,
                    send_sem=move_send_sem.at[slot],
                    recv_sem=move_recv_sem.at[slot],
                    device_id=device(to_z, y, k, x),
                    device_id_type=MESH,
                )
                copy.start()
                arrival = moved_ref.at[pl.ds(pl.multiple_of(from_z * rows, 16), rows), columns]
                moves.append((copy, arrival, slot))

    swaps = []
    for at_pair, (ref, full_ref) in enumerate(zip(pair_refs, paired_refs)):
        span = ref.shape[-1]
        mine = full_ref.at[:, pl.ds(pl.multiple_of(x * span, LANES), span)]
        copy = pltpu.make_async_remote_copy(
            src_ref=ref,
            dst_ref=mine,
            send_sem=pair_sem.at[0, at_pair],
            recv_sem=pair_sem.at[1, at_pair],
            device_id=device(z, y, k, 1 - x),
            device_id_type=MESH,
        )
        copy.start()
        swaps.append(copy)
        copy = pltpu.make_async_copy(ref, mine, pair_sem.at[2, at_pair])
        copy.start()
        swaps.append(copy)
    low = jnp.minimum(z, nd - 1 - z)
    places = []
    for step in range(nd):
        near = (step + 1) // 2
        zigzag = low + near if step % 2 else low - near
        from_low = jnp.where(step <= 2 * low, zigzag, step)
        places.append(jnp.where(2 * z < nd, from_low, nd - 1 - from_low))
    sends = []

    def at(piece):
        step, dy, dk, dx, half = piece
        chip, core, side = ((y + dy) % 2, (k + dk) % 2, (x + dx) % 2)
        if not wide:
            return out_ref.at[places[step], chip, core, side, half]
        columns = pl.ds(pl.multiple_of(side * width, LANES), width)
        return out_ref.at[places[step], chip, core, half, :, columns]

    def slot(piece):
        step, dy, dk, dx, half = piece
        return (((places[step] * 2 + dy) * 2 + dk) * 2 + dx) * 2 + half

    def send(piece, link, condition=None):
        step, dy, dk, dx, half = piece
        if link == "up":
            target, there = (up, piece)
        elif link == "down":
            target, there = (down, piece)
        elif link == "x":
            target, there = (device(z, y, k, 1 - x), (step, dy, dk, 1 - dx, half))
        elif link == "y":
            target, there = (device(z, 1 - y, k, x), (step, 1 - dy, dk, dx, half))
        else:
            target, there = (device(z, y, 1 - k, x), (step, dy, 1 - dk, dx, half))
        own = piece[:4] == (0, 0, 0, 0)
        copy = pltpu.make_async_remote_copy(
            src_ref=own_ref.at[half] if own else at(piece),
            dst_ref=at(piece),
            send_sem=send_sem.at[len(sends)],
            recv_sem=recv_sem.at[slot(there)],
            device_id=target,
            device_id_type=MESH,
        )
        if condition is None:
            copy.start()
        else:
            pl.when(condition)(copy.start)
        sends.append((copy, condition))

    def arrived(piece):
        pltpu.make_async_remote_copy(
            src_ref=at(piece),
            dst_ref=at(piece),
            send_sem=send_sem.at[0],
            recv_sem=recv_sem.at[slot(piece)],
            device_id=device(z, y, k, 1 - x),
            device_id_type=MESH,
        ).wait_recv()

    own_copies = []
    for half in range(2):
        own_copy = pltpu.make_async_copy(
            own_ref.at[half], at((0, 0, 0, 0, half)), local_sem.at[half]
        )
        own_copy.start()
        own_copies.append(own_copy)
    links = (("x", "y"), ("y", "x"))
    for step in range(nd + 2):
        if step < nd:
            came = places[step]
            for half in range(2):
                piece = (step, 0, 0, 0, half)
                if step:
                    arrived(piece)
                send(piece, "up", (came <= z) & (z < nd - 1))
                send(piece, "down", (came >= z) & (z > 0))
                send(piece, links[half][0])
            for half in range(2):
                piece = (step, 0, 0, 0, half)
                send(piece, links[half][1])
                send(piece, "k")
            if step == 0:
                move(0)
            if step == 1:
                for copy, put in kept:
                    copy.wait()
                    put.start()
            if step == nd - 2:
                for hop in [2, 1, 3] if nd == 4 else range(1, nd):
                    move(hop)
        if 1 <= step < nd + 1:
            for half in range(2):
                piece = (step - 1, half, 0, 1 - half, half)
                arrived(piece)
                send(piece, links[half][1])
                send(piece, "k")
        if 2 <= step:
            for half in range(2):
                for d in range(2):
                    piece = (step - 2, 1, 0, d, 0) if half == 0 else (step - 2, d, 0, 1, 1)
                    arrived(piece)
                    send(piece, "k")
    for step in range(nd):
        for dy in range(2):
            for dx in range(2):
                for half in range(2):
                    arrived((step, dy, 1, dx, half))
    for own_copy in own_copies + [put for _, put in kept]:
        own_copy.wait()
    for copy in swaps:
        copy.wait()
    for copy, arrival, slot in moves:
        pltpu.make_async_remote_copy(
            src_ref=arrival,
            dst_ref=arrival,
            send_sem=move_send_sem.at[slot],
            recv_sem=move_recv_sem.at[slot],
            device_id=device(z, y, k, 1 - x),
            device_id_type=MESH,
        ).wait_recv()
        copy.wait_send()
    for copy, condition in sends:
        if condition is None:
            copy.wait_send()
        else:
            pl.when(condition)(copy.wait_send)


def gather_rows(own, weight, units, own_count, nd, collective_id, pairs=(), wide=False):
    rows, width = own.shape
    half = rows // 2
    shape = (nd, 2, 2, 2, half, 2 * width) if wide else (nd, 2, 2, 2, 2, half, width)
    depth, moved = (nd * weight.shape[1], own_count * weight.shape[2] // nd)
    count = moved // units
    vmem, anywhere = (pl.BlockSpec(memory_space=pltpu.VMEM), pl.BlockSpec(memory_space=pl.ANY))
    out = pl.pallas_call(
        functools.partial(gather_kernel, own_count, units, len(pairs)),
        in_specs=[vmem, anywhere] + [vmem] * len(pairs),
        out_specs=[anywhere] * (2 + len(pairs)),
        out_shape=[
            jax.ShapeDtypeStruct(shape, own.dtype),
            jax.ShapeDtypeStruct((depth, moved), weight.dtype),
        ]
        + [jax.ShapeDtypeStruct((p.shape[0], 2 * p.shape[1]), p.dtype) for p in pairs],
        scratch_shapes=[
            pltpu.SemaphoreType.DMA((2,)),
            pltpu.SemaphoreType.DMA((nd * 18,)),
            pltpu.SemaphoreType.DMA((nd * 16,)),
            pltpu.SemaphoreType.DMA((2, count)),
            pltpu.SemaphoreType.DMA(((nd - 1) * count,)),
            pltpu.SemaphoreType.DMA(((nd - 1) * count,)),
            pltpu.SemaphoreType.DMA((3, max(len(pairs), 1))),
            pltpu.VMEM((count, weight.shape[1], units), weight.dtype),
        ],
        compiler_params=pltpu.CompilerParams(collective_id=collective_id, has_side_effects=True),
        cost_estimate=COST,
        name="gather_rows",
    )(own.reshape(2, half, width), weight, *pairs)
    return (out[0].reshape(-1, shape[-1]), *out[1:])


def ctx_kernel(own_ref, out_ref, local_sem, send_sem, recv_sem):
    z, y, k, x = place()
    y_partner, core = (device(z, 1 - y, k, x), device(z, y, 1 - k, x))
    greet([y_partner, core])
    kept = pltpu.make_async_copy(own_ref, out_ref.at[y, k], local_sem)
    kept.start()
    copies = []
    for at, (source, chip, target) in enumerate(
        ((own_ref, y, y_partner), (own_ref, y, core), (out_ref.at[1 - y, k], 1 - y, core))
    ):
        if at == 2:
            copies[0].wait_recv()
        copy = pltpu.make_async_remote_copy(
            src_ref=source,
            dst_ref=out_ref.at[chip, k],
            send_sem=send_sem.at[at],
            recv_sem=recv_sem.at[at],
            device_id=target,
            device_id_type=MESH,
        )
        copy.start()
        copies.append(copy)
    kept.wait()
    for copy in copies[1:]:
        copy.wait_recv()
    for copy in copies:
        copy.wait_send()


def gather_ctx(own, collective_id):
    out = pl.pallas_call(
        ctx_kernel,
        in_specs=[pl.BlockSpec(memory_space=pltpu.VMEM)],
        out_specs=pl.BlockSpec(memory_space=pl.ANY),
        out_shape=jax.ShapeDtypeStruct((2, 2, *own.shape), own.dtype),
        scratch_shapes=[
            pltpu.SemaphoreType.DMA,
            pltpu.SemaphoreType.DMA((3,)),
            pltpu.SemaphoreType.DMA((3,)),
        ],
        compiler_params=pltpu.CompilerParams(collective_id=collective_id, has_side_effects=True),
        name="gather_ctx",
    )(own)
    return out.reshape(-1, own.shape[1])


def reduce_kernel(count, when, *refs):
    parts, moved_ref, out_ref, arrived_ref = (refs[:count], *refs[count : count + 3])
    own, from_core, first, second, across, load_sem, send_sem, recv_sem = refs[count + 3 : -4]
    move_local_sem, move_send_sem, move_recv_sem, held = refs[-4:]
    nd = parts[0].shape[0]
    z, y, k, x = place()
    greet(partners_of(nd, z, y, k, x))
    order = [hop for hop in (2, 1, 3, 0)] if nd == 4 else list(range(1, nd)) + [0]
    sends, loads = ([], [])

    def spot(step, dy, dx, half):
        return ((step * 2 + dy) * 2 + dx) * 2 + half

    def send(source, there, target, slot):
        copy = pltpu.make_async_remote_copy(
            src_ref=source,
            dst_ref=there,
            send_sem=send_sem.at[len(sends)],
            recv_sem=recv_sem.at[slot],
            device_id=target,
            device_id_type=MESH,
        )
        copy.start()
        sends.append(copy)

    def arrived(there, slot):
        pltpu.make_async_remote_copy(
            src_ref=there,
            dst_ref=there,
            send_sem=send_sem.at[0],
            recv_sem=recv_sem.at[slot],
            device_id=device(z, y, k, 1 - x),
            device_id_type=MESH,
        ).wait_recv()

    def add(to, what, index):
        to_rows = own.shape[1]

        def body(i, carry):
            rows = pl.ds(i * 16, 16)
            total = own[to, rows, :].astype(F32) + what[index, rows, :].astype(F32)
            own[to, rows, :] = total.astype(BF)
            return carry

        lax.fori_loop(0, to_rows // 16, body, 0)

    spans, start = ([], 0)
    for ref in parts:
        spans.append(pl.ds(start, ref.shape[-1]))
        start += ref.shape[-1]
    first_slot, second_slot, across_slot, core_slot = (0, nd * 4, nd * 6, nd * 7)
    for step, dz in enumerate(order):
        for dy in range(2):
            for dx in range(2):
                there = pl.ds(spot(step, dy, dx, 0), 2)
                block = ((z + dz) % nd, (y + dy) % 2)
                for ref, span in zip(parts, spans):
                    send(
                        ref.at[block[0], block[1], 1 - k, (x + dx) % 2],
                        from_core.at[there, :, span],
                        device(z, y, 1 - k, x),
                        core_slot + len(loads),
                    )
                    load = pltpu.make_async_copy(
                        ref.at[block[0], block[1], k, (x + dx) % 2],
                        own.at[there, :, span],
                        load_sem.at[len(loads)],
                    )
                    load.start()
                    loads.append(load)
    x_partner, y_partner = (device(z, y, k, 1 - x), device(z, 1 - y, k, x))
    taken = pltpu.make_async_copy(moved_ref.at[z], held, move_local_sem.at[0])
    taken.start()
    kept = pltpu.make_async_copy(held, arrived_ref.at[z], move_local_sem.at[1])
    moves = []

    def move(hop):
        to_z = (z + hop) % nd
        copy = pltpu.make_async_remote_copy(
            src_ref=moved_ref.at[to_z],
            dst_ref=arrived_ref.at[z],
            send_sem=move_send_sem.at[hop - 1],
            recv_sem=move_recv_sem.at[hop - 1],
            device_id=device(to_z, y, k, x),
            device_id_type=MESH,
        )
        copy.start()
        moves.append((copy, hop))

    for step in range(nd + 2):
        if step == 0 and step in when:
            move(when[step])
        if step == 1:
            taken.wait()
            kept.start()
        if step < nd:
            for at in range(4):
                base = spot(step, 0, 0, 0) + at * 2
                for which, span in enumerate(spans):
                    slot = (step * 4 + at) * count + which
                    loads[slot].wait()
                    arrived(from_core.at[pl.ds(base, 2), :, span], core_slot + slot)

            def pair(i, carry, step=step):
                add(step * 8 + i, from_core, step * 8 + i)
                return carry

            lax.fori_loop(0, 8, pair, 0)
            for d in range(2):
                slot = step * 4 + d
                send(own.at[spot(step, 1, d, 0)], first.at[slot], y_partner, first_slot + slot)
                slot = step * 4 + 2 + d
                send(own.at[spot(step, d, 1, 1)], first.at[slot], x_partner, first_slot + slot)
        if 1 <= step < nd + 1:
            now = step - 1
            for d in (1, 0):
                slot = now * 4 + d
                arrived(first.at[slot], first_slot + slot)
                add(spot(now, 0, d, 0), first, slot)
                slot = now * 4 + 2 + d
                arrived(first.at[slot], first_slot + slot)
                add(spot(now, d, 0, 1), first, slot)
                if d == 1:
                    slot = now * 2
                    send(own.at[spot(now, 0, 1, 0)], second.at[slot], x_partner, second_slot + slot)
                    slot = now * 2 + 1
                    send(own.at[spot(now, 1, 0, 1)], second.at[slot], y_partner, second_slot + slot)
        if 2 <= step:
            now = step - 2
            for half in range(2):
                slot = now * 2 + half
                arrived(second.at[slot], second_slot + slot)
                add(spot(now, 0, 0, half), second, slot)
            hop = order[now]
            if hop:
                slot = nd - hop - 1
                send(
                    own.at[pl.ds(spot(now, 0, 0, 0), 2)],
                    across.at[slot],
                    device((z + hop) % nd, y, k, x),
                    across_slot + slot,
                )
        if step and step in when:
            move(when[step])
    for slot in range(nd - 1):
        arrived(across.at[slot], across_slot + slot)
    mine = spot(order.index(0), 0, 0, 0)
    for half in range(2):

        def total(i, carry, half=half):
            rows = pl.ds(i * 16, 16)
            value = own[mine + half, rows, :].astype(F32)
            for slot in range(nd - 1):
                value = value + across[slot, half, rows, :].astype(F32)
            out_ref[half, rows, :] = value
            return carry

        lax.fori_loop(0, own.shape[1] // 16, total, 0)
    kept.wait()
    for copy, hop in moves:
        there = arrived_ref.at[(z + nd - hop) % nd]
        pltpu.make_async_remote_copy(
            src_ref=there,
            dst_ref=there,
            send_sem=move_send_sem.at[hop - 1],
            recv_sem=move_recv_sem.at[hop - 1],
            device_id=x_partner,
            device_id_type=MESH,
        ).wait_recv()
        copy.wait_send()
    for copy in sends:
        copy.wait_send()


def reduce_rows(parts, moved, when, nd, collective_id):
    moved = moved.reshape(nd, moved.shape[0] // nd, moved.shape[1])
    rows = parts[0].shape[0] // (nd * 8)
    width = sum(part.shape[1] for part in parts)
    half, count = (rows // 2, len(parts))
    sends = nd * (4 * count + 7)
    out = pl.pallas_call(
        functools.partial(reduce_kernel, count, when),
        in_specs=[pl.BlockSpec(memory_space=pl.ANY)] * (count + 1),
        out_specs=[pl.BlockSpec(memory_space=pltpu.VMEM), pl.BlockSpec(memory_space=pl.ANY)],
        out_shape=[
            jax.ShapeDtypeStruct((2, half, width), F32),
            jax.ShapeDtypeStruct(moved.shape, moved.dtype),
        ],
        scratch_shapes=[
            pltpu.VMEM((nd * 8, half, width), BF),
            pltpu.VMEM((nd * 8, half, width), BF),
            pltpu.VMEM((nd * 4, half, width), BF),
            pltpu.VMEM((nd * 2, half, width), BF),
            pltpu.VMEM((nd - 1, 2, half, width), BF),
            pltpu.SemaphoreType.DMA((nd * 4 * count,)),
            pltpu.SemaphoreType.DMA((sends,)),
            pltpu.SemaphoreType.DMA((sends,)),
            pltpu.SemaphoreType.DMA((2,)),
            pltpu.SemaphoreType.DMA((nd - 1,)),
            pltpu.SemaphoreType.DMA((nd - 1,)),
            pltpu.VMEM(moved.shape[1:], moved.dtype),
        ],
        compiler_params=pltpu.CompilerParams(
            collective_id=collective_id, has_side_effects=True, vmem_limit_bytes=48 << 20
        ),
        cost_estimate=COST,
        name="reduce_rows",
    )(*[part.reshape(nd, 2, 2, 2, 2, half, part.shape[1]) for part in parts], moved)
    return (out[0].reshape(rows, width), out[1])


def sum_kernel(across_dp, count, *refs):
    parts, gain_ref, out_ref, total_ref = (refs[:count], *refs[count : count + 3])
    own, from_core, from_chip, across, result, gains, load_sem, send_sem, recv_sem, gain_sems = refs[
        count + 3 :
    ]
    spans, start = ([], 0)
    for ref in parts:
        spans.append(pl.ds(start, ref.shape[-1]))
        start += ref.shape[-1]
    nd = parts[0].shape[0]
    z, y, k, x = place()
    y_partner, core = (device(z, 1 - y, k, x), device(z, y, 1 - k, x))
    x_partner = device(z, y, k, 1 - x)
    greet([device((z + hop) % nd, y, k, x) for hop in range(1, nd)] + [x_partner, y_partner, core])
    gain_sends = []

    def gain_copy(slot, target):
        copy = pltpu.make_async_remote_copy(
            src_ref=gains.at[0, slot],
            dst_ref=gains.at[1, slot],
            send_sem=gain_sems.at[0, slot],
            recv_sem=gain_sems.at[1, slot],
            device_id=target,
            device_id_type=MESH,
        )
        copy.start()
        gain_sends.append(copy)

    gains[0, 0] = gain_ref[...]
    gain_copy(0, core)
    order = ([2, 1, 3] if nd == 4 else list(range(1, nd))) + [0]
    sends, loads = ([], [])
    chip_slot, across_slot, result_slot, core_slot = (0, nd, nd * 2, nd * 2 + 3)

    def send(source, there, target, slot):
        copy = pltpu.make_async_remote_copy(
            src_ref=source,
            dst_ref=there,
            send_sem=send_sem.at[len(sends)],
            recv_sem=recv_sem.at[slot],
            device_id=target,
            device_id_type=MESH,
        )
        copy.start()
        sends.append(copy)

    def arrived(there, slot):
        pltpu.make_async_remote_copy(
            src_ref=there,
            dst_ref=there,
            send_sem=send_sem.at[0],
            recv_sem=recv_sem.at[slot],
            device_id=core,
            device_id_type=MESH,
        ).wait_recv()

    def add(to, what, index):
        def body(i, carry):
            rows = pl.ds(i * 16, 16)
            total = own[to, rows, :].astype(F32) + what[index, rows, :].astype(F32)
            own[to, rows, :] = total.astype(BF)
            return carry

        lax.fori_loop(0, own.shape[1] // 16, body, 0)

    for step, dz in enumerate(order):
        for dy in (1, 0):
            at = step * 2 + dy
            for ref, span in zip(parts, spans):
                block = ref.at[(z + dz) % nd, (y + dy) % 2]
                send(block.at[1 - k], from_core.at[at, :, span], core, core_slot + len(loads))
                load = pltpu.make_async_copy(
                    block.at[k], own.at[at, :, span], load_sem.at[len(loads)]
                )
                load.start()
                loads.append(load)
    stages = [y_partner, x_partner]
    if nd > 1:
        stages += [device(z + 1 - z % 2 * 2, y, k, x), device((z + 2) % nd, y, k, x)]
    for slot, target in enumerate(stages + [None], 1):
        gain_sends[-1].wait_recv()
        gains[0, slot] = gains[0, slot - 1] + gains[1, slot - 1]
        if target is not None:
            gain_copy(slot, target)
    total_ref[...] = gains[0, len(stages) + 1]
    for step in range(nd + 1):
        if step < nd:
            for dy in (1, 0):
                at = step * 2 + dy
                for which, span in enumerate(spans):
                    slot = (step * 2 + 1 - dy) * count + which
                    loads[slot].wait()
                    arrived(from_core.at[at, :, span], core_slot + slot)
                add(at, from_core, at)
                if dy:
                    send(own.at[at], from_chip.at[step], y_partner, chip_slot + step)
        if step:
            now = step - 1
            arrived(from_chip.at[now], chip_slot + now)
            hop = order[now]
            if hop or across_dp:
                add(now * 2, from_chip, now)
            if hop:
                slot = nd - hop - 1
                target = device((z + hop) % nd, y, k, x)
                send(own.at[now * 2], across.at[slot], target, across_slot + slot)
    for slot in range(nd - 1):
        arrived(across.at[slot], across_slot + slot)
    mine = (nd - 1) * 2

    def total(i, carry):
        rows = pl.ds(i * 16, 16)
        value = own[mine, rows, :].astype(F32)
        if across_dp:
            for slot in range(nd - 1):
                value = value + across[slot, rows, :].astype(F32)
            result[y, k, rows, :] = value.astype(BF)
        else:
            out_ref[rows, :] = value + from_chip[0, rows, :].astype(F32)
        return carry

    lax.fori_loop(0, own.shape[1] // 16, total, 0)
    if across_dp:
        send(result.at[y, k], result.at[y, k], y_partner, result_slot)
        send(result.at[y, k], result.at[y, k], core, result_slot + 1)
        arrived(result.at[1 - y, k], result_slot)
        send(result.at[1 - y, k], result.at[1 - y, k], core, result_slot + 2)
        arrived(result.at[y, 1 - k], result_slot + 1)
        arrived(result.at[1 - y, 1 - k], result_slot + 2)

        def widen(i, carry):
            rows = pl.ds(i * 16, 16)
            for chip in range(2):
                for side in range(2):
                    out_ref[chip, side, rows, :] = result[chip, side, rows, :].astype(F32)
            return carry

        lax.fori_loop(0, own.shape[1] // 16, widen, 0)
    for copy in gain_sends:
        copy.wait_send()
    for copy in sends:
        copy.wait_send()


def sum_blocks(parts, gain, nd, collective_id):
    rows, width = (parts[0].shape[0] // (nd * 4), sum(part.shape[1] for part in parts))
    count = len(parts)
    sends = nd * (2 * count + 2) + 3
    shape = (2, 2, rows, width) if nd > 1 else (rows, width)
    out = pl.pallas_call(
        functools.partial(sum_kernel, nd > 1, count),
        in_specs=[pl.BlockSpec(memory_space=pl.ANY)] * count
        + [pl.BlockSpec(memory_space=pltpu.VMEM)],
        out_specs=[pl.BlockSpec(memory_space=pltpu.VMEM)] * 2,
        out_shape=[jax.ShapeDtypeStruct(shape, F32), jax.ShapeDtypeStruct(gain.shape, F32)],
        scratch_shapes=[
            pltpu.VMEM((nd * 2, rows, width), BF),
            pltpu.VMEM((nd * 2, rows, width), BF),
            pltpu.VMEM((nd, rows, width), BF),
            pltpu.VMEM((max(nd - 1, 1), rows, width), BF),
            pltpu.VMEM((2, 2, rows, width) if nd > 1 else (1, 1, 16, LANES), BF),
            pltpu.VMEM((2, 6, *gain.shape), F32),
            pltpu.SemaphoreType.DMA((nd * 2 * count,)),
            pltpu.SemaphoreType.DMA((sends,)),
            pltpu.SemaphoreType.DMA((sends,)),
            pltpu.SemaphoreType.DMA((2, 5)),
        ],
        compiler_params=pltpu.CompilerParams(
            collective_id=collective_id, has_side_effects=True, vmem_limit_bytes=48 << 20
        ),
        cost_estimate=COST,
        name="sum_blocks",
    )(*[part.reshape(nd, 2, 2, rows, part.shape[1]) for part in parts], gain)
    return (out[0].reshape(-1, width), out[1])


def spread_kernel(up_ref, low_ref, in_ref, out_ref):
    nc, nd = up_ref.shape[:2]
    own_count = in_ref.shape[0] // nc
    units = low_ref.shape[3] // own_count
    for c in range(nc):
        for e in range(own_count):
            for part in range(3):
                got_ref, to_ref, base = ((up_ref, in_ref, part) if part < 2 else (low_ref, out_ref, 0))
                start = (base * own_count + e) * units
                for at in range(nd):
                    columns = slice((base * nd + at) * units, (base * nd + at + 1) * units)
                    to_ref[c * own_count + e, :, columns] = got_ref[
                        c, at, :, start : start + units
                    ].astype(F32)


def spread(up, low, own_count):
    nc, nd, d_local, low_width = low.shape
    experts, units = (nc * own_count, low_width // own_count)
    block = 32
    into, out = pl.pallas_call(
        spread_kernel,
        grid=(d_local // block,),
        in_specs=[
            pl.BlockSpec((nc, nd, block, ref.shape[3]), lambda i: (0, 0, i, 0)) for ref in (up, low)
        ],
        out_specs=[
            pl.BlockSpec((experts, block, parts * nd * units), lambda i: (0, i, 0))
            for parts in (2, 1)
        ],
        out_shape=[
            jax.ShapeDtypeStruct((experts, d_local, parts * nd * units), F32) for parts in (2, 1)
        ],
        name="spread",
    )(up, low)
    return (jnp.transpose(into, (1, 0, 2)), jnp.transpose(out, (1, 0, 2)))


def rope_tables(position):
    halves = HEAD_DIM // 2
    frequency = THETA ** (-2.0 * jnp.arange(halves, dtype=F32) / HEAD_DIM)
    angles = position[:, None] * frequency[None, :]
    return (jnp.cos(angles)[:, None, :], jnp.sin(angles)[:, None, :])


def rotate(values, cosine_table, sine_table):
    halves = values.shape[-1] // 2
    first_half, second_half = (values[..., :halves], values[..., halves:])
    return jnp.concatenate(
        [
            first_half * cosine_table - second_half * sine_table,
            second_half * cosine_table + first_half * sine_table,
        ],
        axis=-1,
    )


def dot(a, b, dims):
    return lax.dot_general(a, b, (dims, ((), ())), preferred_element_type=F32)


def norm_forward(rows, gain):
    inverse = lax.rsqrt(jnp.mean(rows * rows, axis=1, keepdims=True) + EPS)
    return (inverse, (rows * inverse * gain[None, :]).astype(BF))


def norm_backward(rows, gain, inverse, grad_normed):
    weighted = grad_normed * gain[None, :]
    inner = jnp.sum(weighted * rows, axis=1, keepdims=True)
    grad_rows = weighted * inverse - rows * (inverse * inverse * inverse * inner / D)
    return (grad_rows, jnp.sum(grad_normed * rows * inverse, axis=0))


def exchange(parts, at, count):
    result = lax.dynamic_update_index_in_dim(
        jnp.zeros_like(parts), lax.dynamic_index_in_dim(parts, at, 0), at, 0
    )
    for hop in range(1, count):
        sent = lax.dynamic_index_in_dim(parts, (at + hop) % count, 0)
        got = lax.ppermute(sent, "dp", [(i, (i + hop) % count) for i in range(count)])
        result = lax.dynamic_update_index_in_dim(result, got, (at - hop) % count, 0)
    return result


def scatter_rows(partial, at, count):
    if count != 2:
        return lax.psum_scatter(
            partial.astype(BF), "tensor", scatter_dimension=0, tiled=True
        ).astype(F32)
    half = partial.shape[0] // 2
    sent = lax.dynamic_slice_in_dim(partial, (1 - at) * half, half, 0).astype(BF)
    got = lax.ppermute(sent, "tensor", [(0, 1), (1, 0)])
    return lax.dynamic_slice_in_dim(partial, at * half, half, 0) + got.astype(F32)


def on_device(
    tokens,
    segments,
    order,
    routes,
    gain_one,
    w_query,
    w_key,
    w_value,
    w_output,
    gain_two,
    w_router,
    w_expert_in,
    w_expert_out,
    cotangent,
):
    nd, nc, nt = (lax.axis_size("dp"), lax.axis_size("ctx"), lax.axis_size("tensor"))
    dp_at, ctx_at, tensor_at = (
        lax.axis_index("dp"),
        lax.axis_index("ctx"),
        lax.axis_index("tensor"),
    )
    n_rows, part_width = tokens.shape
    sub = n_rows // nt
    pack_len = order.shape[1]
    d_local = w_query.shape[0]
    q_width, kv_width = (w_query.shape[1], w_key.shape[1])
    q_heads, kv_heads = (q_width // HEAD_DIM, kv_width // HEAD_DIM)
    group = q_heads // kv_heads
    qkv_width = q_width + 2 * kv_width
    local_count = w_expert_in.shape[1]
    capacity = n_rows * 3 // 8

    packed = jnp.concatenate([w_query, w_key, w_value, w_router], axis=1)
    share = d_local // nc
    packed = lax.dynamic_slice_in_dim(packed, ctx_at * share, share, 0)
    packed = lax.all_gather(packed, ("dp", "ctx"), axis=0, tiled=True)
    qkv_w, router_w = (packed[:, :qkv_width], packed[:, qkv_width:])
    output_w = lax.all_gather(
        lax.dynamic_slice_in_dim(w_output, ctx_at * share, share, 0),
        ("dp", "ctx"),
        axis=0,
        tiled=True,
    )
    kernels = (nd, nc, nt) == (4, 4, 2)
    by_expert = local_count % nc == 0
    own_count = local_count // nc if by_expert else local_count
    units = FF // nd if by_expert else FF // (nd * nc)
    width = own_count * units
    gains = jnp.stack([gain_one, gain_two])
    if kernels:
        w_expert_in, w_expert_out = [jnp.transpose(w, (1, 0, 2)) for w in (w_expert_in, w_expert_out)]
        cot_all, lower_w, tokens_full, gains = gather_rows(
            cotangent, w_expert_out, units, own_count, nd, 1, (tokens, gains), wide=True
        )
        cot_sub = lax.dynamic_slice_in_dim(
            cot_all, (dp_at * nc + ctx_at) * n_rows + tensor_at * sub, sub, 0
        )
    else:
        tokens_full = lax.all_gather(tokens, "tensor", axis=1, tiled=True)
        gains = lax.all_gather(gains, "tensor", axis=1, tiled=True)
        cot_sub = lax.all_to_all(cotangent, "tensor", 0, 1, tiled=True)
        cot_all = lax.all_gather(cot_sub, ALL, axis=0, tiled=True)
    gain_one_full, gain_two_full = (gains[0], gains[1])
    tokens_sub = lax.dynamic_slice_in_dim(tokens_full, tensor_at * sub, sub, 0).astype(F32)

    first_expert = tensor_at * local_count + (ctx_at * own_count if by_expert else 0)
    if not kernels:
        if by_expert:
            own_in = lax.dynamic_slice_in_dim(w_expert_in, ctx_at * own_count, own_count, 1)
            own_out = lax.dynamic_slice_in_dim(w_expert_out, ctx_at * own_count, own_count, 1)
            own_in = own_in.reshape(d_local, own_count, 2, nd, units)
            own_out = own_out.reshape(d_local, own_count, nd, units)
        else:
            own_in = w_expert_in.reshape(d_local, own_count, 2, nd, nc, units)
            own_out = w_expert_out.reshape(d_local, own_count, nd, nc, units)
            own_in = lax.dynamic_index_in_dim(own_in, ctx_at, 4, False)
            own_out = lax.dynamic_index_in_dim(own_out, ctx_at, 3, False)
        own_in = jnp.transpose(own_in, (3, 0, 2, 1, 4)).reshape(nd, d_local, 2 * width)
        own_out = jnp.transpose(own_out, (2, 0, 1, 3)).reshape(nd, d_local, width)
        expert_w = exchange(jnp.concatenate([own_in, own_out], axis=2), dp_at, nd)
        expert_w = expert_w.reshape(D, 3 * width)
        upper_w, lower_w = (expert_w[:, : 2 * width], expert_w[:, 2 * width :])

    order_row = order[0]
    places = jnp.arange(pack_len, dtype=jnp.int32)
    dealt = jnp.sum(jnp.where(order_row[:, None] == places[None, :], places[:, None], 0), axis=0)
    sub_start = ctx_at * n_rows + tensor_at * sub
    dealt_sub = lax.dynamic_slice_in_dim(dealt, sub_start, sub)
    experts_all = jnp.arange(EXPERTS, dtype=jnp.int32)
    uses = jnp.any(routes[:, :, None] == experts_all[None, None, :], axis=1)
    earlier = (dealt_sub[:, None] // n_rows == dealt[None, :] // n_rows) & (
        dealt[None, :] < dealt_sub[:, None]
    )
    ranks = dot(earlier.astype(BF), uses.astype(BF), ((1,), (0,)))
    uses_sub = lax.dynamic_slice_in_dim(uses, sub_start, sub, 0)
    kept = (uses_sub & (ranks < capacity)).astype(F32)

    segment_row = segments[0]
    local_segs = lax.dynamic_slice_in_dim(segment_row, ctx_at * n_rows, n_rows)
    local_places = ctx_at * n_rows + jnp.arange(n_rows, dtype=jnp.int32)
    starts = jnp.sum((segment_row[None, :] < local_segs[:, None]).astype(jnp.int32), axis=1)
    cosine_table, sine_table = rope_tables((local_places - starts).astype(F32))
    _, h_one = norm_forward(tokens_full.astype(F32), gain_one_full)
    if kernels:
        h_one, cot_all, cot_sub = lax.optimization_barrier((h_one, cot_all, cot_sub))
    projected = dot(h_one, qkv_w, ((1,), (0,)))
    turned = rotate(
        projected[:, : q_width + kv_width].reshape(n_rows, q_heads + kv_heads, HEAD_DIM),
        cosine_table,
        sine_table,
    ).astype(BF)
    queries = turned[:, :q_heads].reshape(n_rows, kv_heads, group, HEAD_DIM)
    kv_rows = jnp.concatenate(
        [
            turned[:, q_heads:].reshape(n_rows, kv_width),
            projected[:, q_width + kv_width :].astype(BF),
        ],
        axis=1,
    )
    if kernels:
        kv_all = gather_ctx(kv_rows, 7)
    else:
        kv_all = lax.all_gather(kv_rows, "ctx", axis=0, tiled=True)
    key_heads = kv_all[:, :kv_width].reshape(pack_len, kv_heads, HEAD_DIM)
    value_heads = kv_all[:, kv_width:].reshape(pack_len, kv_heads, HEAD_DIM)
    allowed = (local_segs[:, None] == segment_row[None, :]) & (
        local_places[:, None] >= places[None, :]
    )
    score_scale = HEAD_DIM ** (-0.5)
    scores = score_scale * jnp.einsum(
        "bagd,pad->agbp", queries, key_heads, preferred_element_type=F32
    )
    scores = jnp.where(allowed[None, None], scores, NEG)
    highest = jnp.max(scores, axis=-1, keepdims=True)
    weights = jnp.exp(scores - highest)
    totals = jnp.sum(weights, axis=-1, keepdims=True)
    shares_low = (weights / totals).astype(BF)
    log_totals = highest + jnp.log(totals)
    attended = (
        jnp.einsum("agbp,pad->bagd", shares_low, value_heads, preferred_element_type=F32)
        .astype(BF)
        .reshape(n_rows, q_width)
    )
    middle = tokens_sub + scatter_rows(dot(attended, output_w, ((1,), (1,))), tensor_at, nt)

    inverse_two, h_two = norm_forward(middle, gain_two_full)
    logits = jnp.where(uses_sub, dot(h_two, router_w, ((1,), (0,))), NEG)
    raised = jnp.exp(logits - jnp.max(logits, axis=1, keepdims=True))
    gates = raised / jnp.sum(raised, axis=1, keepdims=True)
    gates_kept = gates * kept
    gates_high = gates_kept.astype(BF)
    gates_low = (gates_kept - gates_high.astype(F32)).astype(BF)
    extra = jnp.zeros((sub, LANES - 2 * EXPERTS), BF)
    h_ext = jnp.concatenate([h_two, gates_high, gates_low, extra], axis=1)
    if kernels:
        h_all, upper_w = gather_rows(h_ext, w_expert_in, units, own_count, nd, 2)
    else:
        h_all = lax.all_gather(h_ext, ALL, axis=0, tiled=True)
    gates_all = (
        h_all[:, D : D + EXPERTS].astype(F32) + h_all[:, D + EXPERTS : D + 2 * EXPERTS].astype(F32)
    )
    total_rows = h_all.shape[0]
    gates_own = lax.dynamic_slice_in_dim(gates_all, first_expert, own_count, 1)
    h_two_full = lax.dynamic_slice(h_all, ((dp_at * nc + ctx_at) * n_rows, 0), (n_rows, D))
    h_all = h_all[:, :D]

    gate_wide = jnp.broadcast_to(gates_own[:, :, None], (total_rows, own_count, units)).reshape(
        total_rows, width
    )
    hidden = dot(h_all, upper_w, ((1,), (0,)))
    grad_raw = dot(cot_all, lower_w, ((1,), (0,)))
    gate_part, up_part = (hidden[:, :width], hidden[:, width:])
    sigmoid = jax.nn.sigmoid(gate_part)
    silu = gate_part * sigmoid
    active = (silu * up_part).astype(BF).astype(F32)
    active_gated = (active * gate_wide).astype(BF)
    grad_gates = jnp.sum((grad_raw * active).reshape(total_rows, own_count, units), axis=2)
    grad_active = grad_raw * gate_wide
    grad_hidden = jnp.concatenate(
        [
            grad_active * up_part * sigmoid * (1.0 + gate_part * (1.0 - sigmoid)),
            grad_active * silu,
        ],
        axis=1,
    ).astype(BF)
    grad_in = dot(grad_hidden, upper_w, ((1,), (1,))).astype(BF)
    grad_gates = lax.dynamic_update_slice_in_dim(
        jnp.zeros((total_rows, LANES), BF), grad_gates.astype(BF), first_expert, 1
    )
    mixed = dot(active_gated, lower_w, ((1,), (1,))).astype(BF)
    grad_upper = dot(h_all, grad_hidden, ((0,), (0,))).astype(BF)
    grad_lower = dot(cot_all, active_gated, ((0,), (0,))).astype(BF)
    if kernels:
        grad_in, grad_upper, grad_lower = lax.optimization_barrier((grad_in, grad_upper, grad_lower))
        back_sub, grad_upper = reduce_rows([grad_in, grad_gates], grad_upper, {0: 1, 4: 2, 5: 3}, nd, 3)
        grad_upper = lax.all_gather(grad_upper, "ctx", axis=0)
    else:
        back = jnp.concatenate([grad_in, grad_gates], axis=1)
        back_sub = lax.psum_scatter(back, ALL, scatter_dimension=0, tiled=True).astype(F32)
        mixed_sub = lax.psum_scatter(mixed, ALL, scatter_dimension=0, tiled=True).astype(F32)
        grad_expert = jnp.concatenate([grad_upper, grad_lower], axis=1)
        grad_expert = exchange(grad_expert.reshape(nd, d_local, 3 * width), dp_at, nd)
        grad_expert = lax.all_gather(grad_expert, "ctx", axis=0)
        split = (1, nc) if by_expert else (nc, 1)
        grad_up = grad_expert[..., : 2 * width].reshape(*split, nd, d_local, 2, own_count, units)
        grad_low = grad_expert[..., 2 * width :].reshape(*split, nd, d_local, own_count, units)
        grad_up = jnp.transpose(grad_up, (3, 1, 5, 4, 2, 0, 6))
        grad_low = jnp.transpose(grad_low, (3, 1, 4, 2, 0, 5))
        grad_expert_in = grad_up.reshape(d_local, local_count, 2 * FF).astype(F32)
        grad_expert_out = grad_low.reshape(d_local, local_count, FF).astype(F32)

    gate_grads = back_sub[:, D : D + EXPERTS] * kept
    logit_grads = (
        gates * (gate_grads - jnp.sum(gates * gate_grads, axis=1, keepdims=True))
    ).astype(BF)
    grad_norm_two = back_sub[:, :D] + dot(logit_grads, router_w, ((1,), (1,)))
    grad_middle, grad_gain_two = norm_backward(middle, gain_two_full, inverse_two, grad_norm_two)
    grad_middle = grad_middle + cot_sub.astype(F32)
    extra = jnp.zeros((sub, LANES - EXPERTS), BF)
    grad_attn = lax.all_gather(
        jnp.concatenate([grad_middle.astype(BF), logit_grads, extra], axis=1),
        "tensor",
        axis=0,
        tiled=True,
    )
    logit_grads_full = grad_attn[:, D : D + EXPERTS]
    grad_attn = grad_attn[:, :D]
    grad_router = dot(h_two_full, logit_grads_full, ((0,), (0,)))

    grad_output_w = dot(grad_attn, attended, ((0,), (0,)))
    grad_blended = (
        dot(grad_attn, output_w, ((1,), (0,)))
        .astype(BF)
        .reshape(n_rows, kv_heads, group, HEAD_DIM)
    )
    shares = jnp.exp(scores - log_totals)
    grad_shares = jnp.einsum(
        "bagd,pad->agbp", grad_blended, value_heads, preferred_element_type=F32
    )
    inner = jnp.sum(shares * grad_shares, axis=-1, keepdims=True)
    grad_scores = (shares * (grad_shares - inner)).astype(BF)
    grad_queries = score_scale * jnp.einsum(
        "agbp,pad->bagd", grad_scores, key_heads, preferred_element_type=F32
    )
    grad_keys = score_scale * jnp.einsum(
        "agbp,bagd->pad", grad_scores, queries, preferred_element_type=F32
    )
    grad_values = jnp.einsum(
        "agbp,bagd->pad", shares_low, grad_blended, preferred_element_type=F32
    )
    grad_kv = jnp.concatenate(
        [grad_keys.reshape(pack_len, kv_width), grad_values.reshape(pack_len, kv_width)], axis=1
    ).astype(BF)
    if kernels:
        grad_kv, _ = sum_blocks([grad_kv], jnp.zeros((8, LANES), F32), 1, 5)
        mixed, _ = lax.optimization_barrier((mixed, grad_kv))
        mixed_sub, grad_lower = reduce_rows([mixed], grad_lower, {0: 2, 1: 1, 2: 3}, nd, 4)
        grad_lower, grad_upper = lax.optimization_barrier((grad_lower, grad_upper))
        grad_lower = lax.all_gather(grad_lower, "ctx", axis=0)
        grad_expert_in, grad_expert_out = spread(grad_upper, grad_lower, own_count)
    else:
        grad_kv = lax.psum_scatter(grad_kv, "ctx", scatter_dimension=0, tiled=True).astype(F32)
    result = lax.all_to_all((middle + mixed_sub).astype(BF), "tensor", 1, 0, tiled=True)
    grad_turned = jnp.concatenate(
        [
            grad_queries.reshape(n_rows, q_heads, HEAD_DIM),
            grad_kv[:, :kv_width].reshape(n_rows, kv_heads, HEAD_DIM),
        ],
        axis=1,
    )
    grad_qkv = jnp.concatenate(
        [
            rotate(grad_turned, cosine_table, -sine_table)
            .astype(BF)
            .reshape(n_rows, q_width + kv_width),
            grad_kv[:, kv_width:].astype(BF),
        ],
        axis=1,
    )
    grad_norm_one = scatter_rows(dot(grad_qkv, qkv_w, ((1,), (1,))), tensor_at, nt)
    inverse_sub = lax.rsqrt(jnp.mean(tokens_sub * tokens_sub, axis=1, keepdims=True) + EPS)
    grad_tokens, grad_gain_one = norm_backward(
        tokens_sub, gain_one_full, inverse_sub, grad_norm_one
    )
    grad_tokens = lax.all_to_all(grad_tokens + grad_middle, "tensor", 1, 0, tiled=True)

    grad_qkv_w = dot(h_one, grad_qkv, ((0,), (0,)))
    gain_grads = jnp.stack([grad_gain_one, grad_gain_two])
    grad_router = jnp.pad(grad_router, ((0, 0), (0, LANES - EXPERTS)))
    weight_grads = [w.astype(BF) for w in (grad_qkv_w, grad_output_w, grad_router)]
    if kernels:
        gain_grads, _ = lax.optimization_barrier((gain_grads, mixed_sub))
        weight_grads, gain_grads = sum_blocks(weight_grads, gain_grads, nd, 6)
    else:
        weight_grads = lax.psum_scatter(
            jnp.concatenate(weight_grads, axis=1), ("dp", "ctx"), scatter_dimension=0, tiled=True
        )
        weight_grads = lax.all_gather(weight_grads, "ctx", axis=0, tiled=True).astype(F32)
        gain_grads = jnp.sum(lax.all_gather(gain_grads, ALL, axis=0), axis=0)
    edges = [0, q_width, q_width + kv_width, qkv_width, qkv_width + q_width]
    gain_grads = lax.dynamic_slice_in_dim(gain_grads, tensor_at * part_width, part_width, 1)
    return (
        result,
        grad_tokens,
        gain_grads[0],
        weight_grads[:, edges[0] : edges[1]],
        weight_grads[:, edges[1] : edges[2]],
        weight_grads[:, edges[2] : edges[3]],
        weight_grads[:, edges[3] : edges[4]],
        gain_grads[1],
        weight_grads[:, edges[4] : edges[4] + EXPERTS],
        grad_expert_in,
        grad_expert_out,
    )


def solution(mesh):
    return jax.shard_map(
        on_device,
        mesh=mesh,
        in_specs=(
            P(("dp", "ctx"), "tensor"),
            P("dp", None),
            P("dp", None),
            P("dp", None),
            P("tensor"),
            P("dp", "tensor"),
            P("dp", "tensor"),
            P("dp", "tensor"),
            P("dp", "tensor"),
            P("tensor"),
            P("dp", None),
            P("dp", "tensor", None),
            P("dp", "tensor", None),
            P(("dp", "ctx"), "tensor"),
        ),
        out_specs=(
            P(("dp", "ctx"), "tensor"),
            P(("dp", "ctx"), "tensor"),
            P("tensor"),
            P("dp", "tensor"),
            P("dp", "tensor"),
            P("dp", "tensor"),
            P("dp", "tensor"),
            P("tensor"),
            P("dp", None),
            P("dp", "tensor", None),
            P("dp", "tensor", None),
        ),
        check_vma=False,
    )
```

```python
import functools

import jax
import jax.numpy as jnp
from jax import lax
from jax.experimental import pallas as pl
from jax.experimental.pallas import tpu as pltpu
from jax.sharding import PartitionSpec as P

D = 1536
HEAD_DIM = 64
EXPERTS = 40
TOP_K = 8
FF = 512
EPS = 1e-06
THETA = 10000.0
NEG = -1e30
LANES = 128
ALL = ("dp", "ctx", "tensor")
BF = jnp.bfloat16
F32 = jnp.float32
MESH = pl.DeviceIdType.MESH
COST = pl.CostEstimate(flops=0, bytes_accessed=250_000_000, transcendentals=0)


def place():
    ctx = lax.axis_index("ctx")
    return (lax.axis_index("dp"), ctx // 2, ctx % 2, lax.axis_index("tensor"))


def device(z, y, k, x):
    return {"dp": z, "ctx": y * 2 + k, "tensor": x}


def greet(partners):
    barrier = pltpu.get_barrier_semaphore()
    for partner in partners:
        pl.semaphore_signal(barrier, inc=1, device_id=partner, device_id_type=MESH)
    pl.semaphore_wait(barrier, len(partners))


def partners_of(nd, z, y, k, x):
    return [device((z + hop) % nd, y, k, x) for hop in range(1, nd)] + [
        device(z, y, k, 1 - x),
        device(z, 1 - y, k, x),
        device(z, y, 1 - k, x),
    ]


def gather_kernel(own_count, units, pairs, *refs):
    own_ref, weight_ref, pair_refs = (refs[0], refs[1], refs[2 : 2 + pairs])
    out_ref, moved_ref, paired_refs = (refs[2 + pairs], refs[3 + pairs], refs[4 + pairs : 4 + 2 * pairs])
    local_sem, send_sem, recv_sem, move_local_sem, move_send_sem, move_recv_sem, pair_sem, held = refs[
        4 + 2 * pairs :
    ]
    nd, width = (out_ref.shape[0], own_ref.shape[2])
    wide = out_ref.shape[-1] != width
    z, y, k, x = place()
    up, down = (device((z + 1) % nd, y, k, x), device((z + nd - 1) % nd, y, k, x))
    greet(partners_of(nd, z, y, k, x))
    moves, kept = ([], [])
    rows, parts = (weight_ref.shape[1], weight_ref.shape[2] // (nd * units))

    def move(hop):
        to_z, from_z = ((z + hop) % nd, (z + nd - hop) % nd)
        for part in range(parts):
            for e in range(own_count):
                columns = pl.ds((part * own_count + e) * units, units)
                start = pl.multiple_of((part * nd + to_z) * units, LANES)
                source = weight_ref.at[(y * 2 + k) * own_count + e, :, pl.ds(start, units)]
                target = moved_ref.at[pl.ds(pl.multiple_of(z * rows, 16), rows), columns]
                if hop == 0:
                    at = len(kept)
                    copy = pltpu.make_async_copy(source, held.at[at], move_local_sem.at[0, at])
                    copy.start()
                    put = pltpu.make_async_copy(held.at[at], target, move_local_sem.at[1, at])
                    kept.append((copy, put))
                    continue
                slot = len(moves)
                copy = pltpu.make_async_remote_copy(
                    src_ref=source,
                    dst_ref=target,
                    send_sem=move_send_sem.at[slot],
                    recv_sem=move_recv_sem.at[slot],
                    device_id=device(to_z, y, k, x),
                    device_id_type=MESH,
                )
                copy.start()
                arrival = moved_ref.at[pl.ds(pl.multiple_of(from_z * rows, 16), rows), columns]
                moves.append((copy, arrival, slot))

    swaps = []
    for at_pair, (ref, full_ref) in enumerate(zip(pair_refs, paired_refs)):
        span = ref.shape[-1]
        mine = full_ref.at[:, pl.ds(pl.multiple_of(x * span, LANES), span)]
        copy = pltpu.make_async_remote_copy(
            src_ref=ref,
            dst_ref=mine,
            send_sem=pair_sem.at[0, at_pair],
            recv_sem=pair_sem.at[1, at_pair],
            device_id=device(z, y, k, 1 - x),
            device_id_type=MESH,
        )
        copy.start()
        swaps.append(copy)
        copy = pltpu.make_async_copy(ref, mine, pair_sem.at[2, at_pair])
        copy.start()
        swaps.append(copy)
    low = jnp.minimum(z, nd - 1 - z)
    places = []
    for step in range(nd):
        near = (step + 1) // 2
        zigzag = low + near if step % 2 else low - near
        from_low = jnp.where(step <= 2 * low, zigzag, step)
        places.append(jnp.where(2 * z < nd, from_low, nd - 1 - from_low))
    sends = []

    def at(piece):
        step, dy, dk, dx, half = piece
        chip, core, side = ((y + dy) % 2, (k + dk) % 2, (x + dx) % 2)
        if not wide:
            return out_ref.at[places[step], chip, core, side, half]
        columns = pl.ds(pl.multiple_of(side * width, LANES), width)
        return out_ref.at[places[step], chip, core, half, :, columns]

    def slot(piece):
        step, dy, dk, dx, half = piece
        return (((places[step] * 2 + dy) * 2 + dk) * 2 + dx) * 2 + half

    def send(piece, link, condition=None):
        step, dy, dk, dx, half = piece
        if link == "up":
            target, there = (up, piece)
        elif link == "down":
            target, there = (down, piece)
        elif link == "x":
            target, there = (device(z, y, k, 1 - x), (step, dy, dk, 1 - dx, half))
        elif link == "y":
            target, there = (device(z, 1 - y, k, x), (step, 1 - dy, dk, dx, half))
        else:
            target, there = (device(z, y, 1 - k, x), (step, dy, 1 - dk, dx, half))
        own = piece[:4] == (0, 0, 0, 0)
        copy = pltpu.make_async_remote_copy(
            src_ref=own_ref.at[half] if own else at(piece),
            dst_ref=at(piece),
            send_sem=send_sem.at[len(sends)],
            recv_sem=recv_sem.at[slot(there)],
            device_id=target,
            device_id_type=MESH,
        )
        if condition is None:
            copy.start()
        else:
            pl.when(condition)(copy.start)
        sends.append((copy, condition))

    def arrived(piece):
        pltpu.make_async_remote_copy(
            src_ref=at(piece),
            dst_ref=at(piece),
            send_sem=send_sem.at[0],
            recv_sem=recv_sem.at[slot(piece)],
            device_id=device(z, y, k, 1 - x),
            device_id_type=MESH,
        ).wait_recv()

    own_copies = []
    for half in range(2):
        own_copy = pltpu.make_async_copy(
            own_ref.at[half], at((0, 0, 0, 0, half)), local_sem.at[half]
        )
        own_copy.start()
        own_copies.append(own_copy)
    links = (("x", "y"), ("y", "x"))
    for step in range(nd + 2):
        if step < nd:
            came = places[step]
            for half in range(2):
                piece = (step, 0, 0, 0, half)
                if step:
                    arrived(piece)
                send(piece, "up", (came <= z) & (z < nd - 1))
                send(piece, "down", (came >= z) & (z > 0))
                send(piece, links[half][0])
            for half in range(2):
                piece = (step, 0, 0, 0, half)
                send(piece, links[half][1])
                send(piece, "k")
            if step == 0:
                move(0)
            if step == 1:
                for copy, put in kept:
                    copy.wait()
                    put.start()
            if step == nd - 2:
                for hop in [2, 1, 3] if nd == 4 else range(1, nd):
                    move(hop)
        if 1 <= step < nd + 1:
            for half in range(2):
                piece = (step - 1, half, 0, 1 - half, half)
                arrived(piece)
                send(piece, links[half][1])
                send(piece, "k")
        if 2 <= step:
            for half in range(2):
                for d in range(2):
                    piece = (step - 2, 1, 0, d, 0) if half == 0 else (step - 2, d, 0, 1, 1)
                    arrived(piece)
                    send(piece, "k")
    for step in range(nd):
        for dy in range(2):
            for dx in range(2):
                for half in range(2):
                    arrived((step, dy, 1, dx, half))
    for own_copy in own_copies + [put for _, put in kept]:
        own_copy.wait()
    for copy in swaps:
        copy.wait()
    for copy, arrival, slot in moves:
        pltpu.make_async_remote_copy(
            src_ref=arrival,
            dst_ref=arrival,
            send_sem=move_send_sem.at[slot],
            recv_sem=move_recv_sem.at[slot],
            device_id=device(z, y, k, 1 - x),
            device_id_type=MESH,
        ).wait_recv()
        copy.wait_send()
    for copy, condition in sends:
        if condition is None:
            copy.wait_send()
        else:
            pl.when(condition)(copy.wait_send)


def gather_rows(own, weight, units, own_count, nd, collective_id, pairs=(), wide=False):
    rows, width = own.shape
    half = rows // 2
    shape = (nd, 2, 2, 2, half, 2 * width) if wide else (nd, 2, 2, 2, 2, half, width)
    depth, moved = (nd * weight.shape[1], own_count * weight.shape[2] // nd)
    count = moved // units
    vmem, anywhere = (pl.BlockSpec(memory_space=pltpu.VMEM), pl.BlockSpec(memory_space=pl.ANY))
    out = pl.pallas_call(
        functools.partial(gather_kernel, own_count, units, len(pairs)),
        in_specs=[vmem, anywhere] + [vmem] * len(pairs),
        out_specs=[anywhere] * (2 + len(pairs)),
        out_shape=[
            jax.ShapeDtypeStruct(shape, own.dtype),
            jax.ShapeDtypeStruct((depth, moved), weight.dtype),
        ]
        + [jax.ShapeDtypeStruct((p.shape[0], 2 * p.shape[1]), p.dtype) for p in pairs],
        scratch_shapes=[
            pltpu.SemaphoreType.DMA((2,)),
            pltpu.SemaphoreType.DMA((nd * 18,)),
            pltpu.SemaphoreType.DMA((nd * 16,)),
            pltpu.SemaphoreType.DMA((2, count)),
            pltpu.SemaphoreType.DMA(((nd - 1) * count,)),
            pltpu.SemaphoreType.DMA(((nd - 1) * count,)),
            pltpu.SemaphoreType.DMA((3, max(len(pairs), 1))),
            pltpu.VMEM((count, weight.shape[1], units), weight.dtype),
        ],
        compiler_params=pltpu.CompilerParams(collective_id=collective_id, has_side_effects=True),
        cost_estimate=COST,
        name="gather_rows",
    )(own.reshape(2, half, width), weight, *pairs)
    return (out[0].reshape(-1, shape[-1]), *out[1:])


def ctx_kernel(own_ref, out_ref, local_sem, send_sem, recv_sem):
    z, y, k, x = place()
    y_partner, core = (device(z, 1 - y, k, x), device(z, y, 1 - k, x))
    greet([y_partner, core])
    kept = pltpu.make_async_copy(own_ref, out_ref.at[y, k], local_sem)
    kept.start()
    copies = []
    for at, (source, chip, target) in enumerate(
        ((own_ref, y, y_partner), (own_ref, y, core), (out_ref.at[1 - y, k], 1 - y, core))
    ):
        if at == 2:
            copies[0].wait_recv()
        copy = pltpu.make_async_remote_copy(
            src_ref=source,
            dst_ref=out_ref.at[chip, k],
            send_sem=send_sem.at[at],
            recv_sem=recv_sem.at[at],
            device_id=target,
            device_id_type=MESH,
        )
        copy.start()
        copies.append(copy)
    kept.wait()
    for copy in copies[1:]:
        copy.wait_recv()
    for copy in copies:
        copy.wait_send()


def gather_ctx(own, collective_id):
    out = pl.pallas_call(
        ctx_kernel,
        in_specs=[pl.BlockSpec(memory_space=pltpu.VMEM)],
        out_specs=pl.BlockSpec(memory_space=pl.ANY),
        out_shape=jax.ShapeDtypeStruct((2, 2, *own.shape), own.dtype),
        scratch_shapes=[
            pltpu.SemaphoreType.DMA,
            pltpu.SemaphoreType.DMA((3,)),
            pltpu.SemaphoreType.DMA((3,)),
        ],
        compiler_params=pltpu.CompilerParams(collective_id=collective_id, has_side_effects=True),
        name="gather_ctx",
    )(own)
    return out.reshape(-1, own.shape[1])


def reduce_kernel(count, when, *refs):
    parts, moved_ref, out_ref, arrived_ref = (refs[:count], *refs[count : count + 3])
    own, from_core, first, second, across, load_sem, send_sem, recv_sem = refs[count + 3 : -4]
    move_local_sem, move_send_sem, move_recv_sem, held = refs[-4:]
    nd = parts[0].shape[0]
    z, y, k, x = place()
    greet(partners_of(nd, z, y, k, x))
    order = [hop for hop in (2, 1, 3, 0)] if nd == 4 else list(range(1, nd)) + [0]
    sends, loads = ([], [])

    def spot(step, dy, dx, half):
        return ((step * 2 + dy) * 2 + dx) * 2 + half

    def send(source, there, target, slot):
        copy = pltpu.make_async_remote_copy(
            src_ref=source,
            dst_ref=there,
            send_sem=send_sem.at[len(sends)],
            recv_sem=recv_sem.at[slot],
            device_id=target,
            device_id_type=MESH,
        )
        copy.start()
        sends.append(copy)

    def arrived(there, slot):
        pltpu.make_async_remote_copy(
            src_ref=there,
            dst_ref=there,
            send_sem=send_sem.at[0],
            recv_sem=recv_sem.at[slot],
            device_id=device(z, y, k, 1 - x),
            device_id_type=MESH,
        ).wait_recv()

    def add(to, what, index):
        to_rows = own.shape[1]

        def body(i, carry):
            rows = pl.ds(i * 16, 16)
            total = own[to, rows, :].astype(F32) + what[index, rows, :].astype(F32)
            own[to, rows, :] = total.astype(BF)
            return carry

        lax.fori_loop(0, to_rows // 16, body, 0)

    spans, start = ([], 0)
    for ref in parts:
        spans.append(pl.ds(start, ref.shape[-1]))
        start += ref.shape[-1]
    first_slot, second_slot, across_slot, core_slot = (0, nd * 4, nd * 6, nd * 7)
    for step, dz in enumerate(order):
        for dy in range(2):
            for dx in range(2):
                there = pl.ds(spot(step, dy, dx, 0), 2)
                block = ((z + dz) % nd, (y + dy) % 2)
                for ref, span in zip(parts, spans):
                    send(
                        ref.at[block[0], block[1], 1 - k, (x + dx) % 2],
                        from_core.at[there, :, span],
                        device(z, y, 1 - k, x),
                        core_slot + len(loads),
                    )
                    load = pltpu.make_async_copy(
                        ref.at[block[0], block[1], k, (x + dx) % 2],
                        own.at[there, :, span],
                        load_sem.at[len(loads)],
                    )
                    load.start()
                    loads.append(load)
    x_partner, y_partner = (device(z, y, k, 1 - x), device(z, 1 - y, k, x))
    taken = pltpu.make_async_copy(moved_ref.at[z], held, move_local_sem.at[0])
    taken.start()
    kept = pltpu.make_async_copy(held, arrived_ref.at[z], move_local_sem.at[1])
    moves = []

    def move(hop):
        to_z = (z + hop) % nd
        copy = pltpu.make_async_remote_copy(
            src_ref=moved_ref.at[to_z],
            dst_ref=arrived_ref.at[z],
            send_sem=move_send_sem.at[hop - 1],
            recv_sem=move_recv_sem.at[hop - 1],
            device_id=device(to_z, y, k, x),
            device_id_type=MESH,
        )
        copy.start()
        moves.append((copy, hop))

    for step in range(nd + 2):
        if step == 0 and step in when:
            move(when[step])
        if step == 1:
            taken.wait()
            kept.start()
        if step < nd:
            for at in range(4):
                base = spot(step, 0, 0, 0) + at * 2
                for which, span in enumerate(spans):
                    slot = (step * 4 + at) * count + which
                    loads[slot].wait()
                    arrived(from_core.at[pl.ds(base, 2), :, span], core_slot + slot)

            def pair(i, carry, step=step):
                add(step * 8 + i, from_core, step * 8 + i)
                return carry

            lax.fori_loop(0, 8, pair, 0)
            for d in range(2):
                slot = step * 4 + d
                send(own.at[spot(step, 1, d, 0)], first.at[slot], y_partner, first_slot + slot)
                slot = step * 4 + 2 + d
                send(own.at[spot(step, d, 1, 1)], first.at[slot], x_partner, first_slot + slot)
        if 1 <= step < nd + 1:
            now = step - 1
            for d in (1, 0):
                slot = now * 4 + d
                arrived(first.at[slot], first_slot + slot)
                add(spot(now, 0, d, 0), first, slot)
                slot = now * 4 + 2 + d
                arrived(first.at[slot], first_slot + slot)
                add(spot(now, d, 0, 1), first, slot)
                if d == 1:
                    slot = now * 2
                    send(own.at[spot(now, 0, 1, 0)], second.at[slot], x_partner, second_slot + slot)
                    slot = now * 2 + 1
                    send(own.at[spot(now, 1, 0, 1)], second.at[slot], y_partner, second_slot + slot)
        if 2 <= step:
            now = step - 2
            for half in range(2):
                slot = now * 2 + half
                arrived(second.at[slot], second_slot + slot)
                add(spot(now, 0, 0, half), second, slot)
            hop = order[now]
            if hop:
                slot = nd - hop - 1
                send(
                    own.at[pl.ds(spot(now, 0, 0, 0), 2)],
                    across.at[slot],
                    device((z + hop) % nd, y, k, x),
                    across_slot + slot,
                )
        if step and step in when:
            move(when[step])
    for slot in range(nd - 1):
        arrived(across.at[slot], across_slot + slot)
    mine = spot(order.index(0), 0, 0, 0)
    for half in range(2):

        def total(i, carry, half=half):
            rows = pl.ds(i * 16, 16)
            value = own[mine + half, rows, :].astype(F32)
            for slot in range(nd - 1):
                value = value + across[slot, half, rows, :].astype(F32)
            out_ref[half, rows, :] = value
            return carry

        lax.fori_loop(0, own.shape[1] // 16, total, 0)
    kept.wait()
    for copy, hop in moves:
        there = arrived_ref.at[(z + nd - hop) % nd]
        pltpu.make_async_remote_copy(
            src_ref=there,
            dst_ref=there,
            send_sem=move_send_sem.at[hop - 1],
            recv_sem=move_recv_sem.at[hop - 1],
            device_id=x_partner,
            device_id_type=MESH,
        ).wait_recv()
        copy.wait_send()
    for copy in sends:
        copy.wait_send()


def reduce_rows(parts, moved, when, nd, collective_id):
    moved = moved.reshape(nd, moved.shape[0] // nd, moved.shape[1])
    rows = parts[0].shape[0] // (nd * 8)
    width = sum(part.shape[1] for part in parts)
    half, count = (rows // 2, len(parts))
    sends = nd * (4 * count + 7)
    out = pl.pallas_call(
        functools.partial(reduce_kernel, count, when),
        in_specs=[pl.BlockSpec(memory_space=pl.ANY)] * (count + 1),
        out_specs=[pl.BlockSpec(memory_space=pltpu.VMEM), pl.BlockSpec(memory_space=pl.ANY)],
        out_shape=[
            jax.ShapeDtypeStruct((2, half, width), F32),
            jax.ShapeDtypeStruct(moved.shape, moved.dtype),
        ],
        scratch_shapes=[
            pltpu.VMEM((nd * 8, half, width), BF),
            pltpu.VMEM((nd * 8, half, width), BF),
            pltpu.VMEM((nd * 4, half, width), BF),
            pltpu.VMEM((nd * 2, half, width), BF),
            pltpu.VMEM((nd - 1, 2, half, width), BF),
            pltpu.SemaphoreType.DMA((nd * 4 * count,)),
            pltpu.SemaphoreType.DMA((sends,)),
            pltpu.SemaphoreType.DMA((sends,)),
            pltpu.SemaphoreType.DMA((2,)),
            pltpu.SemaphoreType.DMA((nd - 1,)),
            pltpu.SemaphoreType.DMA((nd - 1,)),
            pltpu.VMEM(moved.shape[1:], moved.dtype),
        ],
        compiler_params=pltpu.CompilerParams(
            collective_id=collective_id, has_side_effects=True, vmem_limit_bytes=48 << 20
        ),
        cost_estimate=COST,
        name="reduce_rows",
    )(*[part.reshape(nd, 2, 2, 2, 2, half, part.shape[1]) for part in parts], moved)
    return (out[0].reshape(rows, width), out[1])


def sum_kernel(across_dp, count, *refs):
    parts, gain_ref, out_ref, total_ref = (refs[:count], *refs[count : count + 3])
    own, from_core, from_chip, across, result, gains, load_sem, send_sem, recv_sem, gain_sems = refs[
        count + 3 :
    ]
    spans, start = ([], 0)
    for ref in parts:
        spans.append(pl.ds(start, ref.shape[-1]))
        start += ref.shape[-1]
    nd = parts[0].shape[0]
    z, y, k, x = place()
    y_partner, core = (device(z, 1 - y, k, x), device(z, y, 1 - k, x))
    x_partner = device(z, y, k, 1 - x)
    greet([device((z + hop) % nd, y, k, x) for hop in range(1, nd)] + [x_partner, y_partner, core])
    gain_sends = []

    def gain_copy(slot, target):
        copy = pltpu.make_async_remote_copy(
            src_ref=gains.at[0, slot],
            dst_ref=gains.at[1, slot],
            send_sem=gain_sems.at[0, slot],
            recv_sem=gain_sems.at[1, slot],
            device_id=target,
            device_id_type=MESH,
        )
        copy.start()
        gain_sends.append(copy)

    gains[0, 0] = gain_ref[...]
    gain_copy(0, core)
    order = ([2, 1, 3] if nd == 4 else list(range(1, nd))) + [0]
    sends, loads = ([], [])
    chip_slot, across_slot, result_slot, core_slot = (0, nd, nd * 2, nd * 2 + 3)

    def send(source, there, target, slot):
        copy = pltpu.make_async_remote_copy(
            src_ref=source,
            dst_ref=there,
            send_sem=send_sem.at[len(sends)],
            recv_sem=recv_sem.at[slot],
            device_id=target,
            device_id_type=MESH,
        )
        copy.start()
        sends.append(copy)

    def arrived(there, slot):
        pltpu.make_async_remote_copy(
            src_ref=there,
            dst_ref=there,
            send_sem=send_sem.at[0],
            recv_sem=recv_sem.at[slot],
            device_id=core,
            device_id_type=MESH,
        ).wait_recv()

    def add(to, what, index):
        def body(i, carry):
            rows = pl.ds(i * 16, 16)
            total = own[to, rows, :].astype(F32) + what[index, rows, :].astype(F32)
            own[to, rows, :] = total.astype(BF)
            return carry

        lax.fori_loop(0, own.shape[1] // 16, body, 0)

    for step, dz in enumerate(order):
        for dy in (1, 0):
            at = step * 2 + dy
            for ref, span in zip(parts, spans):
                block = ref.at[(z + dz) % nd, (y + dy) % 2]
                send(block.at[1 - k], from_core.at[at, :, span], core, core_slot + len(loads))
                load = pltpu.make_async_copy(
                    block.at[k], own.at[at, :, span], load_sem.at[len(loads)]
                )
                load.start()
                loads.append(load)
    stages = [y_partner, x_partner]
    if nd > 1:
        stages += [device(z + 1 - z % 2 * 2, y, k, x), device((z + 2) % nd, y, k, x)]
    for slot, target in enumerate(stages + [None], 1):
        gain_sends[-1].wait_recv()
        gains[0, slot] = gains[0, slot - 1] + gains[1, slot - 1]
        if target is not None:
            gain_copy(slot, target)
    total_ref[...] = gains[0, len(stages) + 1]
    for step in range(nd + 1):
        if step < nd:
            for dy in (1, 0):
                at = step * 2 + dy
                for which, span in enumerate(spans):
                    slot = (step * 2 + 1 - dy) * count + which
                    loads[slot].wait()
                    arrived(from_core.at[at, :, span], core_slot + slot)
                add(at, from_core, at)
                if dy:
                    send(own.at[at], from_chip.at[step], y_partner, chip_slot + step)
        if step:
            now = step - 1
            arrived(from_chip.at[now], chip_slot + now)
            hop = order[now]
            if hop or across_dp:
                add(now * 2, from_chip, now)
            if hop:
                slot = nd - hop - 1
                target = device((z + hop) % nd, y, k, x)
                send(own.at[now * 2], across.at[slot], target, across_slot + slot)
    for slot in range(nd - 1):
        arrived(across.at[slot], across_slot + slot)
    mine = (nd - 1) * 2

    def total(i, carry):
        rows = pl.ds(i * 16, 16)
        value = own[mine, rows, :].astype(F32)
        if across_dp:
            for slot in range(nd - 1):
                value = value + across[slot, rows, :].astype(F32)
            result[y, k, rows, :] = value.astype(BF)
        else:
            out_ref[rows, :] = value + from_chip[0, rows, :].astype(F32)
        return carry

    lax.fori_loop(0, own.shape[1] // 16, total, 0)
    if across_dp:
        send(result.at[y, k], result.at[y, k], y_partner, result_slot)
        send(result.at[y, k], result.at[y, k], core, result_slot + 1)
        arrived(result.at[1 - y, k], result_slot)
        send(result.at[1 - y, k], result.at[1 - y, k], core, result_slot + 2)
        arrived(result.at[y, 1 - k], result_slot + 1)
        arrived(result.at[1 - y, 1 - k], result_slot + 2)

        def widen(i, carry):
            rows = pl.ds(i * 16, 16)
            for chip in range(2):
                for side in range(2):
                    out_ref[chip, side, rows, :] = result[chip, side, rows, :].astype(F32)
            return carry

        lax.fori_loop(0, own.shape[1] // 16, widen, 0)
    for copy in gain_sends:
        copy.wait_send()
    for copy in sends:
        copy.wait_send()


def sum_blocks(parts, gain, nd, collective_id):
    rows, width = (parts[0].shape[0] // (nd * 4), sum(part.shape[1] for part in parts))
    count = len(parts)
    sends = nd * (2 * count + 2) + 3
    shape = (2, 2, rows, width) if nd > 1 else (rows, width)
    out = pl.pallas_call(
        functools.partial(sum_kernel, nd > 1, count),
        in_specs=[pl.BlockSpec(memory_space=pl.ANY)] * count
        + [pl.BlockSpec(memory_space=pltpu.VMEM)],
        out_specs=[pl.BlockSpec(memory_space=pltpu.VMEM)] * 2,
        out_shape=[jax.ShapeDtypeStruct(shape, F32), jax.ShapeDtypeStruct(gain.shape, F32)],
        scratch_shapes=[
            pltpu.VMEM((nd * 2, rows, width), BF),
            pltpu.VMEM((nd * 2, rows, width), BF),
            pltpu.VMEM((nd, rows, width), BF),
            pltpu.VMEM((max(nd - 1, 1), rows, width), BF),
            pltpu.VMEM((2, 2, rows, width) if nd > 1 else (1, 1, 16, LANES), BF),
            pltpu.VMEM((2, 6, *gain.shape), F32),
            pltpu.SemaphoreType.DMA((nd * 2 * count,)),
            pltpu.SemaphoreType.DMA((sends,)),
            pltpu.SemaphoreType.DMA((sends,)),
            pltpu.SemaphoreType.DMA((2, 5)),
        ],
        compiler_params=pltpu.CompilerParams(
            collective_id=collective_id, has_side_effects=True, vmem_limit_bytes=48 << 20
        ),
        cost_estimate=COST,
        name="sum_blocks",
    )(*[part.reshape(nd, 2, 2, rows, part.shape[1]) for part in parts], gain)
    return (out[0].reshape(-1, width), out[1])


def spread_kernel(up_ref, low_ref, in_ref, out_ref):
    nc, nd = up_ref.shape[:2]
    own_count = in_ref.shape[0] // nc
    units = low_ref.shape[3] // own_count
    for c in range(nc):
        for e in range(own_count):
            for part in range(3):
                got_ref, to_ref, base = ((up_ref, in_ref, part) if part < 2 else (low_ref, out_ref, 0))
                start = (base * own_count + e) * units
                for at in range(nd):
                    columns = slice((base * nd + at) * units, (base * nd + at + 1) * units)
                    to_ref[c * own_count + e, :, columns] = got_ref[
                        c, at, :, start : start + units
                    ].astype(F32)


def spread(up, low, own_count):
    nc, nd, d_local, low_width = low.shape
    experts, units = (nc * own_count, low_width // own_count)
    block = 32
    into, out = pl.pallas_call(
        spread_kernel,
        grid=(d_local // block,),
        in_specs=[
            pl.BlockSpec((nc, nd, block, ref.shape[3]), lambda i: (0, 0, i, 0)) for ref in (up, low)
        ],
        out_specs=[
            pl.BlockSpec((experts, block, parts * nd * units), lambda i: (0, i, 0))
            for parts in (2, 1)
        ],
        out_shape=[
            jax.ShapeDtypeStruct((experts, d_local, parts * nd * units), F32) for parts in (2, 1)
        ],
        name="spread",
    )(up, low)
    return (jnp.transpose(into, (1, 0, 2)), jnp.transpose(out, (1, 0, 2)))


def rope_tables(position):
    halves = HEAD_DIM // 2
    frequency = THETA ** (-2.0 * jnp.arange(halves, dtype=F32) / HEAD_DIM)
    angles = position[:, None] * frequency[None, :]
    return (jnp.cos(angles)[:, None, :], jnp.sin(angles)[:, None, :])


def rotate(values, cosine_table, sine_table):
    halves = values.shape[-1] // 2
    first_half, second_half = (values[..., :halves], values[..., halves:])
    return jnp.concatenate(
        [
            first_half * cosine_table - second_half * sine_table,
            second_half * cosine_table + first_half * sine_table,
        ],
        axis=-1,
    )


def dot(a, b, dims):
    return lax.dot_general(a, b, (dims, ((), ())), preferred_element_type=F32)


def norm_forward(rows, gain):
    inverse = lax.rsqrt(jnp.mean(rows * rows, axis=1, keepdims=True) + EPS)
    return (inverse, (rows * inverse * gain[None, :]).astype(BF))


def norm_backward(rows, gain, inverse, grad_normed):
    weighted = grad_normed * gain[None, :]
    inner = jnp.sum(weighted * rows, axis=1, keepdims=True)
    grad_rows = weighted * inverse - rows * (inverse * inverse * inverse * inner / D)
    return (grad_rows, jnp.sum(grad_normed * rows * inverse, axis=0))


def exchange(parts, at, count):
    result = lax.dynamic_update_index_in_dim(
        jnp.zeros_like(parts), lax.dynamic_index_in_dim(parts, at, 0), at, 0
    )
    for hop in range(1, count):
        sent = lax.dynamic_index_in_dim(parts, (at + hop) % count, 0)
        got = lax.ppermute(sent, "dp", [(i, (i + hop) % count) for i in range(count)])
        result = lax.dynamic_update_index_in_dim(result, got, (at - hop) % count, 0)
    return result


def scatter_rows(partial, at, count):
    if count != 2:
        return lax.psum_scatter(
            partial.astype(BF), "tensor", scatter_dimension=0, tiled=True
        ).astype(F32)
    half = partial.shape[0] // 2
    sent = lax.dynamic_slice_in_dim(partial, (1 - at) * half, half, 0).astype(BF)
    got = lax.ppermute(sent, "tensor", [(0, 1), (1, 0)])
    return lax.dynamic_slice_in_dim(partial, at * half, half, 0) + got.astype(F32)


def on_device(
    tokens,
    segments,
    order,
    routes,
    gain_one,
    w_query,
    w_key,
    w_value,
    w_output,
    gain_two,
    w_router,
    w_expert_in,
    w_expert_out,
    cotangent,
):
    nd, nc, nt = (lax.axis_size("dp"), lax.axis_size("ctx"), lax.axis_size("tensor"))
    dp_at, ctx_at, tensor_at = (
        lax.axis_index("dp"),
        lax.axis_index("ctx"),
        lax.axis_index("tensor"),
    )
    n_rows, part_width = tokens.shape
    sub = n_rows // nt
    pack_len = order.shape[1]
    d_local = w_query.shape[0]
    q_width, kv_width = (w_query.shape[1], w_key.shape[1])
    q_heads, kv_heads = (q_width // HEAD_DIM, kv_width // HEAD_DIM)
    group = q_heads // kv_heads
    qkv_width = q_width + 2 * kv_width
    local_count = w_expert_in.shape[1]
    capacity = n_rows * 3 // 8

    packed = jnp.concatenate([w_query, w_key, w_value, w_router], axis=1)
    share = d_local // nc
    packed = lax.dynamic_slice_in_dim(packed, ctx_at * share, share, 0)
    packed = lax.all_gather(packed, ("dp", "ctx"), axis=0, tiled=True)
    qkv_w, router_w = (packed[:, :qkv_width], packed[:, qkv_width:])
    output_w = lax.all_gather(
        lax.dynamic_slice_in_dim(w_output, ctx_at * share, share, 0),
        ("dp", "ctx"),
        axis=0,
        tiled=True,
    )
    kernels = (nd, nc, nt) == (4, 4, 2)
    by_expert = local_count % nc == 0
    own_count = local_count // nc if by_expert else local_count
    units = FF // nd if by_expert else FF // (nd * nc)
    width = own_count * units
    gains = jnp.stack([gain_one, gain_two])
    if kernels:
        w_expert_in, w_expert_out = [jnp.transpose(w, (1, 0, 2)) for w in (w_expert_in, w_expert_out)]
        cot_all, lower_w, tokens_full, gains = gather_rows(
            cotangent, w_expert_out, units, own_count, nd, 1, (tokens, gains), wide=True
        )
        cot_sub = lax.dynamic_slice_in_dim(
            cot_all, (dp_at * nc + ctx_at) * n_rows + tensor_at * sub, sub, 0
        )
    else:
        tokens_full = lax.all_gather(tokens, "tensor", axis=1, tiled=True)
        gains = lax.all_gather(gains, "tensor", axis=1, tiled=True)
        cot_sub = lax.all_to_all(cotangent, "tensor", 0, 1, tiled=True)
        cot_all = lax.all_gather(cot_sub, ALL, axis=0, tiled=True)
    gain_one_full, gain_two_full = (gains[0], gains[1])
    tokens_sub = lax.dynamic_slice_in_dim(tokens_full, tensor_at * sub, sub, 0).astype(F32)

    first_expert = tensor_at * local_count + (ctx_at * own_count if by_expert else 0)
    if not kernels:
        if by_expert:
            own_in = lax.dynamic_slice_in_dim(w_expert_in, ctx_at * own_count, own_count, 1)
            own_out = lax.dynamic_slice_in_dim(w_expert_out, ctx_at * own_count, own_count, 1)
            own_in = own_in.reshape(d_local, own_count, 2, nd, units)
            own_out = own_out.reshape(d_local, own_count, nd, units)
        else:
            own_in = w_expert_in.reshape(d_local, own_count, 2, nd, nc, units)
            own_out = w_expert_out.reshape(d_local, own_count, nd, nc, units)
            own_in = lax.dynamic_index_in_dim(own_in, ctx_at, 4, False)
            own_out = lax.dynamic_index_in_dim(own_out, ctx_at, 3, False)
        own_in = jnp.transpose(own_in, (3, 0, 2, 1, 4)).reshape(nd, d_local, 2 * width)
        own_out = jnp.transpose(own_out, (2, 0, 1, 3)).reshape(nd, d_local, width)
        expert_w = exchange(jnp.concatenate([own_in, own_out], axis=2), dp_at, nd)
        expert_w = expert_w.reshape(D, 3 * width)
        upper_w, lower_w = (expert_w[:, : 2 * width], expert_w[:, 2 * width :])

    order_row = order[0]
    places = jnp.arange(pack_len, dtype=jnp.int32)
    dealt = jnp.sum(jnp.where(order_row[:, None] == places[None, :], places[:, None], 0), axis=0)
    sub_start = ctx_at * n_rows + tensor_at * sub
    dealt_sub = lax.dynamic_slice_in_dim(dealt, sub_start, sub)
    experts_all = jnp.arange(EXPERTS, dtype=jnp.int32)
    uses = jnp.any(routes[:, :, None] == experts_all[None, None, :], axis=1)
    earlier = (dealt_sub[:, None] // n_rows == dealt[None, :] // n_rows) & (
        dealt[None, :] < dealt_sub[:, None]
    )
    ranks = dot(earlier.astype(BF), uses.astype(BF), ((1,), (0,)))
    uses_sub = lax.dynamic_slice_in_dim(uses, sub_start, sub, 0)
    kept = (uses_sub & (ranks < capacity)).astype(F32)

    segment_row = segments[0]
    local_segs = lax.dynamic_slice_in_dim(segment_row, ctx_at * n_rows, n_rows)
    local_places = ctx_at * n_rows + jnp.arange(n_rows, dtype=jnp.int32)
    starts = jnp.sum((segment_row[None, :] < local_segs[:, None]).astype(jnp.int32), axis=1)
    cosine_table, sine_table = rope_tables((local_places - starts).astype(F32))
    _, h_one = norm_forward(tokens_full.astype(F32), gain_one_full)
    if kernels:
        h_one, cot_all, cot_sub = lax.optimization_barrier((h_one, cot_all, cot_sub))
    projected = dot(h_one, qkv_w, ((1,), (0,)))
    turned = rotate(
        projected[:, : q_width + kv_width].reshape(n_rows, q_heads + kv_heads, HEAD_DIM),
        cosine_table,
        sine_table,
    ).astype(BF)
    queries = turned[:, :q_heads].reshape(n_rows, kv_heads, group, HEAD_DIM)
    kv_rows = jnp.concatenate(
        [
            turned[:, q_heads:].reshape(n_rows, kv_width),
            projected[:, q_width + kv_width :].astype(BF),
        ],
        axis=1,
    )
    if kernels:
        kv_all = gather_ctx(kv_rows, 7)
    else:
        kv_all = lax.all_gather(kv_rows, "ctx", axis=0, tiled=True)
    key_heads = kv_all[:, :kv_width].reshape(pack_len, kv_heads, HEAD_DIM)
    value_heads = kv_all[:, kv_width:].reshape(pack_len, kv_heads, HEAD_DIM)
    allowed = (local_segs[:, None] == segment_row[None, :]) & (
        local_places[:, None] >= places[None, :]
    )
    score_scale = HEAD_DIM ** (-0.5)
    scores = score_scale * jnp.einsum(
        "bagd,pad->agbp", queries, key_heads, preferred_element_type=F32
    )
    scores = jnp.where(allowed[None, None], scores, NEG)
    highest = jnp.max(scores, axis=-1, keepdims=True)
    weights = jnp.exp(scores - highest)
    totals = jnp.sum(weights, axis=-1, keepdims=True)
    shares_low = (weights / totals).astype(BF)
    log_totals = highest + jnp.log(totals)
    attended = (
        jnp.einsum("agbp,pad->bagd", shares_low, value_heads, preferred_element_type=F32)
        .astype(BF)
        .reshape(n_rows, q_width)
    )
    middle = tokens_sub + scatter_rows(dot(attended, output_w, ((1,), (1,))), tensor_at, nt)

    inverse_two, h_two = norm_forward(middle, gain_two_full)
    logits = jnp.where(uses_sub, dot(h_two, router_w, ((1,), (0,))), NEG)
    raised = jnp.exp(logits - jnp.max(logits, axis=1, keepdims=True))
    gates = raised / jnp.sum(raised, axis=1, keepdims=True)
    gates_kept = gates * kept
    gates_high = gates_kept.astype(BF)
    gates_low = (gates_kept - gates_high.astype(F32)).astype(BF)
    extra = jnp.zeros((sub, LANES - 2 * EXPERTS), BF)
    h_ext = jnp.concatenate([h_two, gates_high, gates_low, extra], axis=1)
    if kernels:
        h_all, upper_w = gather_rows(h_ext, w_expert_in, units, own_count, nd, 2)
    else:
        h_all = lax.all_gather(h_ext, ALL, axis=0, tiled=True)
    gates_all = (
        h_all[:, D : D + EXPERTS].astype(F32) + h_all[:, D + EXPERTS : D + 2 * EXPERTS].astype(F32)
    )
    total_rows = h_all.shape[0]
    gates_own = lax.dynamic_slice_in_dim(gates_all, first_expert, own_count, 1)
    h_two_full = lax.dynamic_slice(h_all, ((dp_at * nc + ctx_at) * n_rows, 0), (n_rows, D))
    h_all = h_all[:, :D]

    gate_wide = jnp.broadcast_to(gates_own[:, :, None], (total_rows, own_count, units)).reshape(
        total_rows, width
    )
    hidden = dot(h_all, upper_w, ((1,), (0,)))
    grad_raw = dot(cot_all, lower_w, ((1,), (0,)))
    gate_part, up_part = (hidden[:, :width], hidden[:, width:])
    sigmoid = jax.nn.sigmoid(gate_part)
    silu = gate_part * sigmoid
    active = (silu * up_part).astype(BF).astype(F32)
    active_gated = (active * gate_wide).astype(BF)
    grad_gates = jnp.sum((grad_raw * active).reshape(total_rows, own_count, units), axis=2)
    grad_active = grad_raw * gate_wide
    grad_hidden = jnp.concatenate(
        [
            grad_active * up_part * sigmoid * (1.0 + gate_part * (1.0 - sigmoid)),
            grad_active * silu,
        ],
        axis=1,
    ).astype(BF)
    grad_in = dot(grad_hidden, upper_w, ((1,), (1,))).astype(BF)
    grad_gates = lax.dynamic_update_slice_in_dim(
        jnp.zeros((total_rows, LANES), BF), grad_gates.astype(BF), first_expert, 1
    )
    mixed = dot(active_gated, lower_w, ((1,), (1,))).astype(BF)
    grad_upper = dot(h_all, grad_hidden, ((0,), (0,))).astype(BF)
    grad_lower = dot(cot_all, active_gated, ((0,), (0,))).astype(BF)
    if kernels:
        grad_in, grad_upper, grad_lower = lax.optimization_barrier((grad_in, grad_upper, grad_lower))
        back_sub, grad_upper = reduce_rows([grad_in, grad_gates], grad_upper, {0: 1, 4: 2, 5: 3}, nd, 3)
        grad_upper = lax.all_gather(grad_upper, "ctx", axis=0)
    else:
        back = jnp.concatenate([grad_in, grad_gates], axis=1)
        back_sub = lax.psum_scatter(back, ALL, scatter_dimension=0, tiled=True).astype(F32)
        mixed_sub = lax.psum_scatter(mixed, ALL, scatter_dimension=0, tiled=True).astype(F32)
        grad_expert = jnp.concatenate([grad_upper, grad_lower], axis=1)
        grad_expert = exchange(grad_expert.reshape(nd, d_local, 3 * width), dp_at, nd)
        grad_expert = lax.all_gather(grad_expert, "ctx", axis=0)
        split = (1, nc) if by_expert else (nc, 1)
        grad_up = grad_expert[..., : 2 * width].reshape(*split, nd, d_local, 2, own_count, units)
        grad_low = grad_expert[..., 2 * width :].reshape(*split, nd, d_local, own_count, units)
        grad_up = jnp.transpose(grad_up, (3, 1, 5, 4, 2, 0, 6))
        grad_low = jnp.transpose(grad_low, (3, 1, 4, 2, 0, 5))
        grad_expert_in = grad_up.reshape(d_local, local_count, 2 * FF).astype(F32)
        grad_expert_out = grad_low.reshape(d_local, local_count, FF).astype(F32)

    gate_grads = back_sub[:, D : D + EXPERTS] * kept
    logit_grads = (
        gates * (gate_grads - jnp.sum(gates * gate_grads, axis=1, keepdims=True))
    ).astype(BF)
    grad_norm_two = back_sub[:, :D] + dot(logit_grads, router_w, ((1,), (1,)))
    grad_middle, grad_gain_two = norm_backward(middle, gain_two_full, inverse_two, grad_norm_two)
    grad_middle = grad_middle + cot_sub.astype(F32)
    extra = jnp.zeros((sub, LANES - EXPERTS), BF)
    grad_attn = lax.all_gather(
        jnp.concatenate([grad_middle.astype(BF), logit_grads, extra], axis=1),
        "tensor",
        axis=0,
        tiled=True,
    )
    logit_grads_full = grad_attn[:, D : D + EXPERTS]
    grad_attn = grad_attn[:, :D]
    grad_router = dot(h_two_full, logit_grads_full, ((0,), (0,)))

    grad_output_w = dot(grad_attn, attended, ((0,), (0,)))
    grad_blended = (
        dot(grad_attn, output_w, ((1,), (0,)))
        .astype(BF)
        .reshape(n_rows, kv_heads, group, HEAD_DIM)
    )
    shares = jnp.exp(scores - log_totals)
    grad_shares = jnp.einsum(
        "bagd,pad->agbp", grad_blended, value_heads, preferred_element_type=F32
    )
    inner = jnp.sum(shares * grad_shares, axis=-1, keepdims=True)
    grad_scores = (shares * (grad_shares - inner)).astype(BF)
    grad_queries = score_scale * jnp.einsum(
        "agbp,pad->bagd", grad_scores, key_heads, preferred_element_type=F32
    )
    grad_keys = score_scale * jnp.einsum(
        "agbp,bagd->pad", grad_scores, queries, preferred_element_type=F32
    )
    grad_values = jnp.einsum(
        "agbp,bagd->pad", shares_low, grad_blended, preferred_element_type=F32
    )
    grad_kv = jnp.concatenate(
        [grad_keys.reshape(pack_len, kv_width), grad_values.reshape(pack_len, kv_width)], axis=1
    ).astype(BF)
    if kernels:
        grad_kv, _ = sum_blocks([grad_kv], jnp.zeros((8, LANES), F32), 1, 5)
        mixed, _ = lax.optimization_barrier((mixed, grad_kv))
        mixed_sub, grad_lower = reduce_rows([mixed], grad_lower, {0: 2, 1: 1, 2: 3}, nd, 4)
        grad_lower, grad_upper = lax.optimization_barrier((grad_lower, grad_upper))
        grad_lower = lax.all_gather(grad_lower, "ctx", axis=0)
        grad_expert_in, grad_expert_out = spread(grad_upper, grad_lower, own_count)
    else:
        grad_kv = lax.psum_scatter(grad_kv, "ctx", scatter_dimension=0, tiled=True).astype(F32)
    result = lax.all_to_all((middle + mixed_sub).astype(BF), "tensor", 1, 0, tiled=True)
    grad_turned = jnp.concatenate(
        [
            grad_queries.reshape(n_rows, q_heads, HEAD_DIM),
            grad_kv[:, :kv_width].reshape(n_rows, kv_heads, HEAD_DIM),
        ],
        axis=1,
    )
    grad_qkv = jnp.concatenate(
        [
            rotate(grad_turned, cosine_table, -sine_table)
            .astype(BF)
            .reshape(n_rows, q_width + kv_width),
            grad_kv[:, kv_width:].astype(BF),
        ],
        axis=1,
    )
    grad_norm_one = scatter_rows(dot(grad_qkv, qkv_w, ((1,), (1,))), tensor_at, nt)
    inverse_sub = lax.rsqrt(jnp.mean(tokens_sub * tokens_sub, axis=1, keepdims=True) + EPS)
    grad_tokens, grad_gain_one = norm_backward(
        tokens_sub, gain_one_full, inverse_sub, grad_norm_one
    )
    grad_tokens = lax.all_to_all(grad_tokens + grad_middle, "tensor", 1, 0, tiled=True)

    grad_qkv_w = dot(h_one, grad_qkv, ((0,), (0,)))
    gain_grads = jnp.stack([grad_gain_one, grad_gain_two])
    grad_router = jnp.pad(grad_router, ((0, 0), (0, LANES - EXPERTS)))
    weight_grads = [w.astype(BF) for w in (grad_qkv_w, grad_output_w, grad_router)]
    if kernels:
        gain_grads, grad_tokens, _ = lax.optimization_barrier((gain_grads, grad_tokens, mixed_sub))
        weight_grads, gain_grads = sum_blocks(weight_grads, gain_grads, nd, 6)
    else:
        weight_grads = lax.psum_scatter(
            jnp.concatenate(weight_grads, axis=1), ("dp", "ctx"), scatter_dimension=0, tiled=True
        )
        weight_grads = lax.all_gather(weight_grads, "ctx", axis=0, tiled=True).astype(F32)
        gain_grads = jnp.sum(lax.all_gather(gain_grads, ALL, axis=0), axis=0)
    edges = [0, q_width, q_width + kv_width, qkv_width, qkv_width + q_width]
    gain_grads = lax.dynamic_slice_in_dim(gain_grads, tensor_at * part_width, part_width, 1)
    return (
        result,
        grad_tokens,
        gain_grads[0],
        weight_grads[:, edges[0] : edges[1]],
        weight_grads[:, edges[1] : edges[2]],
        weight_grads[:, edges[2] : edges[3]],
        weight_grads[:, edges[3] : edges[4]],
        gain_grads[1],
        weight_grads[:, edges[4] : edges[4] + EXPERTS],
        grad_expert_in,
        grad_expert_out,
    )


def solution(mesh):
    return jax.shard_map(
        on_device,
        mesh=mesh,
        in_specs=(
            P(("dp", "ctx"), "tensor"),
            P("dp", None),
            P("dp", None),
            P("dp", None),
            P("tensor"),
            P("dp", "tensor"),
            P("dp", "tensor"),
            P("dp", "tensor"),
            P("dp", "tensor"),
            P("tensor"),
            P("dp", None),
            P("dp", "tensor", None),
            P("dp", "tensor", None),
            P(("dp", "ctx"), "tensor"),
        ),
        out_specs=(
            P(("dp", "ctx"), "tensor"),
            P(("dp", "ctx"), "tensor"),
            P("tensor"),
            P("dp", "tensor"),
            P("dp", "tensor"),
            P("dp", "tensor"),
            P("dp", "tensor"),
            P("tensor"),
            P("dp", None),
            P("dp", "tensor", None),
            P("dp", "tensor", None),
        ),
        check_vma=False,
    )
```
